32 devices in a mesh: tm: 8 (over z, y), order: 4 (over x, core).
Axes of the slice: x: 2, y: 2, z: 4, core: 2. Of those that a mesh axis runs over, the one named last changes fastest.
Arguments:
- design: bfloat16 [3, 1024, 65536], P(None, 'tm', 'order'), may hold values from -0.109375 to 0.109375
- gap_flags: int32 [1024], P('tm'), may hold values 0 or 1
- segment_ids: int32 [1024], P('tm'), may hold values from 0 to 3, never falling along the last dimension, each value on 1 to 512 neighbouring positions
- ar_order: int32 [3], replicated, may hold values from 1 to 4
- ma_order: int32 [3], replicated, may hold values from 1 to 4
- ar_roots: float32 [3, 4], replicated, may hold values from -0.5 to 1, as said below
- ma_roots: float32 [3, 4], replicated, may hold values from -0.5 to 1, as said below
- kaula: float32 [4, 16384], P('order', 'tm'), may hold values from 0.2 to 2
- precond: float32 [4, 128, 128, 128], P('order', 'tm'), as said below
- solution: float32 [16, 4, 16384], P(None, 'order', 'tm'), may hold values from -6 to 6
- residual: float32 [16, 4, 16384], P(None, 'order', 'tm'), may hold values from -6 to 6
- direction: float32 [16, 4, 16384], P(None, 'order', 'tm'), may hold values from -6 to 6
Outputs:
- new_solution: float32 [16, 4, 16384], P(None, 'order', 'tm')
- new_residual: float32 [16, 4, 16384], P(None, 'order', 'tm')
- new_direction: float32 [16, 4, 16384], P(None, 'order', 'tm')
The draws below stay inside these ranges and needn't reach their ends.
Inputs may be any that keep to these rules, and one draw needn't show every extreme that they name: The first root of each component of ar_roots lies within 2 / 1024 below 1; the others lie within 0.5 of zero. The first root of each component of ma_roots lies within 12 / 1024 below 1; the others lie within 0.5 of zero. `precond`: every block is symmetric positive definite.
All inputs are finite; a program needn't handle non-finite values. No bound on the sum of `gap_flags` on one device may be relied on, other than what follows from the above.
Results may differ from the reference program's by a relative error of at most 0.0036.
Values may be sent and summed in bfloat16 or wider, within the bound.
A program may use at most 64 MiB of HBM per device.

```python
import math
import jax
import jax.numpy as jnp
import numpy as np
from jax import lax

NCOEF = 65536
BLK = 128
PMAX = 4
QMAX = 4
SEGMENTS = 4
NRHS = 16
EPOCHS = 1024
CD = 16384
BLOCKS_O = 128
N_ORDER = 4


def draw_ar_roots(key, part):
    lead_key, rest_key = jax.random.split(jax.random.fold_in(key, 11))
    spread = jax.random.uniform(lead_key, (3,), jnp.float32, 0.5, 2.0)
    leading = 1.0 - spread / EPOCHS
    others = jax.random.uniform(rest_key, (3, PMAX - 1), jnp.float32, -0.5, 0.5)
    return jnp.concatenate([leading[:, None], others], axis=1)


def draw_ma_roots(key, part):
    lead_key, rest_key = jax.random.split(jax.random.fold_in(key, 23))
    spread = jax.random.uniform(lead_key, (3,), jnp.float32, 1.0, 3.0)
    leading = 1.0 - 4.0 * spread / EPOCHS
    others = jax.random.uniform(rest_key, (3, QMAX - 1), jnp.float32, -0.5, 0.5)
    return jnp.concatenate([leading[:, None], others], axis=1)


def draw_precond(key, part):
    off_key, diag_key = jax.random.split(jax.random.fold_in(key, 37), 2)
    raw = jax.random.normal(off_key, (N_ORDER, BLOCKS_O, BLK, BLK), jnp.float32) / BLK
    symmetric = raw + jnp.swapaxes(raw, 2, 3)
    identity = jnp.eye(BLK, dtype=jnp.float32)
    off_diag = symmetric * (1.0 - identity)
    extra = jax.random.uniform(diag_key, (N_ORDER, BLOCKS_O, BLK), jnp.float32, 0.1, 1.0)
    diagonal = 1.25 * jnp.sum(jnp.abs(off_diag), axis=3) + extra
    matrix = off_diag + diagonal[..., None] * identity
    return matrix


def set_ends(values, key, low, top_value):
    dims = values.shape
    place = [jax.random.randint(jax.random.fold_in(key, axis), (), 0, dims[axis]) for axis in range(len(dims))]
    values = values.at[tuple(place)].set(low)
    longest = dims.index(max(dims))
    place[longest] = (place[longest] + 1) % dims[longest]
    return values.at[tuple(place)].set(top_value)


def levels(stream_key, dims, cuts, low, top_value):
    loudness = 1.0
    for axis_at, shards_of in cuts:
        steps = jax.random.uniform(jax.random.fold_in(jax.random.fold_in(stream_key, 6), axis_at), (shards_of,), jnp.float32, low / len(cuts), top_value / len(cuts))
        loudness = loudness * jnp.repeat(jnp.exp(steps), dims[axis_at] // shards_of).reshape((-1,) + (1,) * (len(dims) - 1 - axis_at))
    return loudness


def split_up(count, total, most, skew):
    weights = [(1 << 20) // math.isqrt(rank ** skew) + 1 for rank in range(2, count + 1)]
    spare, holding = total - most - (count - 1), [1] * (count - 1)
    while spare > 0:
        movable = [i for i in range(count - 1) if holding[i] < most]
        whole, remaining = sum([weights[i] for i in movable]), spare
        for i in movable:
            more = min(most - holding[i], max(1, remaining * weights[i] // whole), spare)
            holding[i] = holding[i] + more
            spare = spare - more
    return np.array([most] + holding)


def uneven(own_key, number_of, total, limit, slope):
    if number_of == 2:
        one = jax.random.randint(own_key, (), max(1, total - limit), min(limit, total - 1) + 1)
        return jnp.stack([one, total - one])
    tallies = jnp.asarray(split_up(number_of, total, limit, slope), jnp.int32)
    pairs = (number_of - 1) // 2
    source_of, sink = tallies[1:1 + 2 * pairs:2], tallies[2:2 + 2 * pairs:2]
    slack = jnp.minimum(source_of - 1, limit - sink)
    moved = jax.random.randint(jax.random.fold_in(own_key, 1), (pairs,), 0, 1 << 20) % (slack + 1)
    tallies = tallies.at[1:1 + 2 * pairs:2].set(source_of - moved).at[2:2 + 2 * pairs:2].set(sink + moved)
    return tallies[jax.random.permutation(jax.random.fold_in(own_key, 2), number_of)]


def scatter_about(own_key, extent, scale, reach, cuts=(), kind=jnp.bfloat16):
    gain = levels(own_key, extent, cuts, -0.22, 0.18) if cuts else 1.0
    entries = jax.random.normal(own_key, extent, jnp.float32) * scale * gain
    return jnp.minimum(jnp.maximum(entries, -reach), reach).astype(kind)


def setup_inputs(seed: int = 0) -> dict:
    seeds = jax.random.split(jax.random.key(seed), 13)
    design = scatter_about(seeds[0], (3, EPOCHS, NCOEF), (3 * EPOCHS) ** -0.5, 0.109375, ((1, 8), (2, 4)))
    gap_flags = set_ends((jax.random.randint(seeds[1], (EPOCHS,), 0, 16) < 15).astype(jnp.int32), jax.random.fold_in(seeds[1], 1), 0, 1)
    segment_ids = jnp.searchsorted(jnp.cumsum(uneven(seeds[2], SEGMENTS, EPOCHS, EPOCHS // 2, 0)), jnp.arange(EPOCHS), side="right").astype(jnp.int32)
    ar_order = jax.random.randint(seeds[3], (3,), 1, PMAX + 1).astype(jnp.int32)
    ma_order = jax.random.randint(seeds[4], (3,), 1, QMAX + 1).astype(jnp.int32)
    ar_roots = draw_ar_roots(jax.random.fold_in(seeds[12], 71), 0)
    ma_roots = draw_ma_roots(jax.random.fold_in(seeds[12], 71), 0)
    kaula = jnp.clip(jnp.exp(math.log(2.0) - 2.3025851 * jax.random.uniform(seeds[7], (N_ORDER, CD), jnp.float32) ** levels(seeds[7], (N_ORDER, CD), ((0, 4), (1, 8)), -0.2, 0.2)), 0.2, 2.0)
    precond = draw_precond(jax.random.fold_in(seeds[12], 71), 0)
    solution = scatter_about(seeds[9], (NRHS, N_ORDER, CD), 1.0, 6.0, ((1, 4), (2, 8)), jnp.float32)
    residual = scatter_about(seeds[10], (NRHS, N_ORDER, CD), 1.0, 6.0, ((1, 4), (2, 8)), jnp.float32)
    direction = scatter_about(seeds[11], (NRHS, N_ORDER, CD), 1.0, 6.0, ((1, 4), (2, 8)), jnp.float32)
    return {"design": design, "gap_flags": gap_flags, "segment_ids": segment_ids, "ar_order": ar_order, "ma_order": ma_order, "ar_roots": ar_roots, "ma_roots": ma_roots, "kaula": kaula, "precond": precond, "solution": solution, "residual": residual, "direction": direction}


def polynomial(root_values, filter_order):
    number_roots = root_values.shape[1]
    coeffs = jnp.concatenate([jnp.ones((3, 1), root_values.dtype), jnp.zeros((3, number_roots), root_values.dtype)], axis=1)
    for position in range(number_roots):
        active = jnp.where(position < filter_order, root_values[:, position], jnp.zeros_like(root_values[:, position]))
        lagged = jnp.concatenate([jnp.zeros_like(coeffs[:, :1]), coeffs[:, :-1]], axis=1)
        coeffs = coeffs - active[:, None] * lagged
    return coeffs


def moving_part(series, coeffs, seg_ids, backward):
    length = series.shape[2]
    total = jnp.zeros_like(series)
    for lag_step in range(coeffs.shape[1]):
        if backward:
            moved = jnp.pad(series, ((0, 0), (0, 0), (0, lag_step)))[:, :, lag_step:]
            moved_ids = jnp.pad(seg_ids, (0, lag_step), constant_values=-1)[lag_step:]
        else:
            moved = jnp.pad(series, ((0, 0), (0, 0), (lag_step, 0)))[:, :, :length]
            moved_ids = jnp.pad(seg_ids, (lag_step, 0), constant_values=-1)[:length]
        joined = (moved_ids == seg_ids)[None, None, :]
        total = total + coeffs[:, lag_step][None, :, None] * jnp.where(joined, moved, jnp.zeros_like(moved))
    return total


def recursive_part(series, coeffs, seg_ids, backward):
    lags = coeffs.shape[1] - 1
    weights = coeffs[:, 1:].T[:, None, :]

    def advance(carry, inputs):
        buffer, id_buffer = carry
        value, current = inputs
        joined = (id_buffer == current)[:, None, None]
        coupling = jnp.sum(jnp.where(joined, weights * buffer, jnp.zeros_like(buffer)), axis=0)
        result = value - coupling
        new_buffer = jnp.concatenate([result[None], buffer[:-1]], axis=0)
        new_ids = jnp.concatenate([current[None], id_buffer[:-1]], axis=0)
        return (new_buffer, new_ids), result

    start = (jnp.zeros((lags,) + series.shape[:2], series.dtype), jnp.full((lags,), -1, jnp.int32))
    _, outputs = lax.scan(advance, start, (jnp.moveaxis(series, 2, 0), seg_ids), reverse=backward)
    return jnp.moveaxis(outputs, 0, 2)


def precondition(blocks, vector):
    rows = vector.shape[0]
    shaped = vector.reshape(rows, blocks.shape[0], blocks.shape[1])
    return jnp.einsum("bij,rbj->rbi", blocks, shaped, precision=lax.Precision.HIGHEST).reshape(rows, -1)


def reference(design, gap_flags, segment_ids, ar_order, ma_order, ar_roots, ma_roots, kaula, precond, solution, residual, direction):
    rhs_count = direction.shape[0]
    epochs = design.shape[1]
    columns = design.shape[2]
    flat_dir = direction.reshape(rhs_count, columns)
    flat_res = residual.reshape(rhs_count, columns)
    flat_sol = solution.reshape(rhs_count, columns)
    flat_kaula = kaula.reshape(columns)
    blocks = precond.reshape(-1, precond.shape[2], precond.shape[3])
    design_flat = design.reshape(3 * epochs, columns)
    packed = flat_dir.astype(jnp.bfloat16)
    observed = lax.dot_general(packed, design_flat, (((1,), (1,)), ((), ())), preferred_element_type=jnp.float32)
    observed = observed.reshape(rhs_count, 3, epochs)
    gaps = gap_flags.astype(observed.dtype)
    ar_coeffs = polynomial(ar_roots, ar_order)
    ma_coeffs = polynomial(ma_roots, ma_order)
    masked = observed * gaps[None, None, :]
    moving = moving_part(masked, ma_coeffs, segment_ids, False)
    filtered = recursive_part(moving, ar_coeffs, segment_ids, False)
    adjoint = recursive_part(filtered, ar_coeffs, segment_ids, True)
    weighted = (moving_part(adjoint, ma_coeffs, segment_ids, True) * gaps[None, None, :]).astype(jnp.bfloat16)
    gradient = jnp.dot(weighted.reshape(rhs_count, 3 * epochs), design_flat, preferred_element_type=jnp.float32)
    image = gradient + flat_kaula[None, :] * flat_dir
    applied = precondition(blocks, flat_res)
    old_rz = jnp.sum(flat_res * applied, axis=1)
    curvature = jnp.sum(flat_dir * image, axis=1)
    step_len = (old_rz / curvature)[:, None]
    new_solution = flat_sol + step_len * flat_dir
    new_residual = flat_res - step_len * image
    new_applied = precondition(blocks, new_residual)
    new_rz = jnp.sum(new_residual * new_applied, axis=1)
    new_direction = new_applied + (new_rz / old_rz)[:, None] * flat_dir
    shape = direction.shape
    return new_solution.reshape(shape), new_residual.reshape(shape), new_direction.reshape(shape)
```

```python
import functools

import jax
import jax.numpy as jnp
from jax import lax
from jax.experimental import pallas as pl
from jax.experimental.pallas import tpu as pltpu
from jax.sharding import PartitionSpec as P

LINK = jnp.bfloat16
LAGS = 4
HI = lax.Precision.HIGHEST
NN = (((1,), (0,)), ((), ()))
NT = (((1,), (1,)), ((), ()))


def dot(a, b, dims, precision=None):
    return lax.dot_general(a, b, dims, precision=precision, preferred_element_type=jnp.float32)


def tall(block, rows):
    return jnp.concatenate(
        [block, jnp.zeros((rows - block.shape[0], block.shape[1]), jnp.float32)], axis=0
    )


def halves(x):
    top = x.astype(jnp.bfloat16)
    return top, (x - top.astype(jnp.float32)).astype(jnp.bfloat16)


def dot3(x, high, low, dims):
    rows = x.shape[0]
    top, rest = halves(x)
    both = dot(jnp.concatenate([top, rest], axis=0), high, dims)
    return both[:rows] + both[rows:] + dot(top, low, dims)


def bands(matrix):
    row = lax.broadcasted_iota(jnp.int32, matrix.shape, 0)
    col = lax.broadcasted_iota(jnp.int32, matrix.shape, 1)
    return [
        jnp.sum(jnp.where(row == col - 4 * shift, matrix, 0.0), axis=0, keepdims=True)
        for shift in range(1 - LAGS, LAGS)
    ]


def banded(vector, coeffs):
    width = vector.shape[1]
    total = None
    for shift, coeff in zip(range(1 - LAGS, LAGS), coeffs):
        moved = vector if shift == 0 else pltpu.roll(vector, 4 * shift % width, 1)
        total = moved * coeff if total is None else total + moved * coeff
    return total


def columns(ref, order_ref, comp):
    out = []
    for k in range(LAGS):
        column = jnp.zeros(comp.shape, jnp.float32)
        for c in range(3):
            value = jnp.where(k < order_ref[c], ref[c, k], 0.0)
            column = jnp.where(comp == c, value, column)
        out.append(column)
    return out


def stack(pieces):
    row = lax.broadcasted_iota(jnp.int32, pieces[0].shape, 0)
    real = row % 4 < 3
    both = [jnp.where(row < 4, pieces[i], pieces[i + 1]) for i in range(0, LAGS, 2)]
    return jnp.concatenate([jnp.where(real, block, 0.0) for block in both], axis=0)


def filters(ar_ref, ma_ref, aro_ref, mao_ref, ids, pt_ref):
    n = ids.shape[1]
    lane = lax.broadcasted_iota(jnp.int32, (8, n), 1)
    comp = lax.broadcasted_iota(jnp.int32, (8, n), 0) % 4

    def lagged(v, k):
        return v if k == 0 else jnp.where(lane >= k, pltpu.roll(v, k, 1), 0.0)

    def at(k):
        return jnp.where(lane == k, 1.0, 0.0)

    ar, ma = columns(ar_ref, aro_ref, comp), columns(ma_ref, mao_ref, comp)
    a, b = [1.0] + [0.0] * LAGS, [1.0] + [0.0] * LAGS
    for k in range(LAGS):
        a = [a[0]] + [a[j] - ar[k] * a[j - 1] for j in range(1, LAGS + 1)]
        b = [b[0]] + [b[j] - ma[k] * b[j - 1] for j in range(1, LAGS + 1)]
    h, power, m = at(0), ar, 1
    while m < n:
        s0, q0 = power[0] + power[1], power[0] * power[1]
        s1, q1 = power[2] + power[3], power[2] * power[3]
        e = [s0 + s1, q0 + q1 + s0 * s1, q0 * s1 + s0 * q1, q0 * q1]
        terms = [e[j] * lagged(h, (j + 1) * m) for j in range(LAGS) if (j + 1) * m < n]
        while len(terms) > 1:
            terms = [sum(terms[i + 1 : i + 2], terms[i]) for i in range(0, len(terms), 2)]
        h = h + terms[0]
        power, m = [p * p for p in power], 2 * m
    hs = [lagged(h, k) for k in range(LAGS + 1)]
    g = hs[0] + ((b[1] * hs[1] + b[2] * hs[2]) + (b[3] * hs[3] + b[4] * hs[4]))
    gs = [lagged(g, k) for k in range(LAGS)]
    ins, ends = [], []
    for i in range(1, LAGS + 1):
        acc, end = jnp.zeros_like(g), jnp.zeros_like(g)
        for k in range(LAGS + 1 - i):
            acc = acc + b[i + k] * at(k) - a[i + k] * gs[k]
            end = end - a[i + k] * at(n - 1 - k)
        ins.append(acc)
        ends.append(end)
    yield None
    row = lax.broadcasted_iota(jnp.int32, (n, n), 0)
    col = lax.broadcasted_iota(jnp.int32, (n, n), 1)
    grid = jnp.broadcast_to(ids, (n, n))
    joined = (grid == grid.T) & (col >= row)
    for c in range(3):
        t = pltpu.roll(jnp.broadcast_to(g[c : c + 1], (n, n)), 0, 1, stride=1, stride_axis=0)
        pt_ref[c] = jnp.where(joined, t, 0.0)
    yield None
    ca, ends = stack(hs[:LAGS]), stack(ends)
    flip = jnp.where(row + col == n - 1, 1.0, 0.0).astype(jnp.float32)
    ab = dot(stack(ins), flip, NN, HI)
    fwd = bands(dot(ca, tall(ends, n), NT, HI))
    bwd = bands(dot(ends, tall(ca, n), NT, HI))
    yield ca, ab, fwd, bwd


def spread(block, mask):
    row = lax.broadcasted_iota(jnp.int32, block.shape, 0)
    return jnp.concatenate(
        [jnp.where(row % 4 == c, block * mask, 0.0) for c in range(3)], axis=1
    )


def state_weights(T, me, shape, links, throughs, fwd, bwd, energies):
    row = lax.broadcasted_iota(jnp.int32, shape, 0)
    lane = lax.broadcasted_iota(jnp.int32, shape, 1)
    eye = jnp.where(row == lane, 1.0, 0.0)
    zero = jnp.zeros(shape, jnp.float32)
    state, ins, mine = {}, [], {}

    def keep(blocks, e, into):
        for key, v in blocks.items():
            mine[into, key] = jnp.where(me == e, v, mine.get((into, key), zero))

    for e in range(T):
        entering = {q: v * links[e] for q, v in state.items()}
        ins.append(entering)
        keep(entering, e, "in")
        state = {q: throughs[e] * banded(v, fwd) for q, v in entering.items()}
        state[e] = eye
    back = {}
    for e in range(T - 1, 0, -1):
        new = {key: throughs[e] * banded(v, bwd) for key, v in back.items()}
        for q, v in ins[e].items():
            moved = banded(v, energies[e])
            new["tail", q] = new["tail", q] + moved if ("tail", q) in new else moved
        new["head", e] = eye
        back = {key: v * links[e] for key, v in new.items()}
        keep(back, e - 1, "back")
    out = []
    for e in range(T):
        entering = pltpu.roll(mine["in", e], 16, 1) if ("in", e) in mine else zero
        out.append(mine.get(("back", ("tail", e)), zero) + entering)
        out.append(mine.get(("back", ("head", e)), zero))
    return jnp.concatenate(out, axis=0)


def kernel(
    T, O,
    design, ids_in, gaps_in, ar_ref, ma_ref, aro_ref, mao_ref, kaula, precond_in,
    res_in, direc_in,
    image_out, comb_out, scal_out,
    dv, precond, res, direc, packed, high, low,
    right_in, left_in, obs_out, obs_in, ids_all, part_out, part_in, summ_out, summ_in, pt,
    map_high, map_low, cross_high, cross_low,
    rs_right_out, rs_left_out, rs_right_in, rs_left_in, applied, image_applied,
    tot_out, tot_in,
    dsem, in_sem, agr_s, agr_r, agl_s, agl_r, ob_s, ob_r, id_s, id_r, pa_s, pa_r, su_s, su_r,
    rr_s, rr_r, rl_s, rl_r, t1_s, t1_r,
):
    me, order = lax.axis_index("tm"), lax.axis_index("order")
    A = T // 2
    rhs, share = packed.shape
    n = ids_in.shape[1]
    blocks = precond.shape[0]

    slow, fast = me // 2, me % 2
    partner = {"tm": 2 * slow + 1 - fast}

    def at_slow(k, other=0):
        row = 1 - fast if other else fast
        return 2 * lax.rem(slow + k + A, A) + row

    mesh_ids = pl.DeviceIdType.MESH

    def to_tm(k):
        return {"tm": lax.rem(me + k, T)}

    def to_order(k):
        return {"order": lax.rem(order + k, O)}

    def to_all(k, i):
        return {"tm": lax.rem(me + k, T), "order": lax.rem(order + i, O)}

    def load(k, other):
        q = at_slow(k, other)
        slot = other * A + k % A
        return pltpu.make_async_copy(
            design.at[:, pl.ds(pl.multiple_of(q * share, 128), share)],
            dv.at[slot],
            dsem.at[slot],
        )

    def remote(src, dst, ssem, rsem, to):
        return pltpu.make_async_remote_copy(
            src_ref=src, dst_ref=dst, send_sem=ssem, recv_sem=rsem,
            device_id=to, device_id_type=mesh_ids,
        )

    get_direc = pltpu.make_async_copy(direc_in.at[:, 0, :], direc, in_sem.at[0])
    get_res = pltpu.make_async_copy(res_in.at[:, 0, :], res, in_sem.at[1])
    get_precond = pltpu.make_async_copy(precond_in, precond, in_sem.at[2])
    get_direc.start()
    barrier = pltpu.get_barrier_semaphore()
    for k in range(1, T):
        pl.semaphore_signal(barrier, inc=1, device_id=to_tm(k), device_id_type=mesh_ids)
    for k in range(1, O):
        pl.semaphore_signal(barrier, inc=1, device_id=to_order(k), device_id_type=mesh_ids)
    for i in range(1, O):
        for k in range(1, T):
            pl.semaphore_signal(barrier, inc=1, device_id=to_all(k, i), device_id_type=mesh_ids)
    load(0, 0).start()
    get_precond.start()
    get_res.start()
    load(0, 1).start()
    for k in range(1, A):
        load(-k, 0).start()
        load(-k, 1).start()
    get_direc.wait()
    packed[...] = direc[...].astype(jnp.bfloat16)
    pl.semaphore_wait(barrier, T * O - 1)

    across = [remote(packed, right_in.at[k], agr_s.at[k], agr_r.at[k], {"tm": at_slow(k)})
              for k in range(1, A)]
    beside = [remote(packed, left_in.at[0], agl_s.at[0], agl_r.at[0], partner)]
    beside += [remote(right_in.at[k], left_in.at[k], agl_s.at[k], agl_r.at[k], partner)
               for k in range(1, A)]
    for copy in across + beside[:1]:
        copy.start()
    id_copies = [
        remote(ids_in, ids_all.at[k - 1], id_s.at[k - 1], id_r.at[k - 1], to_tm(k))
        for k in range(1, T)
    ]
    for copy in id_copies:
        copy.start()

    load(0, 0).wait()
    obs = dot(packed[...], dv[0], NT)
    ids = ids_in[0:1, :].astype(jnp.float32)
    gaps3 = jnp.concatenate([gaps_in[0:1, :].astype(jnp.float32)] * 3, axis=1)
    building = filters(ar_ref, ma_ref, aro_ref, mao_ref, ids, pt)
    next(building)

    def preconditioned(v, cols):
        out = []
        for m in range(cols.start // 128, cols.stop // 128):
            x = v[:, m * 128 - cols.start : (m + 1) * 128 - cols.start]
            out.append(dot3(x, high[m], low[m], NT))
        return jnp.concatenate(out, axis=1)

    def arrive(k):
        across[k - 1].wait_recv()
        beside[k].start()

    def right(k, obs):
        load(-k, 0).wait()
        return obs + dot(right_in[k], dv[(-k) % A], NT)

    def left(k, obs):
        beside[k].wait_recv()
        load(-k, 1).wait()
        return obs + dot(left_in[k], dv[A + (-k) % A], NT)

    arrive(1)
    next(building)
    ca, ab, fwd, bwd = next(building)
    first, last = ids[:, 0:1], ids[:, n - 1 : n]
    head_map = spread(ca, jnp.where(ids == first, 1.0, 0.0))
    tail_map = spread(ab, jnp.where(ids == last, 1.0, 0.0))
    head_map = jnp.concatenate(
        [dot(head_map[:, c * n : (c + 1) * n], pt[c], NT, HI) for c in range(3)], axis=1
    )
    both_maps = jnp.concatenate([tail_map, head_map], axis=0)
    slots = jnp.concatenate([both_maps] * (n // 32), axis=0)
    slot_row = lax.broadcasted_iota(jnp.int32, slots.shape, 0) // 32
    top, rest = halves(jnp.where(slot_row == lax.rem(me, n // 32), slots, 0.0))
    map_high[...] = top
    map_low[...] = rest
    obs = right(1, obs)
    obs = left(0, obs)
    get_precond.wait()
    for m in range(blocks):
        top, rest = halves(precond[m])
        high[m] = top
        low[m] = rest
    for k in range(2, A):
        arrive(k)
        obs = right(k, obs)
        obs = left(k - 1, obs)
    get_res.wait()
    applied[...] = preconditioned(res[...], slice(0, share))
    obs = left(A - 1, obs)

    half = rhs // 2
    summary = dot3(obs * gaps3, map_high[...], map_low[...], NT)
    part_out[...] = summary[:half] + pltpu.roll(summary[half:], n // 2, 1)
    obs_out[...] = obs
    pa_copies = [
        remote(part_out, part_in.at[k - 1], pa_s.at[k - 1], pa_r.at[k - 1], to_order(k))
        for k in range(1, O)
    ]
    ob_copies = [
        remote(obs_out, obs_in.at[k - 1], ob_s.at[k - 1], ob_r.at[k - 1], to_order(k))
        for k in range(1, O)
    ]
    for copy in pa_copies + ob_copies:
        copy.start()

    for copy in id_copies:
        copy.wait_recv()
    ids_e = []
    for e in range(T):
        slot = jnp.minimum(lax.rem(me - e + T - 1, T), T - 2)
        ids_e.append(jnp.where(me == e, ids, ids_all[slot].astype(jnp.float32)))
    firsts = [v[:, 0:1] for v in ids_e]
    lasts = [v[:, n - 1 : n] for v in ids_e]
    runs = jnp.concatenate(
        [ca * jnp.where(v == f, 1.0, 0.0) for v, f in zip(ids_e, firsts)], axis=0
    )
    energy = dot(runs, tall(ca, n), NT, HI)
    energies = [bands(energy[16 * e : 16 * e + 16]) for e in range(T)]
    links = [None] + [jnp.where(lasts[e - 1] == firsts[e], 1.0, 0.0) for e in range(1, T)]
    throughs = [jnp.where(firsts[e] == lasts[e], 1.0, 0.0) for e in range(T)]
    direct = T <= 8
    if direct:
        weights = state_weights(T, me, (16, n), links, throughs, fwd, bwd, energies)

    for copy in pa_copies:
        copy.wait_recv()
    summ_out[...] = part_out[...] + sum([part_in[k] for k in range(1, O - 1)], part_in[0])
    su_copies = [
        remote(summ_out, summ_in.at[k - 1], su_s.at[k - 1], su_r.at[k - 1], to_tm(k))
        for k in range(1, T)
    ]
    for copy in su_copies:
        copy.start()
    if direct:
        top, rest = halves(dot(weights, tall(both_maps, n), NN, HI))
        cross_high[...] = top
        cross_low[...] = rest
    for copy in ob_copies:
        copy.wait_recv()
    for k in range(1, O):
        obs = obs + obs_in[k - 1]
    masked = obs * gaps3
    local_back = jnp.concatenate(
        [
            dot(dot(masked[:, c * n : (c + 1) * n], pt[c], NN, HI), pt[c], NT, HI)
            for c in range(3)
        ],
        axis=1,
    )
    for copy in su_copies:
        copy.wait_recv()
    folded = []
    for e in range(T):
        slot = jnp.minimum(lax.rem(me - e + T - 1, T), T - 2)
        folded.append(jnp.where(me == e, summ_out[...], summ_in[slot]))
    lane8 = lax.broadcasted_iota(jnp.int32, (half, n), 1)
    groups = []
    for e in range(0, T, 4):
        front, back = folded[e] + folded[e + 1], folded[e + 2] + folded[e + 3]
        upper = jnp.where(lane8 < n // 2, front, back)
        lower = pltpu.roll(jnp.where(lane8 < n // 2, back, front), n // 2, 1)
        groups.append(jnp.concatenate([upper, lower], axis=0))
    if direct:
        adjoint = local_back + dot3(
            jnp.concatenate(groups, axis=1), cross_high[...], cross_low[...], NN
        )
    else:
        lane = lax.broadcasted_iota(jnp.int32, (rhs, n), 1)
        tails = [
            jnp.where(lane < 16, pltpu.roll(groups[e // 4], (n - 32 * (e % 4)) % n, 1), 0.0)
            for e in range(T)
        ]
        heads = [
            jnp.where(lane < 16, pltpu.roll(groups[e // 4], (n - 32 * (e % 4) - 16) % n, 1), 0.0)
            for e in range(T)
        ]
        state = jnp.zeros((rhs, n), jnp.float32)
        mine_in, mine_back, back, ins = state, state, state, []
        for e in range(T):
            entering = state if e == 0 else state * links[e]
            ins.append(entering)
            mine_in = jnp.where(me == e, entering, mine_in)
            state = tails[e] + throughs[e] * banded(entering, fwd)
        for e in range(T - 1, 0, -1):
            back = heads[e] + banded(ins[e], energies[e]) + throughs[e] * banded(back, bwd)
            back = back * links[e]
            mine_back = jnp.where(me == e - 1, back, mine_back)
        states = mine_back + pltpu.roll(mine_in, 16, 1)
        adjoint = local_back + dot(states, tall(both_maps, n), NN, HI)
    weighted = (adjoint * gaps3).astype(jnp.bfloat16)

    def grad(k, other):
        return dot(weighted, dv[other * A + k % A], NN)

    pair = [remote(rs_left_out.at[k], rs_left_in.at[k], rl_s.at[k], rl_r.at[k], partner)
            for k in range(A)]
    far = [remote(rs_right_out.at[k], rs_right_in.at[k], rr_s.at[k], rr_r.at[k],
                  {"tm": at_slow(k)}) for k in range(1, A)]
    order_of = list(range(1, A)) + [0]
    for k in order_of:
        rs_left_out[k] = grad(k, 1).astype(LINK)
        pair[k].start()
    for k in order_of[:-1]:
        piece = grad(k, 0)
        pair[k].wait_recv()
        rs_right_out[k] = (piece + rs_left_in[k].astype(jnp.float32)).astype(LINK)
        far[k - 1].start()
    image = grad(0, 0) + kaula[...] * direc[...]
    pair[0].wait_recv()
    image = image + rs_left_in[0].astype(jnp.float32)
    for k in order_of[:-1]:
        far[k - 1].wait_recv()
        image = image + rs_right_in[k].astype(jnp.float32)
    image_applied[...] = preconditioned(image, slice(0, share))
    image_out[...] = image
    app, imapp = applied[...], image_applied[...]
    d, r = direc[...], res[...]
    lane = lax.broadcasted_iota(jnp.int32, (rhs, 128), 1)
    row = lax.broadcasted_iota(jnp.int32, (rhs, 128), 0)
    products = [r * app, d * image, image * app, image * imapp]
    total = jnp.zeros((rhs, 128), jnp.float32)
    for q, product in enumerate(products):
        total = jnp.where(lane == q * rhs + row, jnp.sum(product, axis=1, keepdims=True), total)
    total = jnp.sum(total, axis=0, keepdims=True)

    tot_out[...] = total
    tot_copies = []
    for i in range(O):
        for k in range(T):
            if i or k:
                at = i * T + k - 1
                tot_copies.append(
                    remote(tot_out, tot_in.at[at], t1_s.at[at], t1_r.at[at], to_all(k, i))
                )
    for copy in tot_copies:
        copy.start()
    for copy in tot_copies:
        copy.wait_recv()
    total = total + jnp.sum(tot_in[...], axis=0)
    wide = jnp.broadcast_to(total[0:1, :], (rhs, 128))
    old_rz, curvature, cross, quad = [
        jnp.sum(jnp.where(lane == q * rhs + row, wide, 0.0), axis=1, keepdims=True)
        for q in range(4)
    ]
    step = old_rz / curvature
    new_rz = old_rz - 2.0 * step * cross + step * step * quad
    comb_out[...] = app - step * imapp
    scal_out[...] = jnp.where(lane == 0, step, new_rz / old_rz)

    for copy in across + beside + pair + far:
        copy.wait_send()
    for copy in id_copies + pa_copies + ob_copies + su_copies + tot_copies:
        copy.wait_send()


def finish(image, comb, scal, sol, res, direc, new_sol, new_res, new_dir, got, put, isem, osem):
    def fetch(k, ref):
        return pltpu.make_async_copy(ref.at[:, 0, :], got.at[k], isem.at[k])

    def store(k, ref):
        return pltpu.make_async_copy(put.at[k], ref.at[:, 0, :], osem.at[k])

    for k, ref in ((2, direc), (0, sol), (1, res)):
        fetch(k, ref).start()
    step, ratio = scal[:, 0:1], scal[:, 1:2]
    fetch(2, direc).wait()
    put[2] = comb[...] + ratio * got[2]
    store(2, new_dir).start()
    fetch(0, sol).wait()
    put[0] = got[0] + step * got[2]
    store(0, new_sol).start()
    fetch(1, res).wait()
    put[1] = got[1] - step * image[...]
    store(1, new_res).start()
    for k, ref in ((2, new_dir), (0, new_sol), (1, new_res)):
        store(k, ref).wait()


def on_device(
    T, O, design, gap_flags, segment_ids, ar_order, ma_order, ar_roots, ma_roots,
    kaula, precond, solution, residual, direction,
):
    n = segment_ids.shape[0]
    columns = design.shape[2]
    share = direction.shape[2]
    rhs = direction.shape[0]
    blocks = precond.shape[1]
    f32, bf16 = jnp.float32, jnp.bfloat16
    A = T // 2
    vmem = pl.BlockSpec(memory_space=pltpu.VMEM)
    smem = pl.BlockSpec(memory_space=pltpu.SMEM)
    hbm = pl.BlockSpec(memory_space=pl.ANY)
    V, D = pltpu.VMEM, lambda k: pltpu.SemaphoreType.DMA((max(k, 1),))
    vec = jax.ShapeDtypeStruct((rhs, share), f32)
    image, comb, scal = pl.pallas_call(
        functools.partial(kernel, T, O),
        out_shape=[vec, vec, jax.ShapeDtypeStruct((rhs, 128), f32)],
        in_specs=[hbm, vmem, vmem, smem, smem, smem, smem, vmem, hbm, hbm, hbm],
        out_specs=[vmem] * 3,
        scratch_shapes=[
            V((T, 3 * n, share), bf16), V((blocks, 128, 128), f32), V((rhs, share), f32),
            V((rhs, share), f32), V((rhs, share), bf16), V((blocks, 128, 128), bf16),
            V((blocks, 128, 128), bf16),
            V((A, rhs, share), bf16), V((A, rhs, share), bf16),
            V((rhs, 3 * n), f32), V((O - 1, rhs, 3 * n), f32), V((T - 1, 1, n), jnp.int32),
            V((rhs // 2, n), f32), V((O - 1, rhs // 2, n), f32),
            V((rhs // 2, n), f32), V((T - 1, rhs // 2, n), f32), V((3, n, n), f32),
            V((n, 3 * n), bf16), V((n, 3 * n), bf16), V((32 * T, 3 * n), bf16), V((32 * T, 3 * n), bf16),
            V((A, rhs, share), LINK), V((A, rhs, share), LINK),
            V((A, rhs, share), LINK), V((A, rhs, share), LINK),
            V((rhs, share), f32), V((rhs, share), f32),
            V((1, 128), f32), V((T * O - 1, 1, 128), f32),
            D(T), D(3), D(A), D(A), D(A), D(A), D(O - 1), D(O - 1),
            D(T - 1), D(T - 1), D(O - 1), D(O - 1), D(T - 1), D(T - 1), D(A), D(A), D(A),
            D(A), D(T * O - 1), D(T * O - 1),
        ],
        compiler_params=pltpu.CompilerParams(
            collective_id=0, has_side_effects=True, vmem_limit_bytes=56 * 1024 * 1024
        ),
    )(
        design.reshape(3 * n, columns), segment_ids.reshape(1, n), gap_flags.reshape(1, n),
        ar_roots, ma_roots, ar_order, ma_order, kaula, precond[0], residual, direction,
    )
    full = jax.ShapeDtypeStruct(direction.shape, f32)
    return tuple(
        pl.pallas_call(
            finish,
            out_shape=[full] * 3,
            in_specs=[vmem, vmem, vmem, hbm, hbm, hbm],
            out_specs=[hbm] * 3,
            scratch_shapes=[V((3, rhs, share), f32), V((3, rhs, share), f32), D(3), D(3)],
        )(image, comb, scal, solution, residual, direction)
    )


def solution(mesh):
    vec = P(None, "order", "tm")
    in_specs = (
        P(None, "tm", "order"), P("tm"), P("tm"), P(), P(), P(), P(), P("order", "tm"),
        P("order", "tm", None, None), vec, vec, vec,
    )
    body = functools.partial(on_device, mesh.shape["tm"], mesh.shape["order"])
    return jax.shard_map(
        body, mesh=mesh, in_specs=in_specs, out_specs=(vec, vec, vec), check_vma=False
    )
```

```python
import functools

import jax
import jax.numpy as jnp
from jax import lax
from jax.experimental import pallas as pl
from jax.experimental.pallas import tpu as pltpu
from jax.sharding import PartitionSpec as P

LINK = jnp.bfloat16
LAGS = 4
CHUNKS = 2
HI = lax.Precision.HIGHEST
NN = (((1,), (0,)), ((), ()))
NT = (((1,), (1,)), ((), ()))


def dot(a, b, dims, precision=None):
    return lax.dot_general(a, b, dims, precision=precision, preferred_element_type=jnp.float32)


def tall(block, rows):
    return jnp.concatenate(
        [block, jnp.zeros((rows - block.shape[0], block.shape[1]), jnp.float32)], axis=0
    )


def halves(x):
    top = x.astype(jnp.bfloat16)
    return top, (x - top.astype(jnp.float32)).astype(jnp.bfloat16)


def dot3(x, high, low, dims):
    rows = x.shape[0]
    top, rest = halves(x)
    both = dot(jnp.concatenate([top, rest], axis=0), high, dims)
    return both[:rows] + both[rows:] + dot(top, low, dims)


def bands(matrix):
    row = lax.broadcasted_iota(jnp.int32, matrix.shape, 0)
    col = lax.broadcasted_iota(jnp.int32, matrix.shape, 1)
    return [
        jnp.sum(jnp.where(row == col - 4 * shift, matrix, 0.0), axis=0, keepdims=True)
        for shift in range(1 - LAGS, LAGS)
    ]


def banded(vector, coeffs):
    width = vector.shape[1]
    total = None
    for shift, coeff in zip(range(1 - LAGS, LAGS), coeffs):
        moved = vector if shift == 0 else pltpu.roll(vector, 4 * shift % width, 1)
        total = moved * coeff if total is None else total + moved * coeff
    return total


def columns(ref, order_ref, comp):
    out = []
    for k in range(LAGS):
        column = jnp.zeros(comp.shape, jnp.float32)
        for c in range(3):
            value = jnp.where(k < order_ref[c], ref[c, k], 0.0)
            column = jnp.where(comp == c, value, column)
        out.append(column)
    return out


def stack(pieces):
    row = lax.broadcasted_iota(jnp.int32, pieces[0].shape, 0)
    real = row % 4 < 3
    both = [jnp.where(row < 4, pieces[i], pieces[i + 1]) for i in range(0, LAGS, 2)]
    return jnp.concatenate([jnp.where(real, block, 0.0) for block in both], axis=0)


def filters(ar_ref, ma_ref, aro_ref, mao_ref, ids, pt_ref):
    n = ids.shape[1]
    lane = lax.broadcasted_iota(jnp.int32, (8, n), 1)
    comp = lax.broadcasted_iota(jnp.int32, (8, n), 0) % 4

    def lagged(v, k):
        return v if k == 0 else jnp.where(lane >= k, pltpu.roll(v, k, 1), 0.0)

    def at(k):
        return jnp.where(lane == k, 1.0, 0.0)

    ar, ma = columns(ar_ref, aro_ref, comp), columns(ma_ref, mao_ref, comp)
    a, b = [1.0] + [0.0] * LAGS, [1.0] + [0.0] * LAGS
    for k in range(LAGS):
        a = [a[0]] + [a[j] - ar[k] * a[j - 1] for j in range(1, LAGS + 1)]
        b = [b[0]] + [b[j] - ma[k] * b[j - 1] for j in range(1, LAGS + 1)]
    h, power, m = at(0), ar, 1
    while m < n:
        s0, q0 = power[0] + power[1], power[0] * power[1]
        s1, q1 = power[2] + power[3], power[2] * power[3]
        e = [s0 + s1, q0 + q1 + s0 * s1, q0 * s1 + s0 * q1, q0 * q1]
        terms = [e[j] * lagged(h, (j + 1) * m) for j in range(LAGS) if (j + 1) * m < n]
        while len(terms) > 1:
            terms = [sum(terms[i + 1 : i + 2], terms[i]) for i in range(0, len(terms), 2)]
        h = h + terms[0]
        power, m = [p * p for p in power], 2 * m
    hs = [lagged(h, k) for k in range(LAGS + 1)]
    g = hs[0] + ((b[1] * hs[1] + b[2] * hs[2]) + (b[3] * hs[3] + b[4] * hs[4]))
    gs = [lagged(g, k) for k in range(LAGS)]
    ins, ends = [], []
    for i in range(1, LAGS + 1):
        acc, end = jnp.zeros_like(g), jnp.zeros_like(g)
        for k in range(LAGS + 1 - i):
            acc = acc + b[i + k] * at(k) - a[i + k] * gs[k]
            end = end - a[i + k] * at(n - 1 - k)
        ins.append(acc)
        ends.append(end)
    yield None
    row = lax.broadcasted_iota(jnp.int32, (n, n), 0)
    col = lax.broadcasted_iota(jnp.int32, (n, n), 1)
    grid = jnp.broadcast_to(ids, (n, n))
    joined = (grid == grid.T) & (col >= row)
    for c in range(3):
        t = pltpu.roll(jnp.broadcast_to(g[c : c + 1], (n, n)), 0, 1, stride=1, stride_axis=0)
        pt_ref[c] = jnp.where(joined, t, 0.0)
    yield None
    ca, ends = stack(hs[:LAGS]), stack(ends)
    flip = jnp.where(row + col == n - 1, 1.0, 0.0).astype(jnp.float32)
    ab = dot(stack(ins), flip, NN, HI)
    fwd = bands(dot(ca, tall(ends, n), NT, HI))
    bwd = bands(dot(ends, tall(ca, n), NT, HI))
    yield ca, ab, fwd, bwd


def spread(block, mask):
    row = lax.broadcasted_iota(jnp.int32, block.shape, 0)
    return jnp.concatenate(
        [jnp.where(row % 4 == c, block * mask, 0.0) for c in range(3)], axis=1
    )


def state_weights(T, me, shape, links, throughs, fwd, bwd, energies):
    row = lax.broadcasted_iota(jnp.int32, shape, 0)
    lane = lax.broadcasted_iota(jnp.int32, shape, 1)
    eye = jnp.where(row == lane, 1.0, 0.0)
    zero = jnp.zeros(shape, jnp.float32)
    state, ins, mine = {}, [], {}

    def keep(blocks, e, into):
        for key, v in blocks.items():
            mine[into, key] = jnp.where(me == e, v, mine.get((into, key), zero))

    for e in range(T):
        entering = {q: v * links[e] for q, v in state.items()}
        ins.append(entering)
        keep(entering, e, "in")
        state = {q: throughs[e] * banded(v, fwd) for q, v in entering.items()}
        state[e] = eye
    back = {}
    for e in range(T - 1, 0, -1):
        new = {key: throughs[e] * banded(v, bwd) for key, v in back.items()}
        for q, v in ins[e].items():
            moved = banded(v, energies[e])
            new["tail", q] = new["tail", q] + moved if ("tail", q) in new else moved
        new["head", e] = eye
        back = {key: v * links[e] for key, v in new.items()}
        keep(back, e - 1, "back")
    out = []
    for e in range(T):
        entering = pltpu.roll(mine["in", e], 16, 1) if ("in", e) in mine else zero
        out.append(mine.get(("back", ("tail", e)), zero) + entering)
        out.append(mine.get(("back", ("head", e)), zero))
    return jnp.concatenate(out, axis=0)


def kernel(
    T, O,
    design, ids_in, gaps_in, ar_ref, ma_ref, aro_ref, mao_ref, kaula, precond_in,
    res_in, direc_in,
    image_out, comb_out, scal_out,
    dv, precond, res, direc, packed, high, low_part,
    got, obs_out, obs_in, ids_all, part_out, part_in, summ_out, summ_in, pt,
    map_high, map_low, cross_high, cross_low, rs_out, rs_in, applied, image_applied,
    tot_out, tot_in,
    dsem, in_sem, ga_s, ga_r, ob_s, ob_r, id_s, id_r, pa_s, pa_r, su_s, su_r,
    rs_s, rs_r, t1_s, t1_r,
):
    me, order = lax.axis_index("tm"), lax.axis_index("order")
    rhs, share = packed.shape
    n = ids_in.shape[1]
    blocks = precond.shape[0]
    wide = share // CHUNKS
    bits = T.bit_length() - 1

    def low(x):
        return (x & -x).bit_length() - 1 if x else bits

    def across(x):
        out = me
        for b in range(bits):
            if x >> b & 1:
                out = out + (1 << b) * (1 - 2 * lax.rem(lax.div(me, 1 << b), 2))
        return out

    def cols(c):
        return slice(c * wide, (c + 1) * wide)

    mesh_ids = pl.DeviceIdType.MESH

    def to_tm(k):
        return {"tm": lax.rem(me + k, T)}

    def to_order(k):
        return {"order": lax.rem(order + k, O)}

    def to_all(k, i):
        return {"tm": lax.rem(me + k, T), "order": lax.rem(order + i, O)}

    def load(x):
        return pltpu.make_async_copy(
            design.at[:, pl.ds(pl.multiple_of(across(x) * share, 128), share)],
            dv.at[x],
            dsem.at[x],
        )

    def remote(src, dst, ssem, rsem, to):
        return pltpu.make_async_remote_copy(
            src_ref=src, dst_ref=dst, send_sem=ssem, recv_sem=rsem,
            device_id=to, device_id_type=mesh_ids,
        )

    get_direc = pltpu.make_async_copy(direc_in.at[:, 0, :], direc, in_sem.at[0])
    get_res = pltpu.make_async_copy(res_in.at[:, 0, :], res, in_sem.at[1])
    get_precond = pltpu.make_async_copy(precond_in, precond, in_sem.at[2])
    get_direc.start()
    barrier = pltpu.get_barrier_semaphore()
    for b in range(bits):
        pl.semaphore_signal(
            barrier, inc=1, device_id={"tm": across(1 << b)}, device_id_type=mesh_ids
        )
    for k in range(1, O):
        pl.semaphore_signal(barrier, inc=1, device_id=to_order(k), device_id_type=mesh_ids)
    plan = [4, 2, 1, 6, 3, 5, 7] if T == 8 else sorted(range(1, T), key=lambda x: -low(x))
    load(0).start()
    for x in plan:
        load(x).start()
    get_precond.start()
    get_res.start()
    get_direc.wait()
    packed[...] = direc[...].astype(jnp.bfloat16)
    pl.semaphore_wait(barrier, bits + O - 1)

    id_copies, ga_copies = {}, {}

    def pass_on(x, c):
        for b in reversed(range(low(x))):
            to = x | 1 << b
            if c == 0:
                id_copies[to] = remote(
                    ids_all.at[x - 1] if x else ids_in, ids_all.at[to - 1],
                    id_s.at[to - 1], id_r.at[to - 1], {"tm": across(1 << b)},
                )
                id_copies[to].start()
            ga_copies[to, c] = remote(
                (got.at[x - 1] if x else packed).at[:, cols(c)], got.at[to - 1, :, cols(c)],
                ga_s.at[to - 1, c], ga_r.at[to - 1, c], {"tm": across(1 << b)},
            )
            ga_copies[to, c].start()

    def arrive(x, c):
        if c == 0:
            id_copies[x].wait_recv()
        ga_copies[x, c].wait_recv()
        pass_on(x, c)

    for c in range(CHUNKS):
        pass_on(0, c)

    load(0).wait()
    obs = dot(packed[...], dv[0], NT)
    ids = ids_in[0:1, :].astype(jnp.float32)
    gaps3 = jnp.concatenate([gaps_in[0:1, :].astype(jnp.float32)] * 3, axis=1)
    building = filters(ar_ref, ma_ref, aro_ref, mao_ref, ids, pt)
    next(building)

    def preconditioned(v, at):
        out = []
        for m in range(at.start // 128, at.stop // 128):
            x = v[:, m * 128 - at.start : (m + 1) * 128 - at.start]
            out.append(dot3(x, high[m], low_part[m], NT))
        return jnp.concatenate(out, axis=1)

    def observe(x, c, obs):
        if c == 0:
            load(x).wait()
        return obs + dot(got[x - 1, :, cols(c)], dv[x, :, cols(c)], NT)

    next(building)
    ca, ab, fwd, bwd = next(building)
    first, last = ids[:, 0:1], ids[:, n - 1 : n]
    head_map = spread(ca, jnp.where(ids == first, 1.0, 0.0))
    tail_map = spread(ab, jnp.where(ids == last, 1.0, 0.0))
    head_map = jnp.concatenate(
        [dot(head_map[:, c * n : (c + 1) * n], pt[c], NT, HI) for c in range(3)], axis=1
    )
    both_maps = jnp.concatenate([tail_map, head_map], axis=0)
    slots = jnp.concatenate([both_maps] * (n // 32), axis=0)
    slot_row = lax.broadcasted_iota(jnp.int32, slots.shape, 0) // 32
    top, rest = halves(jnp.where(slot_row == lax.rem(me, n // 32), slots, 0.0))
    map_high[...] = top
    map_low[...] = rest
    steps = [("a", 4), ("a", 2), ("a", 1), ("o", 1), ("o", 4), ("a", 6), ("o", 2), ("o", 6),
             ("b", 3), ("b", 5), ("b", 7)]
    if T != 8:
        steps = [("b", x) for x in plan]
    for what, x in steps:
        for c in range(CHUNKS):
            if what != "o":
                arrive(x, c)
            if what != "a":
                obs = observe(x, c, obs)
    half = rhs // 2
    summary = dot3(obs * gaps3, map_high[...], map_low[...], NT)
    part_out[...] = summary[:half] + pltpu.roll(summary[half:], n // 2, 1)
    obs_out[...] = obs
    pa_copies = [
        remote(part_out, part_in.at[k - 1], pa_s.at[k - 1], pa_r.at[k - 1], to_order(k))
        for k in range(1, O)
    ]
    ob_copies = [
        remote(obs_out, obs_in.at[k - 1], ob_s.at[k - 1], ob_r.at[k - 1], to_order(k))
        for k in range(1, O)
    ]
    for copy in pa_copies + ob_copies:
        copy.start()

    ids_e = []
    for e in range(T):
        v = ids
        for x in range(1, T):
            v = jnp.where(across(x) == e, ids_all[x - 1].astype(jnp.float32), v)
        ids_e.append(v)
    firsts = [v[:, 0:1] for v in ids_e]
    lasts = [v[:, n - 1 : n] for v in ids_e]
    runs = jnp.concatenate(
        [ca * jnp.where(v == f, 1.0, 0.0) for v, f in zip(ids_e, firsts)], axis=0
    )
    energy = dot(runs, tall(ca, n), NT, HI)
    energies = [bands(energy[16 * e : 16 * e + 16]) for e in range(T)]
    links = [None] + [jnp.where(lasts[e - 1] == firsts[e], 1.0, 0.0) for e in range(1, T)]
    throughs = [jnp.where(firsts[e] == lasts[e], 1.0, 0.0) for e in range(T)]
    direct = T <= 8
    if direct:
        weights = state_weights(T, me, (16, n), links, throughs, fwd, bwd, energies)

    for copy in pa_copies:
        copy.wait_recv()
    summ_out[...] = part_out[...] + sum([part_in[k] for k in range(1, O - 1)], part_in[0])
    su_copies = [
        remote(summ_out, summ_in.at[k - 1], su_s.at[k - 1], su_r.at[k - 1], to_tm(k))
        for k in range(1, T)
    ]
    for copy in su_copies:
        copy.start()
    if direct:
        top, rest = halves(dot(weights, tall(both_maps, n), NN, HI))
        cross_high[...] = top
        cross_low[...] = rest
    for copy in ob_copies:
        copy.wait_recv()
    for k in range(1, O):
        obs = obs + obs_in[k - 1]
    masked = obs * gaps3
    local_back = jnp.concatenate(
        [
            dot(dot(masked[:, c * n : (c + 1) * n], pt[c], NN, HI), pt[c], NT, HI)
            for c in range(3)
        ],
        axis=1,
    )
    get_precond.wait()
    for m in range(blocks):
        top, rest = halves(precond[m])
        high[m] = top
        low_part[m] = rest
    get_res.wait()
    applied[...] = preconditioned(res[...], slice(0, share))
    for copy in su_copies:
        copy.wait_recv()
    folded = []
    for e in range(T):
        slot = jnp.minimum(lax.rem(me - e + T - 1, T), T - 2)
        folded.append(jnp.where(me == e, summ_out[...], summ_in[slot]))
    lane8 = lax.broadcasted_iota(jnp.int32, (half, n), 1)
    groups = []
    for e in range(0, T, 4):
        front, back = folded[e] + folded[e + 1], folded[e + 2] + folded[e + 3]
        upper = jnp.where(lane8 < n // 2, front, back)
        lower = pltpu.roll(jnp.where(lane8 < n // 2, back, front), n // 2, 1)
        groups.append(jnp.concatenate([upper, lower], axis=0))
    if direct:
        adjoint = local_back + dot3(
            jnp.concatenate(groups, axis=1), cross_high[...], cross_low[...], NN
        )
    else:
        lane = lax.broadcasted_iota(jnp.int32, (rhs, n), 1)
        tails = [
            jnp.where(lane < 16, pltpu.roll(groups[e // 4], (n - 32 * (e % 4)) % n, 1), 0.0)
            for e in range(T)
        ]
        heads = [
            jnp.where(lane < 16, pltpu.roll(groups[e // 4], (n - 32 * (e % 4) - 16) % n, 1), 0.0)
            for e in range(T)
        ]
        state = jnp.zeros((rhs, n), jnp.float32)
        mine_in, mine_back, back, ins = state, state, state, []
        for e in range(T):
            entering = state if e == 0 else state * links[e]
            ins.append(entering)
            mine_in = jnp.where(me == e, entering, mine_in)
            state = tails[e] + throughs[e] * banded(entering, fwd)
        for e in range(T - 1, 0, -1):
            back = heads[e] + banded(ins[e], energies[e]) + throughs[e] * banded(back, bwd)
            back = back * links[e]
            mine_back = jnp.where(me == e - 1, back, mine_back)
        states = mine_back + pltpu.roll(mine_in, 16, 1)
        adjoint = local_back + dot(states, tall(both_maps, n), NN, HI)
    weighted = (adjoint * gaps3).astype(jnp.bfloat16)

    rs_copies = {}

    def sum_of(x, c):
        total = dot(weighted, dv[x, :, cols(c)], NN)
        if x == 0:
            total = total + kaula[:, cols(c)] * direc[:, cols(c)]
        for b in range(low(x)):
            rs_copies[x | 1 << b, c].wait_recv()
            total = total + rs_in[(x | 1 << b) - 1, :, cols(c)].astype(jnp.float32)
        return total

    for x in [7, 5, 3, 1, 6, 4, 2] if T == 8 else sorted(range(1, T), key=lambda x: (low(x), -x)):
        for c in range(CHUNKS):
            rs_out[x - 1, :, cols(c)] = sum_of(x, c).astype(LINK)
            rs_copies[x, c] = remote(
                rs_out.at[x - 1, :, cols(c)], rs_in.at[x - 1, :, cols(c)],
                rs_s.at[x - 1, c], rs_r.at[x - 1, c], {"tm": across(1 << low(x))},
            )
            rs_copies[x, c].start()
    for c in range(CHUNKS):
        piece = sum_of(0, c)
        image_out[:, cols(c)] = piece
        image_applied[:, cols(c)] = preconditioned(piece, cols(c))
    image = image_out[...]
    app, imapp = applied[...], image_applied[...]
    d, r = direc[...], res[...]
    lane = lax.broadcasted_iota(jnp.int32, (rhs, 128), 1)
    row = lax.broadcasted_iota(jnp.int32, (rhs, 128), 0)
    products = [r * app, d * image, image * app, image * imapp]
    total = jnp.zeros((rhs, 128), jnp.float32)
    for q, product in enumerate(products):
        total = jnp.where(lane == q * rhs + row, jnp.sum(product, axis=1, keepdims=True), total)
    total = jnp.sum(total, axis=0, keepdims=True)

    tot_out[...] = total
    tot_copies = []
    for i in range(O):
        for k in range(T):
            if i or k:
                at = i * T + k - 1
                tot_copies.append(
                    remote(tot_out, tot_in.at[at], t1_s.at[at], t1_r.at[at], to_all(k, i))
                )
    for copy in tot_copies:
        copy.start()
    for copy in tot_copies:
        copy.wait_recv()
    total = total + jnp.sum(tot_in[...], axis=0)
    wide = jnp.broadcast_to(total[0:1, :], (rhs, 128))
    old_rz, curvature, cross, quad = [
        jnp.sum(jnp.where(lane == q * rhs + row, wide, 0.0), axis=1, keepdims=True)
        for q in range(4)
    ]
    step = old_rz / curvature
    new_rz = old_rz - 2.0 * step * cross + step * step * quad
    comb_out[...] = app - step * imapp
    scal_out[...] = jnp.where(lane == 0, step, new_rz / old_rz)

    for copies in (id_copies, ga_copies, rs_copies):
        for copy in copies.values():
            copy.wait_send()
    for copy in pa_copies + ob_copies + su_copies + tot_copies:
        copy.wait_send()


def finish(image, comb, scal, sol, res, direc, new_sol, new_res, new_dir, got, put, isem, osem):
    def fetch(k, ref):
        return pltpu.make_async_copy(ref.at[:, 0, :], got.at[k], isem.at[k])

    def store(k, ref):
        return pltpu.make_async_copy(put.at[k], ref.at[:, 0, :], osem.at[k])

    for k, ref in ((2, direc), (0, sol), (1, res)):
        fetch(k, ref).start()
    step, ratio = scal[:, 0:1], scal[:, 1:2]
    fetch(2, direc).wait()
    put[2] = comb[...] + ratio * got[2]
    store(2, new_dir).start()
    fetch(0, sol).wait()
    put[0] = got[0] + step * got[2]
    store(0, new_sol).start()
    fetch(1, res).wait()
    put[1] = got[1] - step * image[...]
    store(1, new_res).start()
    for k, ref in ((2, new_dir), (0, new_sol), (1, new_res)):
        store(k, ref).wait()


def on_device(
    T, O, design, gap_flags, segment_ids, ar_order, ma_order, ar_roots, ma_roots,
    kaula, precond, solution, residual, direction,
):
    n = segment_ids.shape[0]
    columns = design.shape[2]
    share = direction.shape[2]
    rhs = direction.shape[0]
    blocks = precond.shape[1]
    f32, bf16 = jnp.float32, jnp.bfloat16
    vmem = pl.BlockSpec(memory_space=pltpu.VMEM)
    smem = pl.BlockSpec(memory_space=pltpu.SMEM)
    hbm = pl.BlockSpec(memory_space=pl.ANY)
    V, D = pltpu.VMEM, lambda *k: pltpu.SemaphoreType.DMA(k)
    vec = jax.ShapeDtypeStruct((rhs, share), f32)
    image, comb, scal = pl.pallas_call(
        functools.partial(kernel, T, O),
        out_shape=[vec, vec, jax.ShapeDtypeStruct((rhs, 128), f32)],
        in_specs=[hbm, vmem, vmem, smem, smem, smem, smem, vmem, hbm, hbm, hbm],
        out_specs=[vmem] * 3,
        scratch_shapes=[
            V((T, 3 * n, share), bf16), V((blocks, 128, 128), f32), V((rhs, share), f32),
            V((rhs, share), f32), V((rhs, share), bf16), V((blocks, 128, 128), bf16),
            V((blocks, 128, 128), bf16),
            V((T - 1, rhs, share), bf16),
            V((rhs, 3 * n), f32), V((O - 1, rhs, 3 * n), f32), V((T - 1, 1, n), jnp.int32),
            V((rhs // 2, n), f32), V((O - 1, rhs // 2, n), f32),
            V((rhs // 2, n), f32), V((T - 1, rhs // 2, n), f32), V((3, n, n), f32),
            V((n, 3 * n), bf16), V((n, 3 * n), bf16), V((32 * T, 3 * n), bf16), V((32 * T, 3 * n), bf16),
            V((T - 1, rhs, share), LINK), V((T - 1, rhs, share), LINK),
            V((rhs, share), f32), V((rhs, share), f32),
            V((1, 128), f32), V((T * O - 1, 1, 128), f32),
            D(T), D(3), D(T - 1, CHUNKS), D(T - 1, CHUNKS), D(O - 1), D(O - 1),
            D(T - 1), D(T - 1), D(O - 1), D(O - 1), D(T - 1), D(T - 1),
            D(T - 1, CHUNKS), D(T - 1, CHUNKS), D(T * O - 1), D(T * O - 1),
        ],
        compiler_params=pltpu.CompilerParams(
            collective_id=0, has_side_effects=True, vmem_limit_bytes=56 * 1024 * 1024
        ),
    )(
        design.reshape(3 * n, columns), segment_ids.reshape(1, n), gap_flags.reshape(1, n),
        ar_roots, ma_roots, ar_order, ma_order, kaula, precond[0], residual, direction,
    )
    full = jax.ShapeDtypeStruct(direction.shape, f32)
    return tuple(
        pl.pallas_call(
            finish,
            out_shape=[full] * 3,
            in_specs=[vmem, vmem, vmem, hbm, hbm, hbm],
            out_specs=[hbm] * 3,
            scratch_shapes=[V((3, rhs, share), f32), V((3, rhs, share), f32), D(3), D(3)],
        )(image, comb, scal, solution, residual, direction)
    )


def solution(mesh):
    vec = P(None, "order", "tm")
    in_specs = (
        P(None, "tm", "order"), P("tm"), P("tm"), P(), P(), P(), P(), P("order", "tm"),
        P("order", "tm", None, None), vec, vec, vec,
    )
    body = functools.partial(on_device, mesh.shape["tm"], mesh.shape["order"])
    return jax.shard_map(
        body, mesh=mesh, in_specs=in_specs, out_specs=(vec, vec, vec), check_vma=False
    )
```

```python
import functools

import jax
import jax.numpy as jnp
from jax import lax
from jax.experimental import pallas as pl
from jax.experimental.pallas import tpu as pltpu
from jax.sharding import PartitionSpec as P

LINK = jnp.bfloat16
LAGS = 4
CHUNKS = 2
HI = lax.Precision.HIGHEST
NN = (((1,), (0,)), ((), ()))
NT = (((1,), (1,)), ((), ()))


def dot(a, b, dims, precision=None):
    return lax.dot_general(a, b, dims, precision=precision, preferred_element_type=jnp.float32)


def tall(block, rows):
    return jnp.concatenate(
        [block, jnp.zeros((rows - block.shape[0], block.shape[1]), jnp.float32)], axis=0
    )


def halves(x):
    top = x.astype(jnp.bfloat16)
    return top, (x - top.astype(jnp.float32)).astype(jnp.bfloat16)


def dot3(x, high, low, dims):
    rows = x.shape[0]
    top, rest = halves(x)
    both = dot(jnp.concatenate([top, rest], axis=0), high, dims)
    return both[:rows] + both[rows:] + dot(top, low, dims)


def bands(matrix):
    row = lax.broadcasted_iota(jnp.int32, matrix.shape, 0)
    col = lax.broadcasted_iota(jnp.int32, matrix.shape, 1)
    return [
        jnp.sum(jnp.where(row == col - 4 * shift, matrix, 0.0), axis=0, keepdims=True)
        for shift in range(1 - LAGS, LAGS)
    ]


def banded(vector, coeffs):
    width = vector.shape[1]
    total = None
    for shift, coeff in zip(range(1 - LAGS, LAGS), coeffs):
        moved = vector if shift == 0 else pltpu.roll(vector, 4 * shift % width, 1)
        total = moved * coeff if total is None else total + moved * coeff
    return total


def columns(ref, order_ref, comp):
    out = []
    for k in range(LAGS):
        column = jnp.zeros(comp.shape, jnp.float32)
        for c in range(3):
            value = jnp.where(k < order_ref[c], ref[c, k], 0.0)
            column = jnp.where(comp == c, value, column)
        out.append(column)
    return out


def stack(pieces):
    row = lax.broadcasted_iota(jnp.int32, pieces[0].shape, 0)
    real = row % 4 < 3
    both = [jnp.where(row < 4, pieces[i], pieces[i + 1]) for i in range(0, LAGS, 2)]
    return jnp.concatenate([jnp.where(real, block, 0.0) for block in both], axis=0)


def filters(ar_ref, ma_ref, aro_ref, mao_ref, ids, pt_ref):
    n = ids.shape[1]
    lane = lax.broadcasted_iota(jnp.int32, (8, n), 1)
    comp = lax.broadcasted_iota(jnp.int32, (8, n), 0) % 4

    def lagged(v, k):
        return v if k == 0 else jnp.where(lane >= k, pltpu.roll(v, k, 1), 0.0)

    def at(k):
        return jnp.where(lane == k, 1.0, 0.0)

    ar, ma = columns(ar_ref, aro_ref, comp), columns(ma_ref, mao_ref, comp)
    a, b = [1.0] + [0.0] * LAGS, [1.0] + [0.0] * LAGS
    for k in range(LAGS):
        a = [a[0]] + [a[j] - ar[k] * a[j - 1] for j in range(1, LAGS + 1)]
        b = [b[0]] + [b[j] - ma[k] * b[j - 1] for j in range(1, LAGS + 1)]
    h, power, m = at(0), ar, 1
    while m < n:
        s0, q0 = power[0] + power[1], power[0] * power[1]
        s1, q1 = power[2] + power[3], power[2] * power[3]
        e = [s0 + s1, q0 + q1 + s0 * s1, q0 * s1 + s0 * q1, q0 * q1]
        terms = [e[j] * lagged(h, (j + 1) * m) for j in range(LAGS) if (j + 1) * m < n]
        while len(terms) > 1:
            terms = [sum(terms[i + 1 : i + 2], terms[i]) for i in range(0, len(terms), 2)]
        h = h + terms[0]
        power, m = [p * p for p in power], 2 * m
    hs = [lagged(h, k) for k in range(LAGS + 1)]
    g = hs[0] + ((b[1] * hs[1] + b[2] * hs[2]) + (b[3] * hs[3] + b[4] * hs[4]))
    gs = [lagged(g, k) for k in range(LAGS)]
    ins, ends = [], []
    for i in range(1, LAGS + 1):
        acc, end = jnp.zeros_like(g), jnp.zeros_like(g)
        for k in range(LAGS + 1 - i):
            acc = acc + b[i + k] * at(k) - a[i + k] * gs[k]
            end = end - a[i + k] * at(n - 1 - k)
        ins.append(acc)
        ends.append(end)
    yield None
    row = lax.broadcasted_iota(jnp.int32, (n, n), 0)
    col = lax.broadcasted_iota(jnp.int32, (n, n), 1)
    grid = jnp.broadcast_to(ids, (n, n))
    joined = (grid == grid.T) & (col >= row)
    for c in range(3):
        t = pltpu.roll(jnp.broadcast_to(g[c : c + 1], (n, n)), 0, 1, stride=1, stride_axis=0)
        pt_ref[c] = jnp.where(joined, t, 0.0)
    yield None
    ca, ends = stack(hs[:LAGS]), stack(ends)
    flip = jnp.where(row + col == n - 1, 1.0, 0.0).astype(jnp.float32)
    ab = dot(stack(ins), flip, NN, HI)
    fwd = bands(dot(ca, tall(ends, n), NT, HI))
    bwd = bands(dot(ends, tall(ca, n), NT, HI))
    yield ca, ab, fwd, bwd


def spread(block, mask):
    row = lax.broadcasted_iota(jnp.int32, block.shape, 0)
    return jnp.concatenate(
        [jnp.where(row % 4 == c, block * mask, 0.0) for c in range(3)], axis=1
    )


def state_weights(T, me, shape, links, throughs, fwd, bwd, energies):
    row = lax.broadcasted_iota(jnp.int32, shape, 0)
    lane = lax.broadcasted_iota(jnp.int32, shape, 1)
    eye = jnp.where(row == lane, 1.0, 0.0)
    zero = jnp.zeros(shape, jnp.float32)
    state, ins, mine = {}, [], {}

    def keep(blocks, e, into):
        for key, v in blocks.items():
            mine[into, key] = jnp.where(me == e, v, mine.get((into, key), zero))

    for e in range(T):
        entering = {q: v * links[e] for q, v in state.items()}
        ins.append(entering)
        keep(entering, e, "in")
        state = {q: throughs[e] * banded(v, fwd) for q, v in entering.items()}
        state[e] = eye
    back = {}
    for e in range(T - 1, 0, -1):
        new = {key: throughs[e] * banded(v, bwd) for key, v in back.items()}
        for q, v in ins[e].items():
            moved = banded(v, energies[e])
            new["tail", q] = new["tail", q] + moved if ("tail", q) in new else moved
        new["head", e] = eye
        back = {key: v * links[e] for key, v in new.items()}
        keep(back, e - 1, "back")
    out = []
    for e in range(T):
        entering = pltpu.roll(mine["in", e], 16, 1) if ("in", e) in mine else zero
        out.append(mine.get(("back", ("tail", e)), zero) + entering)
        out.append(mine.get(("back", ("head", e)), zero))
    return jnp.concatenate(out, axis=0)


def kernel(
    T, O,
    design, ids_hbm, gaps_hbm, ar_hbm, ma_hbm, aro_hbm, mao_hbm, kaula_hbm, precond_in,
    sol_in, res_in, direc_in,
    new_sol, new_res, new_dir,
    ids_in, gaps_in, ar_ref, ma_ref, aro_ref, mao_ref, kaula, dv, precond, sol, res, direc, packed, high, low_part,
    image_out, got, obs_out, obs_in, ids_all, part_out, part_in, summ_out, summ_in, pt,
    map_high, map_low, cross_high, cross_low, rs_out, rs_in, applied, image_applied,
    tot_out, tot_in,
    dsem, in_sem, ga_s, ga_r, ob_s, ob_r, id_s, id_r, pa_s, pa_r, su_s, su_r,
    rs_s, rs_r, t1_s, t1_r,
):
    me, order = lax.axis_index("tm"), lax.axis_index("order")
    rhs, share = packed.shape
    n = ids_in.shape[1]
    blocks = precond.shape[0]
    wide = share // CHUNKS
    bits = T.bit_length() - 1

    def low(x):
        return (x & -x).bit_length() - 1 if x else bits

    def across(x):
        out = me
        for b in range(bits):
            if x >> b & 1:
                out = out + (1 << b) * (1 - 2 * lax.rem(lax.div(me, 1 << b), 2))
        return out

    def cols(c):
        return slice(c * wide, (c + 1) * wide)

    mesh_ids = pl.DeviceIdType.MESH

    def to_tm(k):
        return {"tm": lax.rem(me + k, T)}

    def to_order(k):
        return {"order": lax.rem(order + k, O)}

    def to_all(k, i):
        return {"tm": lax.rem(me + k, T), "order": lax.rem(order + i, O)}

    def load(x):
        return pltpu.make_async_copy(
            design.at[:, pl.ds(pl.multiple_of(across(x) * share, 128), share)],
            dv.at[x],
            dsem.at[x],
        )

    def remote(src, dst, ssem, rsem, to):
        return pltpu.make_async_remote_copy(
            src_ref=src, dst_ref=dst, send_sem=ssem, recv_sem=rsem,
            device_id=to, device_id_type=mesh_ids,
        )

    get_direc = pltpu.make_async_copy(direc_in.at[:, 0, :], direc, in_sem.at[0])
    get_res = pltpu.make_async_copy(res_in.at[:, 0, :], res, in_sem.at[1])
    get_sol = pltpu.make_async_copy(sol_in.at[:, 0, :], sol, in_sem.at[3])
    get_precond = pltpu.make_async_copy(precond_in, precond, in_sem.at[2])
    get_direc.start()
    get_small = [
        pltpu.make_async_copy(src, dst, in_sem.at[4 + k])
        for k, (src, dst) in enumerate((
            (ids_hbm, ids_in), (ar_hbm, ar_ref), (ma_hbm, ma_ref), (aro_hbm, aro_ref),
            (mao_hbm, mao_ref), (gaps_hbm, gaps_in), (kaula_hbm, kaula),
        ))
    ]
    barrier = pltpu.get_barrier_semaphore()
    for b in range(bits):
        pl.semaphore_signal(
            barrier, inc=1, device_id={"tm": across(1 << b)}, device_id_type=mesh_ids
        )
    for k in range(1, O):
        pl.semaphore_signal(barrier, inc=1, device_id=to_order(k), device_id_type=mesh_ids)
    plan = [4, 2, 1, 6, 3, 5, 7] if T == 8 else sorted(range(1, T), key=lambda x: -low(x))
    for copy in get_small:
        copy.start()
    load(0).start()
    for x in plan:
        load(x).start()
    get_precond.start()
    get_res.start()
    get_sol.start()
    get_direc.wait()
    packed[...] = direc[...].astype(jnp.bfloat16)
    get_small[0].wait()
    pl.semaphore_wait(barrier, bits + O - 1)

    id_copies, ga_copies = {}, {}

    def pass_on(x, c):
        for b in reversed(range(low(x))):
            to = x | 1 << b
            if c == 0:
                id_copies[to] = remote(
                    ids_all.at[x - 1] if x else ids_in, ids_all.at[to - 1],
                    id_s.at[to - 1], id_r.at[to - 1], {"tm": across(1 << b)},
                )
                id_copies[to].start()
            ga_copies[to, c] = remote(
                (got.at[x - 1] if x else packed).at[:, cols(c)], got.at[to - 1, :, cols(c)],
                ga_s.at[to - 1, c], ga_r.at[to - 1, c], {"tm": across(1 << b)},
            )
            ga_copies[to, c].start()

    def arrive(x, c):
        if c == 0:
            id_copies[x].wait_recv()
        ga_copies[x, c].wait_recv()
        pass_on(x, c)

    for c in range(CHUNKS):
        pass_on(0, c)

    for copy in get_small[1:]:
        copy.wait()
    load(0).wait()
    obs = dot(packed[...], dv[0], NT)
    ids = ids_in[0:1, :].astype(jnp.float32)
    gaps3 = jnp.concatenate([gaps_in[0:1, :].astype(jnp.float32)] * 3, axis=1)
    building = filters(ar_ref, ma_ref, aro_ref, mao_ref, ids, pt)
    next(building)

    def preconditioned(v, at):
        out = []
        for m in range(at.start // 128, at.stop // 128):
            x = v[:, m * 128 - at.start : (m + 1) * 128 - at.start]
            out.append(dot3(x, high[m], low_part[m], NT))
        return jnp.concatenate(out, axis=1)

    def observe(x, c, obs):
        if c == 0:
            load(x).wait()
        return obs + dot(got[x - 1, :, cols(c)], dv[x, :, cols(c)], NT)

    next(building)
    ca, ab, fwd, bwd = next(building)
    first, last = ids[:, 0:1], ids[:, n - 1 : n]
    head_map = spread(ca, jnp.where(ids == first, 1.0, 0.0))
    tail_map = spread(ab, jnp.where(ids == last, 1.0, 0.0))
    head_map = jnp.concatenate(
        [dot(head_map[:, c * n : (c + 1) * n], pt[c], NT, HI) for c in range(3)], axis=1
    )
    both_maps = jnp.concatenate([tail_map, head_map], axis=0)
    slots = jnp.concatenate([both_maps] * (n // 32), axis=0)
    slot_row = lax.broadcasted_iota(jnp.int32, slots.shape, 0) // 32
    top, rest = halves(jnp.where(slot_row == lax.rem(me, n // 32), slots, 0.0))
    map_high[...] = top
    map_low[...] = rest
    steps = [("a", 4), ("a", 2), ("a", 1), ("o", 1), ("o", 4), ("a", 6), ("o", 2), ("o", 6),
             ("b", 3), ("b", 5), ("b", 7)]
    if T != 8:
        steps = [("b", x) for x in plan]
    for what, x in steps:
        for c in range(CHUNKS):
            if what != "o":
                arrive(x, c)
            if what != "a":
                obs = observe(x, c, obs)
    half = rhs // 2
    summary = dot3(obs * gaps3, map_high[...], map_low[...], NT)
    part_out[...] = summary[:half] + pltpu.roll(summary[half:], n // 2, 1)
    obs_out[...] = obs
    pa_copies = [
        remote(part_out, part_in.at[k - 1], pa_s.at[k - 1], pa_r.at[k - 1], to_order(k))
        for k in range(1, O)
    ]
    ob_copies = [
        remote(obs_out, obs_in.at[k - 1], ob_s.at[k - 1], ob_r.at[k - 1], to_order(k))
        for k in range(1, O)
    ]
    for copy in pa_copies + ob_copies:
        copy.start()

    ids_e = []
    for e in range(T):
        v = ids
        for x in range(1, T):
            v = jnp.where(across(x) == e, ids_all[x - 1].astype(jnp.float32), v)
        ids_e.append(v)
    firsts = [v[:, 0:1] for v in ids_e]
    lasts = [v[:, n - 1 : n] for v in ids_e]
    runs = jnp.concatenate(
        [ca * jnp.where(v == f, 1.0, 0.0) for v, f in zip(ids_e, firsts)], axis=0
    )
    energy = dot(runs, tall(ca, n), NT, HI)
    energies = [bands(energy[16 * e : 16 * e + 16]) for e in range(T)]
    links = [None] + [jnp.where(lasts[e - 1] == firsts[e], 1.0, 0.0) for e in range(1, T)]
    throughs = [jnp.where(firsts[e] == lasts[e], 1.0, 0.0) for e in range(T)]
    direct = T <= 8
    if direct:
        weights = state_weights(T, me, (16, n), links, throughs, fwd, bwd, energies)

    for copy in pa_copies:
        copy.wait_recv()
    summ_out[...] = part_out[...] + sum([part_in[k] for k in range(1, O - 1)], part_in[0])
    su_copies = [
        remote(summ_out, summ_in.at[k - 1], su_s.at[k - 1], su_r.at[k - 1], to_tm(k))
        for k in range(1, T)
    ]
    for copy in su_copies:
        copy.start()
    if direct:
        top, rest = halves(dot(weights, tall(both_maps, n), NN, HI))
        cross_high[...] = top
        cross_low[...] = rest
    for copy in ob_copies:
        copy.wait_recv()
    for k in range(1, O):
        obs = obs + obs_in[k - 1]
    masked = obs * gaps3
    local_back = jnp.concatenate(
        [
            dot(dot(masked[:, c * n : (c + 1) * n], pt[c], NN, HI), pt[c], NT, HI)
            for c in range(3)
        ],
        axis=1,
    )
    get_precond.wait()
    for m in range(blocks):
        top, rest = halves(precond[m])
        high[m] = top
        low_part[m] = rest
    get_res.wait()
    applied[...] = preconditioned(res[...], slice(0, share))
    for copy in su_copies:
        copy.wait_recv()
    folded = []
    for e in range(T):
        slot = jnp.minimum(lax.rem(me - e + T - 1, T), T - 2)
        folded.append(jnp.where(me == e, summ_out[...], summ_in[slot]))
    lane8 = lax.broadcasted_iota(jnp.int32, (half, n), 1)
    groups = []
    for e in range(0, T, 4):
        front, back = folded[e] + folded[e + 1], folded[e + 2] + folded[e + 3]
        upper = jnp.where(lane8 < n // 2, front, back)
        lower = pltpu.roll(jnp.where(lane8 < n // 2, back, front), n // 2, 1)
        groups.append(jnp.concatenate([upper, lower], axis=0))
    if direct:
        adjoint = local_back + dot3(
            jnp.concatenate(groups, axis=1), cross_high[...], cross_low[...], NN
        )
    else:
        lane = lax.broadcasted_iota(jnp.int32, (rhs, n), 1)
        tails = [
            jnp.where(lane < 16, pltpu.roll(groups[e // 4], (n - 32 * (e % 4)) % n, 1), 0.0)
            for e in range(T)
        ]
        heads = [
            jnp.where(lane < 16, pltpu.roll(groups[e // 4], (n - 32 * (e % 4) - 16) % n, 1), 0.0)
            for e in range(T)
        ]
        state = jnp.zeros((rhs, n), jnp.float32)
        mine_in, mine_back, back, ins = state, state, state, []
        for e in range(T):
            entering = state if e == 0 else state * links[e]
            ins.append(entering)
            mine_in = jnp.where(me == e, entering, mine_in)
            state = tails[e] + throughs[e] * banded(entering, fwd)
        for e in range(T - 1, 0, -1):
            back = heads[e] + banded(ins[e], energies[e]) + throughs[e] * banded(back, bwd)
            back = back * links[e]
            mine_back = jnp.where(me == e - 1, back, mine_back)
        states = mine_back + pltpu.roll(mine_in, 16, 1)
        adjoint = local_back + dot(states, tall(both_maps, n), NN, HI)
    weighted = (adjoint * gaps3).astype(jnp.bfloat16)

    rs_copies = {}

    def sum_of(x, c):
        total = dot(weighted, dv[x, :, cols(c)], NN)
        if x == 0:
            total = total + kaula[:, cols(c)] * direc[:, cols(c)]
        for b in range(low(x)):
            rs_copies[x | 1 << b, c].wait_recv()
            total = total + rs_in[(x | 1 << b) - 1, :, cols(c)].astype(jnp.float32)
        return total

    for x in [7, 5, 3, 1, 6, 4, 2] if T == 8 else sorted(range(1, T), key=lambda x: (low(x), -x)):
        for c in range(CHUNKS):
            rs_out[x - 1, :, cols(c)] = sum_of(x, c).astype(LINK)
            rs_copies[x, c] = remote(
                rs_out.at[x - 1, :, cols(c)], rs_in.at[x - 1, :, cols(c)],
                rs_s.at[x - 1, c], rs_r.at[x - 1, c], {"tm": across(1 << low(x))},
            )
            rs_copies[x, c].start()
    for c in range(CHUNKS):
        piece = sum_of(0, c)
        image_out[:, cols(c)] = piece
        image_applied[:, cols(c)] = preconditioned(piece, cols(c))
    image = image_out[...]
    get_sol.wait()
    app, imapp = applied[...], image_applied[...]
    d, r = direc[...], res[...]
    lane = lax.broadcasted_iota(jnp.int32, (rhs, 128), 1)
    row = lax.broadcasted_iota(jnp.int32, (rhs, 128), 0)
    products = [r * app, d * image, image * app, image * imapp]
    total = jnp.zeros((rhs, 128), jnp.float32)
    for q, product in enumerate(products):
        total = jnp.where(lane == q * rhs + row, jnp.sum(product, axis=1, keepdims=True), total)
    total = jnp.sum(total, axis=0, keepdims=True)

    tot_out[...] = total
    tot_copies = []
    for i in range(O):
        for k in range(T):
            if i or k:
                at = i * T + k - 1
                tot_copies.append(
                    remote(tot_out, tot_in.at[at], t1_s.at[at], t1_r.at[at], to_all(k, i))
                )
    for copy in tot_copies:
        copy.start()
    for copy in tot_copies:
        copy.wait_recv()
    total = total + jnp.sum(tot_in[...], axis=0)
    wide = jnp.broadcast_to(total[0:1, :], (rhs, 128))
    old_rz, curvature, cross, quad = [
        jnp.sum(jnp.where(lane == q * rhs + row, wide, 0.0), axis=1, keepdims=True)
        for q in range(4)
    ]
    step = old_rz / curvature
    new_rz = old_rz - 2.0 * step * cross + step * step * quad
    new_sol[...] = sol[...] + step * d
    new_res[...] = r - step * image
    new_dir[...] = app - step * imapp + (new_rz / old_rz) * d
    for copies in (id_copies, ga_copies, rs_copies):
        for copy in copies.values():
            copy.wait_send()
    for copy in pa_copies + ob_copies + su_copies + tot_copies:
        copy.wait_send()


def finish(new_sol, new_res, new_dir, sol_out, res_out, dir_out, sem):
    copies = [
        pltpu.make_async_copy(src, dst.at[:, 0, :], sem.at[k])
        for k, (src, dst) in enumerate(
            ((new_sol, sol_out), (new_res, res_out), (new_dir, dir_out))
        )
    ]
    for copy in copies:
        copy.start()
    for copy in copies:
        copy.wait()


def on_device(
    T, O, design, gap_flags, segment_ids, ar_order, ma_order, ar_roots, ma_roots,
    kaula, precond, solution, residual, direction,
):
    n = segment_ids.shape[0]
    columns = design.shape[2]
    share = direction.shape[2]
    rhs = direction.shape[0]
    blocks = precond.shape[1]
    f32, bf16 = jnp.float32, jnp.bfloat16
    vmem = pl.BlockSpec(memory_space=pltpu.VMEM)
    hbm = pl.BlockSpec(memory_space=pl.ANY)
    V, S, D = pltpu.VMEM, pltpu.SMEM, lambda *k: pltpu.SemaphoreType.DMA(k)
    vec = pltpu.VMEM((rhs, share), f32)
    results = pl.pallas_call(
        functools.partial(kernel, T, O),
        out_shape=[vec] * 3,
        in_specs=[hbm] * 12,
        out_specs=[vmem] * 3,
        scratch_shapes=[
            V((1, n), jnp.int32), V((1, n), jnp.int32), S((3, 4), f32), S((3, 4), f32),
            S((3,), jnp.int32), S((3,), jnp.int32), V((1, share), f32),
            V((T, 3 * n, share), bf16), V((blocks, 128, 128), f32), V((rhs, share), f32),
            V((rhs, share), f32), V((rhs, share), f32), V((rhs, share), bf16), V((blocks, 128, 128), bf16),
            V((blocks, 128, 128), bf16),
            V((rhs, share), f32), V((T - 1, rhs, share), bf16),
            V((rhs, 3 * n), f32), V((O - 1, rhs, 3 * n), f32), V((T - 1, 1, n), jnp.int32),
            V((rhs // 2, n), f32), V((O - 1, rhs // 2, n), f32),
            V((rhs // 2, n), f32), V((T - 1, rhs // 2, n), f32), V((3, n, n), f32),
            V((n, 3 * n), bf16), V((n, 3 * n), bf16), V((32 * T, 3 * n), bf16), V((32 * T, 3 * n), bf16),
            V((T - 1, rhs, share), LINK), V((T - 1, rhs, share), LINK),
            V((rhs, share), f32), V((rhs, share), f32),
            V((1, 128), f32), V((T * O - 1, 1, 128), f32),
            D(T), D(11), D(T - 1, CHUNKS), D(T - 1, CHUNKS), D(O - 1), D(O - 1),
            D(T - 1), D(T - 1), D(O - 1), D(O - 1), D(T - 1), D(T - 1),
            D(T - 1, CHUNKS), D(T - 1, CHUNKS), D(T * O - 1), D(T * O - 1),
        ],
        compiler_params=pltpu.CompilerParams(
            collective_id=0, has_side_effects=True, vmem_limit_bytes=28 * 1024 * 1024
        ),
    )(*[
        pltpu.with_memory_space_constraint(v, pltpu.HBM)
        for v in (
            design.reshape(3 * n, columns), segment_ids.reshape(1, n), gap_flags.reshape(1, n),
            ar_roots, ma_roots, ar_order, ma_order, kaula, precond[0], solution, residual,
            direction,
        )
    ])
    full = jax.ShapeDtypeStruct(direction.shape, f32)
    return tuple(
        pl.pallas_call(
            finish,
            out_shape=[full] * 3,
            in_specs=[vmem] * 3,
            out_specs=[hbm] * 3,
            scratch_shapes=[D(3)],
            compiler_params=pltpu.CompilerParams(vmem_limit_bytes=1024 * 1024),
        )(*[pltpu.with_memory_space_constraint(v, pltpu.VMEM) for v in results])
    )


def solution(mesh):
    vec = P(None, "order", "tm")
    in_specs = (
        P(None, "tm", "order"), P("tm"), P("tm"), P(), P(), P(), P(), P("order", "tm"),
        P("order", "tm", None, None), vec, vec, vec,
    )
    body = functools.partial(on_device, mesh.shape["tm"], mesh.shape["order"])
    return jax.shard_map(
        body, mesh=mesh, in_specs=in_specs, out_specs=(vec, vec, vec), check_vma=False
    )
```

```python
import functools

import jax
import jax.numpy as jnp
from jax import lax
from jax.experimental import pallas as pl
from jax.experimental.pallas import tpu as pltpu
from jax.sharding import PartitionSpec as P

LINK = jnp.bfloat16
LAGS = 4
CHUNKS = 2
APPLIED_AFTER = 5
HI = lax.Precision.HIGHEST
NN = (((1,), (0,)), ((), ()))
NT = (((1,), (1,)), ((), ()))


def dot(a, b, dims, precision=None):
    return lax.dot_general(a, b, dims, precision=precision, preferred_element_type=jnp.float32)


def tall(block, rows):
    return jnp.concatenate(
        [block, jnp.zeros((rows - block.shape[0], block.shape[1]), jnp.float32)], axis=0
    )


def halves(x):
    top = x.astype(jnp.bfloat16)
    return top, (x - top.astype(jnp.float32)).astype(jnp.bfloat16)


def dot3(x, high, low, dims):
    rows = x.shape[0]
    top, rest = halves(x)
    both = dot(jnp.concatenate([top, rest], axis=0), high, dims)
    return both[:rows] + both[rows:] + dot(top, low, dims)


def bands(matrix):
    row = lax.broadcasted_iota(jnp.int32, matrix.shape, 0)
    col = lax.broadcasted_iota(jnp.int32, matrix.shape, 1)
    return [
        jnp.sum(jnp.where(row == col - 4 * shift, matrix, 0.0), axis=0, keepdims=True)
        for shift in range(1 - LAGS, LAGS)
    ]


def banded(vector, coeffs):
    width = vector.shape[1]
    total = None
    for shift, coeff in zip(range(1 - LAGS, LAGS), coeffs):
        moved = vector if shift == 0 else pltpu.roll(vector, 4 * shift % width, 1)
        total = moved * coeff if total is None else total + moved * coeff
    return total


def columns(ref, order_ref, comp):
    out = []
    for k in range(LAGS):
        column = jnp.zeros(comp.shape, jnp.float32)
        for c in range(3):
            value = jnp.where(k < order_ref[c], ref[c, k], 0.0)
            column = jnp.where(comp == c, value, column)
        out.append(column)
    return out


def stack(pieces):
    row = lax.broadcasted_iota(jnp.int32, pieces[0].shape, 0)
    real = row % 4 < 3
    both = [jnp.where(row < 4, pieces[i], pieces[i + 1]) for i in range(0, LAGS, 2)]
    return jnp.concatenate([jnp.where(real, block, 0.0) for block in both], axis=0)


def filters(ar_ref, ma_ref, aro_ref, mao_ref, ids, pt_ref):
    n = ids.shape[1]
    lane = lax.broadcasted_iota(jnp.int32, (8, n), 1)
    comp = lax.broadcasted_iota(jnp.int32, (8, n), 0) % 4

    def lagged(v, k):
        return v if k == 0 else jnp.where(lane >= k, pltpu.roll(v, k, 1), 0.0)

    def at(k):
        return jnp.where(lane == k, 1.0, 0.0)

    ar, ma = columns(ar_ref, aro_ref, comp), columns(ma_ref, mao_ref, comp)
    a, b = [1.0] + [0.0] * LAGS, [1.0] + [0.0] * LAGS
    for k in range(LAGS):
        a = [a[0]] + [a[j] - ar[k] * a[j - 1] for j in range(1, LAGS + 1)]
        b = [b[0]] + [b[j] - ma[k] * b[j - 1] for j in range(1, LAGS + 1)]
    h, power, m = at(0), ar, 1
    while m < n:
        s0, q0 = power[0] + power[1], power[0] * power[1]
        s1, q1 = power[2] + power[3], power[2] * power[3]
        e = [s0 + s1, q0 + q1 + s0 * s1, q0 * s1 + s0 * q1, q0 * q1]
        terms = [e[j] * lagged(h, (j + 1) * m) for j in range(LAGS) if (j + 1) * m < n]
        while len(terms) > 1:
            terms = [sum(terms[i + 1 : i + 2], terms[i]) for i in range(0, len(terms), 2)]
        h = h + terms[0]
        power, m = [p * p for p in power], 2 * m
    hs = [lagged(h, k) for k in range(LAGS + 1)]
    g = hs[0] + ((b[1] * hs[1] + b[2] * hs[2]) + (b[3] * hs[3] + b[4] * hs[4]))
    gs = [lagged(g, k) for k in range(LAGS)]
    ins, ends = [], []
    for i in range(1, LAGS + 1):
        acc, end = jnp.zeros_like(g), jnp.zeros_like(g)
        for k in range(LAGS + 1 - i):
            acc = acc + b[i + k] * at(k) - a[i + k] * gs[k]
            end = end - a[i + k] * at(n - 1 - k)
        ins.append(acc)
        ends.append(end)
    yield None
    row = lax.broadcasted_iota(jnp.int32, (n, n), 0)
    col = lax.broadcasted_iota(jnp.int32, (n, n), 1)
    grid = jnp.broadcast_to(ids, (n, n))
    joined = (grid == grid.T) & (col >= row)
    for c in range(3):
        t = pltpu.roll(jnp.broadcast_to(g[c : c + 1], (n, n)), 0, 1, stride=1, stride_axis=0)
        pt_ref[c] = jnp.where(joined, t, 0.0)
    yield None
    ca, ends = stack(hs[:LAGS]), stack(ends)
    flip = jnp.where(row + col == n - 1, 1.0, 0.0).astype(jnp.float32)
    ab = dot(stack(ins), flip, NN, HI)
    fwd = bands(dot(ca, tall(ends, n), NT, HI))
    bwd = bands(dot(ends, tall(ca, n), NT, HI))
    yield ca, ab, fwd, bwd


def spread(block, mask):
    row = lax.broadcasted_iota(jnp.int32, block.shape, 0)
    return jnp.concatenate(
        [jnp.where(row % 4 == c, block * mask, 0.0) for c in range(3)], axis=1
    )


def state_weights(T, me, shape, links, throughs, fwd, bwd, energies):
    row = lax.broadcasted_iota(jnp.int32, shape, 0)
    lane = lax.broadcasted_iota(jnp.int32, shape, 1)
    eye = jnp.where(row == lane, 1.0, 0.0)
    zero = jnp.zeros(shape, jnp.float32)
    state, ins, mine = {}, [], {}

    def keep(blocks, e, into):
        for key, v in blocks.items():
            mine[into, key] = jnp.where(me == e, v, mine.get((into, key), zero))

    for e in range(T):
        entering = {q: v * links[e] for q, v in state.items()}
        ins.append(entering)
        keep(entering, e, "in")
        state = {q: throughs[e] * banded(v, fwd) for q, v in entering.items()}
        state[e] = eye
    back = {}
    for e in range(T - 1, 0, -1):
        new = {key: throughs[e] * banded(v, bwd) for key, v in back.items()}
        for q, v in ins[e].items():
            moved = banded(v, energies[e])
            new["tail", q] = new["tail", q] + moved if ("tail", q) in new else moved
        new["head", e] = eye
        back = {key: v * links[e] for key, v in new.items()}
        keep(back, e - 1, "back")
    out = []
    for e in range(T):
        entering = pltpu.roll(mine["in", e], 16, 1) if ("in", e) in mine else zero
        out.append(mine.get(("back", ("tail", e)), zero) + entering)
        out.append(mine.get(("back", ("head", e)), zero))
    return jnp.concatenate(out, axis=0)


def kernel(
    T, O,
    design, ids_hbm, gaps_hbm, ar_hbm, ma_hbm, aro_hbm, mao_hbm, kaula_hbm, precond_in,
    sol_in, res_in, direc_in,
    new_sol, new_res, new_dir,
    ids_in, gaps_in, ar_ref, ma_ref, aro_ref, mao_ref, kaula, dv, precond, sol, res, direc, packed, high, low_part,
    image_out, got, obs_out, obs_in, ids_all, summ_out, summ_in, pt,
    map_high, map_low, cross_high, cross_low, rs_out, rs_in, applied, image_applied,
    tot_out, tot_in,
    dsem, in_sem, ga_s, ga_r, ob_s, ob_r, id_s, id_r, su_s, su_r,
    rs_s, rs_r, t1_s, t1_r,
):
    me, order = lax.axis_index("tm"), lax.axis_index("order")
    rhs, share = packed.shape
    n = ids_in.shape[1]
    blocks = precond.shape[0]
    wide = share // CHUNKS
    bits = T.bit_length() - 1

    levels = [(1 << b,) for b in reversed(range(2, bits))] + [(3, 2, 1)]

    def level(x):
        return max([i for i, offsets in enumerate(levels) if any(x & o for o in offsets)], default=-1)

    def into(x):
        return [o for offsets in levels[level(x) + 1 :] for o in offsets]

    def across(x):
        out = me
        for b in range(bits):
            if x >> b & 1:
                out = out + (1 << b) * (1 - 2 * lax.rem(lax.div(me, 1 << b), 2))
        return out

    def cols(c):
        return slice(c * wide, (c + 1) * wide)

    mesh_ids = pl.DeviceIdType.MESH

    def to_tm(k):
        return {"tm": lax.rem(me + k, T)}

    def to_order(k):
        return {"order": lax.rem(order + k, O)}

    def to_all(k, i):
        return {"tm": lax.rem(me + k, T), "order": lax.rem(order + i, O)}

    def load(x):
        return pltpu.make_async_copy(
            design.at[:, pl.ds(pl.multiple_of(across(x) * share, 128), share)],
            dv.at[x],
            dsem.at[x],
        )

    def remote(src, dst, ssem, rsem, to):
        return pltpu.make_async_remote_copy(
            src_ref=src, dst_ref=dst, send_sem=ssem, recv_sem=rsem,
            device_id=to, device_id_type=mesh_ids,
        )

    get_direc = pltpu.make_async_copy(direc_in.at[:, 0, :], direc, in_sem.at[0])
    get_res = pltpu.make_async_copy(res_in.at[:, 0, :], res, in_sem.at[1])
    get_sol = pltpu.make_async_copy(sol_in.at[:, 0, :], sol, in_sem.at[3])
    get_precond = pltpu.make_async_copy(precond_in, precond, in_sem.at[2])
    get_direc.start()
    get_small = [
        pltpu.make_async_copy(src, dst, in_sem.at[4 + k])
        for k, (src, dst) in enumerate((
            (ids_hbm, ids_in), (ar_hbm, ar_ref), (ma_hbm, ma_ref), (aro_hbm, aro_ref),
            (mao_hbm, mao_ref), (gaps_hbm, gaps_in), (kaula_hbm, kaula),
        ))
    ]
    barrier = pltpu.get_barrier_semaphore()
    for x in into(0):
        pl.semaphore_signal(
            barrier, inc=1, device_id={"tm": across(x)}, device_id_type=mesh_ids
        )
    for k in range(1, O):
        pl.semaphore_signal(barrier, inc=1, device_id=to_order(k), device_id_type=mesh_ids)
    plan = sorted(range(1, T), key=lambda x: (level(x), x))
    for copy in get_small:
        copy.start()
    for x in range(T):
        load(x).start()
    get_precond.start()
    get_res.start()
    get_sol.start()
    get_direc.wait()
    packed[...] = direc[...].astype(jnp.bfloat16)
    get_small[0].wait()
    pl.semaphore_wait(barrier, len(into(0)) + O - 1)

    id_copies, ga_copies = {}, {}

    def pass_on(x, c):
        for o in into(x):
            to = x | o
            if c == 0:
                id_copies[to] = remote(
                    ids_all.at[x - 1] if x else ids_in, ids_all.at[to - 1],
                    id_s.at[to - 1], id_r.at[to - 1], {"tm": across(o)},
                )
                id_copies[to].start()
            ga_copies[to, c] = remote(
                (got.at[x - 1] if x else packed).at[:, cols(c)], got.at[to - 1, :, cols(c)],
                ga_s.at[to - 1, c], ga_r.at[to - 1, c], {"tm": across(o)},
            )
            ga_copies[to, c].start()

    def arrive(x, c):
        if c == 0:
            id_copies[x].wait_recv()
        ga_copies[x, c].wait_recv()
        pass_on(x, c)

    for c in range(CHUNKS):
        pass_on(0, c)

    for copy in get_small[1:]:
        copy.wait()
    ids = ids_in[0:1, :].astype(jnp.float32)
    gaps3 = jnp.concatenate([gaps_in[0:1, :].astype(jnp.float32)] * 3, axis=1)
    building = filters(ar_ref, ma_ref, aro_ref, mao_ref, ids, pt)
    next(building)

    def preconditioned(v, at):
        out = []
        for m in range(at.start // 128, at.stop // 128):
            x = v[:, m * 128 - at.start : (m + 1) * 128 - at.start]
            out.append(dot3(x, high[m], low_part[m], NT))
        return jnp.concatenate(out, axis=1)

    def observe(x, c, obs):
        if c == 0:
            load(x).wait()
        return obs + dot(got[x - 1, :, cols(c)], dv[x, :, cols(c)], NT)

    next(building)
    ca, ab, fwd, bwd = next(building)
    first, last = ids[:, 0:1], ids[:, n - 1 : n]
    head_map = spread(ca, jnp.where(ids == first, 1.0, 0.0))
    tail_map = spread(ab, jnp.where(ids == last, 1.0, 0.0))
    head_map = jnp.concatenate(
        [dot(head_map[:, c * n : (c + 1) * n], pt[c], NT, HI) for c in range(3)], axis=1
    )
    both_maps = jnp.concatenate([tail_map, head_map], axis=0)
    top, rest = halves(jnp.concatenate([both_maps] * 4, axis=0))
    map_high[...] = top
    map_low[...] = rest
    far = [x for x in plan if level(x) < len(levels) - 1]
    near = [x for x in plan if level(x) == len(levels) - 1]
    for x in far:
        for c in range(CHUNKS):
            arrive(x, c)
    load(0).wait()
    obs = dot(packed[...], dv[0], NT)
    for x in near[:3] + far + near[3:]:
        for c in range(CHUNKS):
            if x in near:
                arrive(x, c)
            obs = observe(x, c, obs)
    quarter = rhs // 4
    summary = dot3(obs * gaps3, map_high[...], map_low[...], NT)
    row = lax.broadcasted_iota(jnp.int32, summary.shape, 0)
    lane = lax.broadcasted_iota(jnp.int32, summary.shape, 1)
    turn = lax.rem(me, 4)
    summary = jnp.where(lane // 32 == (row // quarter + turn) % 4, summary, 0.0)
    summary = summary[: 2 * quarter] + summary[2 * quarter :]
    summary = summary[:quarter] + summary[quarter:]
    summ_out[...] = summary
    summ_in[order * T + me] = summary
    obs_out[...] = obs
    su_copies = []
    for k in list(range(1, T)) + [0]:
        for i in range(O):
            if i or k:
                at = i * T + k - 1
                su_copies.append(
                    remote(summ_out, summ_in.at[order * T + me], su_s.at[at], su_r.at[at], to_all(k, i))
                )
    ob_copies = [
        remote(obs_out, obs_in.at[k - 1], ob_s.at[k - 1], ob_r.at[k - 1], to_order(k))
        for k in range(1, O)
    ]
    for copy in su_copies + ob_copies:
        copy.start()

    ids_e = []
    for e in range(T):
        v = ids
        for x in range(1, T):
            v = jnp.where(across(x) == e, ids_all[x - 1].astype(jnp.float32), v)
        ids_e.append(v)
    firsts = [v[:, 0:1] for v in ids_e]
    lasts = [v[:, n - 1 : n] for v in ids_e]
    runs = jnp.concatenate(
        [ca * jnp.where(v == f, 1.0, 0.0) for v, f in zip(ids_e, firsts)], axis=0
    )
    energy = dot(runs, tall(ca, n), NT, HI)
    energies = [bands(energy[16 * e : 16 * e + 16]) for e in range(T)]
    links = [None] + [jnp.where(lasts[e - 1] == firsts[e], 1.0, 0.0) for e in range(1, T)]
    throughs = [jnp.where(firsts[e] == lasts[e], 1.0, 0.0) for e in range(T)]
    direct = T <= 8
    if direct:
        weights = state_weights(T, me, (16, n), links, throughs, fwd, bwd, energies)

    if direct:
        top, rest = halves(dot(weights, tall(both_maps, n), NN, HI))
        cross_high[...] = top
        cross_low[...] = rest
    for copy in ob_copies:
        copy.wait_recv()
    for k in range(1, O):
        obs = obs + obs_in[k - 1]
    masked = obs * gaps3
    local_back = jnp.concatenate(
        [
            dot(dot(masked[:, c * n : (c + 1) * n], pt[c], NN, HI), pt[c], NT, HI)
            for c in range(3)
        ],
        axis=1,
    )
    for copy in su_copies:
        copy.wait_recv()
    slot = lax.broadcasted_iota(jnp.int32, (quarter, n), 1) // 32
    sums = [sum([summ_in[i * T + e] for i in range(1, O)], summ_in[e]) for e in range(T)]
    groups = []
    for e in range(0, T, 4):
        rows = []
        for q in range(4):
            picked = sums[e + (3 - q) % 4]
            for at in range(3):
                picked = jnp.where(slot == at, sums[e + (at - q) % 4], picked)
            rows.append(pltpu.roll(picked, (n - 32 * q) % n, 1) if q else picked)
        groups.append(jnp.concatenate(rows, axis=0))
    if direct:
        adjoint = local_back + dot3(
            jnp.concatenate(groups, axis=1), cross_high[...], cross_low[...], NN
        )
    else:
        lane = lax.broadcasted_iota(jnp.int32, (rhs, n), 1)
        tails = [
            jnp.where(lane < 16, pltpu.roll(groups[e // 4], (n - 32 * (e % 4)) % n, 1), 0.0)
            for e in range(T)
        ]
        heads = [
            jnp.where(lane < 16, pltpu.roll(groups[e // 4], (n - 32 * (e % 4) - 16) % n, 1), 0.0)
            for e in range(T)
        ]
        state = jnp.zeros((rhs, n), jnp.float32)
        mine_in, mine_back, back, ins = state, state, state, []
        for e in range(T):
            entering = state if e == 0 else state * links[e]
            ins.append(entering)
            mine_in = jnp.where(me == e, entering, mine_in)
            state = tails[e] + throughs[e] * banded(entering, fwd)
        for e in range(T - 1, 0, -1):
            back = heads[e] + banded(ins[e], energies[e]) + throughs[e] * banded(back, bwd)
            back = back * links[e]
            mine_back = jnp.where(me == e - 1, back, mine_back)
        states = mine_back + pltpu.roll(mine_in, 16, 1)
        adjoint = local_back + dot(states, tall(both_maps, n), NN, HI)
    weighted = (adjoint * gaps3).astype(jnp.bfloat16)

    rs_copies = {}

    def sum_of(x, c):
        total = dot(weighted, dv[x, :, cols(c)], NN)
        if x == 0:
            total = total + kaula[:, cols(c)] * direc[:, cols(c)]
        for o in into(x):
            rs_copies[x | o, c].wait_recv()
            total = total + rs_in[(x | o) - 1, :, cols(c)].astype(jnp.float32)
        return total

    def give_precond():
        get_precond.wait()
        for m in range(blocks):
            top, rest = halves(precond[m])
            high[m] = top
            low_part[m] = rest
        get_res.wait()
        applied[...] = preconditioned(res[...], slice(0, share))

    def last_offset(x):
        return x & max(levels[level(x)])

    outgoing = sorted(range(1, T), key=lambda x: (-level(x), -x))
    for x in outgoing:
        for c in range(CHUNKS):
            rs_out[x - 1, :, cols(c)] = sum_of(x, c).astype(LINK)
            rs_copies[x, c] = remote(
                rs_out.at[x - 1, :, cols(c)], rs_in.at[x - 1, :, cols(c)],
                rs_s.at[x - 1, c], rs_r.at[x - 1, c], {"tm": across(last_offset(x))},
            )
            rs_copies[x, c].start()
        if x == outgoing[APPLIED_AFTER]:
            give_precond()
    for c in range(CHUNKS):
        piece = sum_of(0, c)
        image_out[:, cols(c)] = piece
        image_applied[:, cols(c)] = preconditioned(piece, cols(c))
    image = image_out[...]
    get_sol.wait()
    app, imapp = applied[...], image_applied[...]
    d, r = direc[...], res[...]
    lane = lax.broadcasted_iota(jnp.int32, (rhs, 128), 1)
    row = lax.broadcasted_iota(jnp.int32, (rhs, 128), 0)
    products = [r * app, d * image, image * app, image * imapp]
    total = jnp.zeros((rhs, 128), jnp.float32)
    for q, product in enumerate(products):
        total = jnp.where(lane == q * rhs + row, jnp.sum(product, axis=1, keepdims=True), total)
    total = jnp.sum(total, axis=0, keepdims=True)

    tot_out[...] = total
    tot_copies = []
    for i in range(O):
        for k in range(T):
            if i or k:
                at = i * T + k - 1
                tot_copies.append(
                    remote(tot_out, tot_in.at[at], t1_s.at[at], t1_r.at[at], to_all(k, i))
                )
    for copy in tot_copies:
        copy.start()
    for copy in tot_copies:
        copy.wait_recv()
    total = total + jnp.sum(tot_in[...], axis=0)
    wide = jnp.broadcast_to(total[0:1, :], (rhs, 128))
    old_rz, curvature, cross, quad = [
        jnp.sum(jnp.where(lane == q * rhs + row, wide, 0.0), axis=1, keepdims=True)
        for q in range(4)
    ]
    step = old_rz / curvature
    new_rz = old_rz - 2.0 * step * cross + step * step * quad
    new_sol[...] = sol[...] + step * d
    new_res[...] = r - step * image
    new_dir[...] = app - step * imapp + (new_rz / old_rz) * d
    for copies in (id_copies, ga_copies, rs_copies):
        for copy in copies.values():
            copy.wait_send()
    for copy in ob_copies + su_copies + tot_copies:
        copy.wait_send()


def finish(new_sol, new_res, new_dir, sol_out, res_out, dir_out, sem):
    copies = [
        pltpu.make_async_copy(src, dst.at[:, 0, :], sem.at[k])
        for k, (src, dst) in enumerate(
            ((new_sol, sol_out), (new_res, res_out), (new_dir, dir_out))
        )
    ]
    for copy in copies:
        copy.start()
    for copy in copies:
        copy.wait()


def on_device(
    T, O, design, gap_flags, segment_ids, ar_order, ma_order, ar_roots, ma_roots,
    kaula, precond, solution, residual, direction,
):
    n = segment_ids.shape[0]
    columns = design.shape[2]
    share = direction.shape[2]
    rhs = direction.shape[0]
    blocks = precond.shape[1]
    f32, bf16 = jnp.float32, jnp.bfloat16
    vmem = pl.BlockSpec(memory_space=pltpu.VMEM)
    hbm = pl.BlockSpec(memory_space=pl.ANY)
    V, S, D = pltpu.VMEM, pltpu.SMEM, lambda *k: pltpu.SemaphoreType.DMA(k)
    vec = pltpu.VMEM((rhs, share), f32)
    results = pl.pallas_call(
        functools.partial(kernel, T, O),
        out_shape=[vec] * 3,
        in_specs=[hbm] * 12,
        out_specs=[vmem] * 3,
        scratch_shapes=[
            V((1, n), jnp.int32), V((1, n), jnp.int32), S((3, 4), f32), S((3, 4), f32),
            S((3,), jnp.int32), S((3,), jnp.int32), V((1, share), f32),
            V((T, 3 * n, share), bf16), V((blocks, 128, 128), f32), V((rhs, share), f32),
            V((rhs, share), f32), V((rhs, share), f32), V((rhs, share), bf16), V((blocks, 128, 128), bf16),
            V((blocks, 128, 128), bf16),
            V((rhs, share), f32), V((T - 1, rhs, share), bf16),
            V((rhs, 3 * n), f32), V((O - 1, rhs, 3 * n), f32), V((T - 1, 1, n), jnp.int32),
            V((rhs // 4, n), f32), V((T * O, rhs // 4, n), f32), V((3, n, n), f32),
            V((n, 3 * n), bf16), V((n, 3 * n), bf16), V((32 * T, 3 * n), bf16), V((32 * T, 3 * n), bf16),
            V((T - 1, rhs, share), LINK), V((T - 1, rhs, share), LINK),
            V((rhs, share), f32), V((rhs, share), f32),
            V((1, 128), f32), V((T * O - 1, 1, 128), f32),
            D(T), D(11), D(T - 1, CHUNKS), D(T - 1, CHUNKS), D(O - 1), D(O - 1),
            D(T - 1), D(T - 1), D(T * O - 1), D(T * O - 1),
            D(T - 1, CHUNKS), D(T - 1, CHUNKS), D(T * O - 1), D(T * O - 1),
        ],
        compiler_params=pltpu.CompilerParams(
            collective_id=0, has_side_effects=True, vmem_limit_bytes=28 * 1024 * 1024
        ),
    )(*[
        pltpu.with_memory_space_constraint(v, pltpu.HBM)
        for v in (
            design.reshape(3 * n, columns), segment_ids.reshape(1, n), gap_flags.reshape(1, n),
            ar_roots, ma_roots, ar_order, ma_order, kaula, precond[0], solution, residual,
            direction,
        )
    ])
    full = jax.ShapeDtypeStruct(direction.shape, f32)
    return tuple(
        pl.pallas_call(
            finish,
            out_shape=[full] * 3,
            in_specs=[vmem] * 3,
            out_specs=[hbm] * 3,
            scratch_shapes=[D(3)],
            compiler_params=pltpu.CompilerParams(vmem_limit_bytes=1024 * 1024),
        )(*[pltpu.with_memory_space_constraint(v, pltpu.VMEM) for v in results])
    )


def solution(mesh):
    vec = P(None, "order", "tm")
    in_specs = (
        P(None, "tm", "order"), P("tm"), P("tm"), P(), P(), P(), P(), P("order", "tm"),
        P("order", "tm", None, None), vec, vec, vec,
    )
    body = functools.partial(on_device, mesh.shape["tm"], mesh.shape["order"])
    return jax.shard_map(
        body, mesh=mesh, in_specs=in_specs, out_specs=(vec, vec, vec), check_vma=False
    )
```

```python
import functools

import jax
import jax.numpy as jnp
from jax import lax
from jax.experimental import pallas as pl
from jax.experimental.pallas import tpu as pltpu
from jax.sharding import PartitionSpec as P

LINK = jnp.bfloat16
LAGS = 4
CHUNKS = 2
HI = lax.Precision.HIGHEST
NN = (((1,), (0,)), ((), ()))
NT = (((1,), (1,)), ((), ()))


def dot(a, b, dims, precision=None):
    return lax.dot_general(a, b, dims, precision=precision, preferred_element_type=jnp.float32)


def tall(block, rows):
    return jnp.concatenate(
        [block, jnp.zeros((rows - block.shape[0], block.shape[1]), jnp.float32)], axis=0
    )


def halves(x):
    top = x.astype(jnp.bfloat16)
    return top, (x - top.astype(jnp.float32)).astype(jnp.bfloat16)


def dot3(x, high, low, dims):
    rows = x.shape[0]
    top, rest = halves(x)
    both = dot(jnp.concatenate([top, rest], axis=0), high, dims)
    return both[:rows] + both[rows:] + dot(top, low, dims)


def bands(matrix):
    row = lax.broadcasted_iota(jnp.int32, matrix.shape, 0)
    col = lax.broadcasted_iota(jnp.int32, matrix.shape, 1)
    return [
        jnp.sum(jnp.where(row == col - 4 * shift, matrix, 0.0), axis=0, keepdims=True)
        for shift in range(1 - LAGS, LAGS)
    ]


def banded(vector, coeffs):
    width = vector.shape[1]
    total = None
    for shift, coeff in zip(range(1 - LAGS, LAGS), coeffs):
        moved = vector if shift == 0 else pltpu.roll(vector, 4 * shift % width, 1)
        total = moved * coeff if total is None else total + moved * coeff
    return total


def columns(ref, order_ref, comp):
    out = []
    for k in range(LAGS):
        column = jnp.zeros(comp.shape, jnp.float32)
        for c in range(3):
            value = jnp.where(k < order_ref[c], ref[c, k], 0.0)
            column = jnp.where(comp == c, value, column)
        out.append(column)
    return out


def stack(pieces):
    row = lax.broadcasted_iota(jnp.int32, pieces[0].shape, 0)
    real = row % 4 < 3
    both = [jnp.where(row < 4, pieces[i], pieces[i + 1]) for i in range(0, LAGS, 2)]
    return jnp.concatenate([jnp.where(real, block, 0.0) for block in both], axis=0)


def filters(ar_ref, ma_ref, aro_ref, mao_ref, ids, pt_ref):
    n = ids.shape[1]
    lane = lax.broadcasted_iota(jnp.int32, (8, n), 1)
    comp = lax.broadcasted_iota(jnp.int32, (8, n), 0) % 4

    def lagged(v, k):
        return v if k == 0 else jnp.where(lane >= k, pltpu.roll(v, k, 1), 0.0)

    def at(k):
        return jnp.where(lane == k, 1.0, 0.0)

    ar, ma = columns(ar_ref, aro_ref, comp), columns(ma_ref, mao_ref, comp)
    a, b = [1.0] + [0.0] * LAGS, [1.0] + [0.0] * LAGS
    for k in range(LAGS):
        a = [a[0]] + [a[j] - ar[k] * a[j - 1] for j in range(1, LAGS + 1)]
        b = [b[0]] + [b[j] - ma[k] * b[j - 1] for j in range(1, LAGS + 1)]
    h, power, m = at(0), ar, 1
    while m < n:
        s0, q0 = power[0] + power[1], power[0] * power[1]
        s1, q1 = power[2] + power[3], power[2] * power[3]
        e = [s0 + s1, q0 + q1 + s0 * s1, q0 * s1 + s0 * q1, q0 * q1]
        terms = [e[j] * lagged(h, (j + 1) * m) for j in range(LAGS) if (j + 1) * m < n]
        while len(terms) > 1:
            terms = [sum(terms[i + 1 : i + 2], terms[i]) for i in range(0, len(terms), 2)]
        h = h + terms[0]
        power, m = [p * p for p in power], 2 * m
    hs = [lagged(h, k) for k in range(LAGS + 1)]
    g = hs[0] + ((b[1] * hs[1] + b[2] * hs[2]) + (b[3] * hs[3] + b[4] * hs[4]))
    gs = [lagged(g, k) for k in range(LAGS)]
    ins, ends = [], []
    for i in range(1, LAGS + 1):
        acc, end = jnp.zeros_like(g), jnp.zeros_like(g)
        for k in range(LAGS + 1 - i):
            acc = acc + b[i + k] * at(k) - a[i + k] * gs[k]
            end = end - a[i + k] * at(n - 1 - k)
        ins.append(acc)
        ends.append(end)
    yield None
    row = lax.broadcasted_iota(jnp.int32, (n, n), 0)
    col = lax.broadcasted_iota(jnp.int32, (n, n), 1)
    grid = jnp.broadcast_to(ids, (n, n))
    joined = (grid == grid.T) & (col >= row)
    for c in range(3):
        t = pltpu.roll(jnp.broadcast_to(g[c : c + 1], (n, n)), 0, 1, stride=1, stride_axis=0)
        pt_ref[c] = jnp.where(joined, t, 0.0)
    yield None
    ca, ends = stack(hs[:LAGS]), stack(ends)
    flip = jnp.where(row + col == n - 1, 1.0, 0.0).astype(jnp.float32)
    ab = dot(stack(ins), flip, NN, HI)
    fwd = bands(dot(ca, tall(ends, n), NT, HI))
    bwd = bands(dot(ends, tall(ca, n), NT, HI))
    yield ca, ab, fwd, bwd


def spread(block, mask):
    row = lax.broadcasted_iota(jnp.int32, block.shape, 0)
    return jnp.concatenate(
        [jnp.where(row % 4 == c, block * mask, 0.0) for c in range(3)], axis=1
    )


def state_weights(T, me, shape, links, throughs, fwd, bwd, energies):
    row = lax.broadcasted_iota(jnp.int32, shape, 0)
    lane = lax.broadcasted_iota(jnp.int32, shape, 1)
    eye = jnp.where(row == lane, 1.0, 0.0)
    zero = jnp.zeros(shape, jnp.float32)
    state, ins, mine = {}, [], {}

    def keep(blocks, e, into):
        for key, v in blocks.items():
            mine[into, key] = jnp.where(me == e, v, mine.get((into, key), zero))

    for e in range(T):
        entering = {q: v * links[e] for q, v in state.items()}
        ins.append(entering)
        keep(entering, e, "in")
        state = {q: throughs[e] * banded(v, fwd) for q, v in entering.items()}
        state[e] = eye
    back = {}
    for e in range(T - 1, 0, -1):
        new = {key: throughs[e] * banded(v, bwd) for key, v in back.items()}
        for q, v in ins[e].items():
            moved = banded(v, energies[e])
            new["tail", q] = new["tail", q] + moved if ("tail", q) in new else moved
        new["head", e] = eye
        back = {key: v * links[e] for key, v in new.items()}
        keep(back, e - 1, "back")
    out = []
    for e in range(T):
        entering = pltpu.roll(mine["in", e], 16, 1) if ("in", e) in mine else zero
        out.append(mine.get(("back", ("tail", e)), zero) + entering)
        out.append(mine.get(("back", ("head", e)), zero))
    return jnp.concatenate(out, axis=0)


def kernel(
    T, O,
    design, ids_hbm, gaps_hbm, ar_hbm, ma_hbm, aro_hbm, mao_hbm, kaula_hbm, precond_in,
    sol_in, res_in, direc_in,
    new_sol, new_res, new_dir,
    ids_in, gaps_in, ar_ref, ma_ref, aro_ref, mao_ref, kaula, dv, precond, sol, res, direc, packed, split,
    image_out, got, obs_out, obs_in, ids_all, summ_out, summ_in, pt, back_high, back_low, local_back,
    map_high, map_low, cross_high, cross_low, rs_out, rs_in, parts, applied, image_applied,
    tot_out, tot_in,
    dsem, in_sem, ga_s, ga_r, ob_s, ob_r, id_s, id_r, su_s, su_r,
    rs_s, rs_r, t1_s, t1_r,
):
    me, order = lax.axis_index("tm"), lax.axis_index("order")
    rhs, share = packed.shape
    n = ids_in.shape[1]
    blocks = precond.shape[0]
    wide = share // CHUNKS
    bits = T.bit_length() - 1

    levels = [(1 << b,) for b in reversed(range(2, bits))] + [(3, 2, 1)]

    def level(x):
        return max([i for i, offsets in enumerate(levels) if any(x & o for o in offsets)], default=-1)

    def into(x):
        return [o for offsets in levels[level(x) + 1 :] for o in offsets]

    def place(x):
        out = me
        for b in range(bits):
            if x >> b & 1:
                out = out + (1 << b) * (1 - 2 * lax.rem(lax.div(me, 1 << b), 2))
        return out

    places = [place(x) for x in range(T)]

    def across(x):
        return places[x]

    def cols(c):
        return slice(c * wide, (c + 1) * wide)

    mesh_ids = pl.DeviceIdType.MESH
    apart = pl.when(me >= 0)

    def to_tm(k):
        return {"tm": lax.rem(me + k, T)}

    def to_order(k):
        return {"order": lax.rem(order + k, O)}

    def to_all(k, i):
        return {"tm": lax.rem(me + k, T), "order": lax.rem(order + i, O)}

    def load(x):
        return pltpu.make_async_copy(
            design.at[:, pl.ds(pl.multiple_of(across(x) * share, 128), share)],
            dv.at[x],
            dsem.at[x],
        )

    def remote(src, dst, ssem, rsem, to):
        return pltpu.make_async_remote_copy(
            src_ref=src, dst_ref=dst, send_sem=ssem, recv_sem=rsem,
            device_id=to, device_id_type=mesh_ids,
        )

    get_direc = pltpu.make_async_copy(direc_in.at[:, 0, :], direc, in_sem.at[0])
    get_res = pltpu.make_async_copy(res_in.at[:, 0, :], res, in_sem.at[1])
    get_sol = pltpu.make_async_copy(sol_in.at[:, 0, :], sol, in_sem.at[3])
    get_precond = pltpu.make_async_copy(precond_in, precond, in_sem.at[2])
    get_direc.start()
    get_small = [
        pltpu.make_async_copy(src, dst, in_sem.at[4 + k])
        for k, (src, dst) in enumerate((
            (ids_hbm, ids_in), (ar_hbm, ar_ref), (ma_hbm, ma_ref), (aro_hbm, aro_ref),
            (mao_hbm, mao_ref), (gaps_hbm, gaps_in), (kaula_hbm, kaula),
        ))
    ]
    barrier = pltpu.get_barrier_semaphore()
    for x in into(0):
        pl.semaphore_signal(
            barrier, inc=1, device_id={"tm": across(x)}, device_id_type=mesh_ids
        )
    for k in range(1, O):
        pl.semaphore_signal(barrier, inc=1, device_id=to_order(k), device_id_type=mesh_ids)
    plan = sorted(range(1, T), key=lambda x: (level(x), x))
    for copy in get_small:
        copy.start()
    for x in range(T):
        load(x).start()
    get_precond.start()
    get_res.start()
    get_sol.start()
    get_direc.wait()
    packed[...] = direc[...].astype(jnp.bfloat16)
    get_small[0].wait()
    pl.semaphore_wait(barrier, len(into(0)) + O - 1)

    id_copies, ga_copies = {}, {}

    def pass_on(x, c, offsets):
        for o in offsets:
            to = x | o
            if c == 0:
                id_copies[to] = remote(
                    ids_all.at[x - 1] if x else ids_in, ids_all.at[to - 1],
                    id_s, id_r.at[to - 1], {"tm": across(o)},
                )
                id_copies[to].start()
            ga_copies[to, c] = remote(
                (got.at[x - 1] if x else packed).at[:, cols(c)], got.at[to - 1, :, cols(c)],
                ga_s, ga_r.at[to - 1, c], {"tm": across(o)},
            )
            ga_copies[to, c].start()

    def arrive(x, c):
        if c == 0:
            id_copies[x].wait_recv()
        ga_copies[x, c].wait_recv()
        pass_on(x, c, into(x))

    for o in into(0):
        for c in range(CHUNKS):
            pass_on(0, c, [o])

    for copy in get_small[1:]:
        copy.wait()
    ids = ids_in[0:1, :].astype(jnp.float32)
    gaps3 = jnp.concatenate([gaps_in[0:1, :].astype(jnp.float32)] * 3, axis=1)
    building = filters(ar_ref, ma_ref, aro_ref, mao_ref, ids, pt)
    next(building)

    def preconditioned(v, at):
        out = []
        for m in range(at.start // 128, at.stop // 128):
            x = v[:, m * 128 - at.start : (m + 1) * 128 - at.start]
            top, rest = halves(x)
            both = dot(jnp.concatenate([top, rest], axis=0), split[m], NT)
            out.append(both[:rhs, :128] + both[rhs:, :128] + both[:rhs, 128:])
        return jnp.concatenate(out, axis=1)

    def observe(x, c, at):
        if c == 0:
            load(x).wait()

        @apart
        def _():
            for k in range(0, 3 * n, n):
                obs_out[:, k : k + n] += dot(got[x - 1, :, at], dv[x, k : k + n, at], NT)

    next(building)
    ca, ab, fwd, bwd = next(building)
    first, last = ids[:, 0:1], ids[:, n - 1 : n]
    head_map = spread(ca, jnp.where(ids == first, 1.0, 0.0))
    tail_map = spread(ab, jnp.where(ids == last, 1.0, 0.0))
    head_map = jnp.concatenate(
        [dot(head_map[:, c * n : (c + 1) * n], pt[c], NT, HI) for c in range(3)], axis=1
    )
    both_maps = jnp.concatenate([tail_map, head_map], axis=0)
    top, rest = halves(jnp.concatenate([both_maps] * 4, axis=0))
    map_high[...] = top
    map_low[...] = rest
    for c in range(3):
        top, rest = halves(dot(pt[c], pt[c], NT, HI))
        back_high[c] = top
        back_low[c] = rest
    load(0).wait()
    obs_out[...] = dot(packed[...], dv[0], NT)
    far = [x for x in plan if level(x) < len(levels) - 1]
    near = [x for x in plan if level(x) == len(levels) - 1]
    for x in far:
        for c in range(CHUNKS):
            arrive(x, c)
    for x in near[:3] + far + near[3:]:
        for c in range(CHUNKS):
            if x in near:
                arrive(x, c)
            if x == T - 1:
                observe(x, c, cols(c))
        if x < T - 1:
            observe(x, 0, slice(0, share))
    quarter = rhs // 4
    obs = obs_out[...]
    summary = dot3(obs * gaps3, map_high[...], map_low[...], NT)
    row = lax.broadcasted_iota(jnp.int32, summary.shape, 0)
    lane = lax.broadcasted_iota(jnp.int32, summary.shape, 1)
    turn = lax.rem(me, 4)
    summary = jnp.where(lane // 32 == (row // quarter + turn) % 4, summary, 0.0)
    summary = summary[: 2 * quarter] + summary[2 * quarter :]
    summary = summary[:quarter] + summary[quarter:]
    summ_out[...] = summary
    summ_in[order * T + me] = summary
    su_copies = []
    for k in list(range(1, T)) + [0]:
        for i in range(O):
            if i or k:
                su_copies.append(
                    remote(summ_out, summ_in.at[order * T + me], su_s, su_r, to_all(k, i))
                )
    ob_copies = [
        remote(obs_out, obs_in.at[k - 1], ob_s, ob_r, to_order(k))
        for k in range(1, O)
    ]
    for copy in su_copies + ob_copies:
        copy.start()

    direct = T <= 8

    def ranges():
        ids_e = []
        for e in range(T):
            v = ids
            for x in range(1, T):
                v = jnp.where(across(x) == e, ids_all[x - 1].astype(jnp.float32), v)
            ids_e.append(v)
        firsts = [v[:, 0:1] for v in ids_e]
        lasts = [v[:, n - 1 : n] for v in ids_e]
        runs = jnp.concatenate(
            [ca * jnp.where(v == f, 1.0, 0.0) for v, f in zip(ids_e, firsts)], axis=0
        )
        energy = dot(runs, tall(ca, n), NT, HI)
        energies = [bands(energy[16 * e : 16 * e + 16]) for e in range(T)]
        links = [None] + [
            jnp.where(lasts[e - 1] == firsts[e], 1.0, 0.0) for e in range(1, T)
        ]
        throughs = [jnp.where(firsts[e] == lasts[e], 1.0, 0.0) for e in range(T)]
        return links, throughs, energies

    if direct:
        @apart
        def _():
            links, throughs, energies = ranges()
            weights = state_weights(T, me, (16, n), links, throughs, fwd, bwd, energies)
            top, rest = halves(dot(weights, tall(both_maps, n), NN, HI))
            cross_high[...] = top
            cross_low[...] = rest
    else:
        links, throughs, energies = ranges()
    ob_all = remote(obs_in, obs_in, ob_s, ob_r, to_tm(1))
    ob_all.wait_recv()
    for k in range(1, O):
        obs = obs + obs_in[k - 1]
    masked = obs * gaps3
    for c in range(3):
        at = slice(c * n, (c + 1) * n)
        local_back[:, at] = dot3(masked[:, at], back_high[c], back_low[c], NN)
    others = summ_in.at[pl.ds(1, T * O - 1)]
    su_all = remote(others, others, su_s, su_r, to_tm(1))
    su_all.wait_recv()
    slot = lax.broadcasted_iota(jnp.int32, (quarter, n), 1) // 32
    sums = [sum([summ_in[i * T + e] for i in range(1, O)], summ_in[e]) for e in range(T)]
    groups = []
    for e in range(0, T, 4):
        rows = []
        for q in range(4):
            picked = sums[e + (3 - q) % 4]
            for at in range(3):
                picked = jnp.where(slot == at, sums[e + (at - q) % 4], picked)
            rows.append(pltpu.roll(picked, (n - 32 * q) % n, 1) if q else picked)
        groups.append(jnp.concatenate(rows, axis=0))
    if direct:
        adjoint = local_back[...] + dot3(
            jnp.concatenate(groups, axis=1), cross_high[...], cross_low[...], NN
        )
    else:
        lane = lax.broadcasted_iota(jnp.int32, (rhs, n), 1)
        tails = [
            jnp.where(lane < 16, pltpu.roll(groups[e // 4], (n - 32 * (e % 4)) % n, 1), 0.0)
            for e in range(T)
        ]
        heads = [
            jnp.where(lane < 16, pltpu.roll(groups[e // 4], (n - 32 * (e % 4) - 16) % n, 1), 0.0)
            for e in range(T)
        ]
        state = jnp.zeros((rhs, n), jnp.float32)
        mine_in, mine_back, back, ins = state, state, state, []
        for e in range(T):
            entering = state if e == 0 else state * links[e]
            ins.append(entering)
            mine_in = jnp.where(me == e, entering, mine_in)
            state = tails[e] + throughs[e] * banded(entering, fwd)
        for e in range(T - 1, 0, -1):
            back = heads[e] + banded(ins[e], energies[e]) + throughs[e] * banded(back, bwd)
            back = back * links[e]
            mine_back = jnp.where(me == e - 1, back, mine_back)
        states = mine_back + pltpu.roll(mine_in, 16, 1)
        adjoint = local_back[...] + dot(states, tall(both_maps, n), NN, HI)
    weighted = (adjoint * gaps3).astype(jnp.bfloat16)

    rs_copies = {}

    def part(x):
        return dot(weighted, dv[x], NN)

    def sum_of(x, c):
        total = parts[([0] + far).index(x), :, cols(c)]
        for o in into(x):
            rs_copies[x | o, c].wait_recv()
            total = total + rs_in[(x | o) - 1, :, cols(c)].astype(jnp.float32)
        return total

    def give_precond():
        get_precond.wait()
        for m in range(blocks):
            top, rest = halves(precond[m])
            split[m, :128] = top
            split[m, 128:] = rest
        get_res.wait()
        applied[...] = preconditioned(res[...], slice(0, share))

    def last_offset(x):
        return x & max(levels[level(x)])

    def send(x, c):
        rs_copies[x, c] = remote(
            rs_out.at[x - 1, :, cols(c)], rs_in.at[x - 1, :, cols(c)],
            rs_s, rs_r.at[x - 1, c], {"tm": across(last_offset(x))},
        )
        rs_copies[x, c].start()

    leaves = [x for x in reversed(plan) if level(x) == len(levels) - 1]
    for x in [x for x in leaves if x > 3] + [3, 2, 1]:
        @apart
        def _(x=x):
            rs_out[x - 1] = part(x).astype(LINK)
        for c in range(CHUNKS):
            send(x, c)
    @apart
    def _():
        for x in far:
            parts[1 + far.index(x)] = part(x)
        parts[0] = part(0) + kaula[...] * direc[...]
    give_precond()
    for x in reversed(far):
        for c in range(CHUNKS):
            rs_out[x - 1, :, cols(c)] = sum_of(x, c).astype(LINK)
            send(x, c)
    for c in range(CHUNKS):
        piece = sum_of(0, c)
        image_out[:, cols(c)] = piece
        image_applied[:, cols(c)] = preconditioned(piece, cols(c))
    image = image_out[...]
    get_sol.wait()
    app, imapp = applied[...], image_applied[...]
    d, r = direc[...], res[...]
    lane = lax.broadcasted_iota(jnp.int32, (rhs, 128), 1)
    row = lax.broadcasted_iota(jnp.int32, (rhs, 128), 0)
    products = [r * app, d * image, image * app, image * imapp]
    total = jnp.zeros((rhs, 128), jnp.float32)
    for q, product in enumerate(products):
        total = jnp.where(lane == q * rhs + row, jnp.sum(product, axis=1, keepdims=True), total)
    total = jnp.sum(total, axis=0, keepdims=True)

    tot_out[...] = total
    tot_copies = []
    for i in range(O):
        for k in range(T):
            if i or k:
                at = i * T + k - 1
                tot_copies.append(remote(tot_out, tot_in.at[at], t1_s, t1_r, to_all(k, i)))
    for copy in tot_copies:
        copy.start()
    tot_all = remote(tot_in, tot_in, t1_s, t1_r, to_tm(1))
    tot_all.wait_recv()
    total = total + jnp.sum(tot_in[...], axis=0)
    wide = jnp.broadcast_to(total[0:1, :], (rhs, 128))
    old_rz, curvature, cross, quad = [
        jnp.sum(jnp.where(lane == q * rhs + row, wide, 0.0), axis=1, keepdims=True)
        for q in range(4)
    ]
    step = old_rz / curvature
    new_rz = old_rz - 2.0 * step * cross + step * step * quad
    new_sol[...] = sol[...] + step * d
    new_res[...] = r - step * image
    new_dir[...] = app - step * imapp + (new_rz / old_rz) * d
    sent = [(ids_all, id_s, id_r.at[0]), (got, ga_s, ga_r.at[0, 0]), (rs_out, rs_s, rs_r.at[0, 0])]
    for ref, out, back in sent:
        remote(ref, ref, out, back, to_tm(1)).wait_send()
    for copy in (su_all, ob_all, tot_all):
        copy.wait_send()


def finish(new_sol, new_res, new_dir, sol_out, res_out, dir_out, sem):
    copies = [
        pltpu.make_async_copy(src, dst.at[:, 0, :], sem.at[k])
        for k, (src, dst) in enumerate(
            ((new_sol, sol_out), (new_res, res_out), (new_dir, dir_out))
        )
    ]
    for copy in copies:
        copy.start()
    for copy in copies:
        copy.wait()


def on_device(
    T, O, design, gap_flags, segment_ids, ar_order, ma_order, ar_roots, ma_roots,
    kaula, precond, solution, residual, direction,
):
    n = segment_ids.shape[0]
    columns = design.shape[2]
    share = direction.shape[2]
    rhs = direction.shape[0]
    blocks = precond.shape[1]
    f32, bf16 = jnp.float32, jnp.bfloat16
    vmem = pl.BlockSpec(memory_space=pltpu.VMEM)
    hbm = pl.BlockSpec(memory_space=pl.ANY)
    V, S, D = pltpu.VMEM, pltpu.SMEM, lambda *k: pltpu.SemaphoreType.DMA(k) if k else pltpu.SemaphoreType.DMA
    vec = pltpu.VMEM((rhs, share), f32)
    results = pl.pallas_call(
        functools.partial(kernel, T, O),
        out_shape=[vec] * 3,
        in_specs=[hbm] * 12,
        out_specs=[vmem] * 3,
        scratch_shapes=[
            V((1, n), jnp.int32), V((1, n), jnp.int32), S((3, 4), f32), S((3, 4), f32),
            S((3,), jnp.int32), S((3,), jnp.int32), V((1, share), f32),
            V((T, 3 * n, share), bf16), V((blocks, 128, 128), f32), V((rhs, share), f32),
            V((rhs, share), f32), V((rhs, share), f32), V((rhs, share), bf16), V((blocks, 256, 128), bf16),
            V((rhs, share), f32), V((T - 1, rhs, share), bf16),
            V((rhs, 3 * n), f32), V((O - 1, rhs, 3 * n), f32), V((T - 1, 1, n), jnp.int32),
            V((rhs // 4, n), f32), V((T * O, rhs // 4, n), f32), V((3, n, n), f32), V((3, n, n), bf16), V((3, n, n), bf16),
            V((rhs, 3 * n), f32),
            V((n, 3 * n), bf16), V((n, 3 * n), bf16), V((32 * T, 3 * n), bf16), V((32 * T, 3 * n), bf16),
            V((T - 1, rhs, share), LINK), V((T - 1, rhs, share), LINK),
            V((max(T // 4, 1), rhs, share), f32),
            V((rhs, share), f32), V((rhs, share), f32),
            V((1, 128), f32), V((T * O - 1, 1, 128), f32),
            D(T), D(11), D(), D(T - 1, CHUNKS), D(), D(), D(), D(T - 1), D(), D(),
            D(), D(T - 1, CHUNKS), D(), D(),
        ],
        compiler_params=pltpu.CompilerParams(
            collective_id=0, has_side_effects=True, vmem_limit_bytes=28 * 1024 * 1024
        ),
    )(*[
        pltpu.with_memory_space_constraint(v, pltpu.HBM)
        for v in (
            design.reshape(3 * n, columns), segment_ids.reshape(1, n), gap_flags.reshape(1, n),
            ar_roots, ma_roots, ar_order, ma_order, kaula, precond[0], solution, residual,
            direction,
        )
    ])
    full = jax.ShapeDtypeStruct(direction.shape, f32)
    return tuple(
        pl.pallas_call(
            finish,
            out_shape=[full] * 3,
            in_specs=[vmem] * 3,
            out_specs=[hbm] * 3,
            scratch_shapes=[D(3)],
            compiler_params=pltpu.CompilerParams(vmem_limit_bytes=1024 * 1024),
        )(*[pltpu.with_memory_space_constraint(v, pltpu.VMEM) for v in results])
    )


def solution(mesh):
    vec = P(None, "order", "tm")
    in_specs = (
        P(None, "tm", "order"), P("tm"), P("tm"), P(), P(), P(), P(), P("order", "tm"),
        P("order", "tm", None, None), vec, vec, vec,
    )
    body = functools.partial(on_device, mesh.shape["tm"], mesh.shape["order"])
    return jax.shard_map(
        body, mesh=mesh, in_specs=in_specs, out_specs=(vec, vec, vec), check_vma=False
    )
```

```python
import functools

import jax
import jax.numpy as jnp
from jax import lax
from jax.experimental import pallas as pl
from jax.experimental.pallas import tpu as pltpu
from jax.sharding import PartitionSpec as P

LINK = jnp.bfloat16
LAGS = 4
CHUNKS = 2
HI = lax.Precision.HIGHEST
NN = (((1,), (0,)), ((), ()))
NT = (((1,), (1,)), ((), ()))


def dot(a, b, dims, precision=None):
    return lax.dot_general(a, b, dims, precision=precision, preferred_element_type=jnp.float32)


def tall(block, rows):
    return jnp.concatenate(
        [block, jnp.zeros((rows - block.shape[0], block.shape[1]), jnp.float32)], axis=0
    )


def halves(x):
    top = x.astype(jnp.bfloat16)
    return top, (x - top.astype(jnp.float32)).astype(jnp.bfloat16)


def dot3(x, high, low, dims):
    rows = x.shape[0]
    top, rest = halves(x)
    both = dot(jnp.concatenate([top, rest], axis=0), high, dims)
    return both[:rows] + both[rows:] + dot(top, low, dims)


def bands(matrix):
    row = lax.broadcasted_iota(jnp.int32, matrix.shape, 0)
    col = lax.broadcasted_iota(jnp.int32, matrix.shape, 1)
    return [
        jnp.sum(jnp.where(row == col - 4 * shift, matrix, 0.0), axis=0, keepdims=True)
        for shift in range(1 - LAGS, LAGS)
    ]


def banded(vector, coeffs):
    width = vector.shape[1]
    total = None
    for shift, coeff in zip(range(1 - LAGS, LAGS), coeffs):
        moved = vector if shift == 0 else pltpu.roll(vector, 4 * shift % width, 1)
        total = moved * coeff if total is None else total + moved * coeff
    return total


def columns(ref, order_ref, comp):
    out = []
    for k in range(LAGS):
        column = jnp.zeros(comp.shape, jnp.float32)
        for c in range(3):
            value = jnp.where(k < order_ref[c], ref[c, k], 0.0)
            column = jnp.where(comp == c, value, column)
        out.append(column)
    return out


def stack(pieces):
    row = lax.broadcasted_iota(jnp.int32, pieces[0].shape, 0)
    real = row % 4 < 3
    both = [jnp.where(row < 4, pieces[i], pieces[i + 1]) for i in range(0, LAGS, 2)]
    return jnp.concatenate([jnp.where(real, block, 0.0) for block in both], axis=0)


def filters(ar_ref, ma_ref, aro_ref, mao_ref, ids, pt_ref):
    n = ids.shape[1]
    lane = lax.broadcasted_iota(jnp.int32, (8, n), 1)
    comp = lax.broadcasted_iota(jnp.int32, (8, n), 0) % 4

    def lagged(v, k):
        return v if k == 0 else jnp.where(lane >= k, pltpu.roll(v, k, 1), 0.0)

    def at(k):
        return jnp.where(lane == k, 1.0, 0.0)

    ar, ma = columns(ar_ref, aro_ref, comp), columns(ma_ref, mao_ref, comp)
    a, b = [1.0] + [0.0] * LAGS, [1.0] + [0.0] * LAGS
    for k in range(LAGS):
        a = [a[0]] + [a[j] - ar[k] * a[j - 1] for j in range(1, LAGS + 1)]
        b = [b[0]] + [b[j] - ma[k] * b[j - 1] for j in range(1, LAGS + 1)]
    h, power, m = at(0), ar, 1
    while m < n:
        s0, q0 = power[0] + power[1], power[0] * power[1]
        s1, q1 = power[2] + power[3], power[2] * power[3]
        e = [s0 + s1, q0 + q1 + s0 * s1, q0 * s1 + s0 * q1, q0 * q1]
        terms = [e[j] * lagged(h, (j + 1) * m) for j in range(LAGS) if (j + 1) * m < n]
        while len(terms) > 1:
            terms = [sum(terms[i + 1 : i + 2], terms[i]) for i in range(0, len(terms), 2)]
        h = h + terms[0]
        power, m = [p * p for p in power], 2 * m
    hs = [lagged(h, k) for k in range(LAGS + 1)]
    g = hs[0] + ((b[1] * hs[1] + b[2] * hs[2]) + (b[3] * hs[3] + b[4] * hs[4]))
    gs = [lagged(g, k) for k in range(LAGS)]
    ins, ends = [], []
    for i in range(1, LAGS + 1):
        acc, end = jnp.zeros_like(g), jnp.zeros_like(g)
        for k in range(LAGS + 1 - i):
            acc = acc + b[i + k] * at(k) - a[i + k] * gs[k]
            end = end - a[i + k] * at(n - 1 - k)
        ins.append(acc)
        ends.append(end)
    yield None
    row = lax.broadcasted_iota(jnp.int32, (n, n), 0)
    col = lax.broadcasted_iota(jnp.int32, (n, n), 1)
    grid = jnp.broadcast_to(ids, (n, n))
    joined = (grid == grid.T) & (col >= row)
    for c in range(3):
        t = pltpu.roll(jnp.broadcast_to(g[c : c + 1], (n, n)), 0, 1, stride=1, stride_axis=0)
        pt_ref[c] = jnp.where(joined, t, 0.0)
    yield None
    ca, ends = stack(hs[:LAGS]), stack(ends)
    flip = jnp.where(row + col == n - 1, 1.0, 0.0).astype(jnp.float32)
    ab = dot(stack(ins), flip, NN, HI)
    fwd = bands(dot(ca, tall(ends, n), NT, HI))
    bwd = bands(dot(ends, tall(ca, n), NT, HI))
    yield ca, ab, fwd, bwd


def spread(block, mask):
    row = lax.broadcasted_iota(jnp.int32, block.shape, 0)
    return jnp.concatenate(
        [jnp.where(row % 4 == c, block * mask, 0.0) for c in range(3)], axis=1
    )


def state_weights(T, me, shape, links, throughs, fwd, bwd, energies):
    row = lax.broadcasted_iota(jnp.int32, shape, 0)
    lane = lax.broadcasted_iota(jnp.int32, shape, 1)
    eye = jnp.where(row == lane, 1.0, 0.0)
    zero = jnp.zeros(shape, jnp.float32)
    state, ins, mine = {}, [], {}

    def keep(blocks, e, into):
        for key, v in blocks.items():
            mine[into, key] = jnp.where(me == e, v, mine.get((into, key), zero))

    for e in range(T):
        entering = {q: v * links[e] for q, v in state.items()}
        ins.append(entering)
        keep(entering, e, "in")
        state = {q: throughs[e] * banded(v, fwd) for q, v in entering.items()}
        state[e] = eye
    back = {}
    for e in range(T - 1, 0, -1):
        new = {key: throughs[e] * banded(v, bwd) for key, v in back.items()}
        for q, v in ins[e].items():
            moved = banded(v, energies[e])
            new["tail", q] = new["tail", q] + moved if ("tail", q) in new else moved
        new["head", e] = eye
        back = {key: v * links[e] for key, v in new.items()}
        keep(back, e - 1, "back")
    out = []
    for e in range(T):
        entering = pltpu.roll(mine["in", e], 16, 1) if ("in", e) in mine else zero
        out.append(mine.get(("back", ("tail", e)), zero) + entering)
        out.append(mine.get(("back", ("head", e)), zero))
    return jnp.concatenate(out, axis=0)


def kernel(
    T, O,
    design, ids_hbm, gaps_hbm, ar_hbm, ma_hbm, aro_hbm, mao_hbm, kaula_hbm, precond_in,
    sol_in, res_in, direc_in,
    new_sol, new_res, new_dir,
    ids_in, gaps_in, ar_ref, ma_ref, aro_ref, mao_ref, kaula, dv, precond, sol, res, direc, packed, split,
    image_out, got, obs_out, obs_in, ids_all, summ_out, summ_in, pt, back_high, back_low, local_back,
    map_high, map_low, cross_high, cross_low, rs_out, rs_in, parts, first_sum, applied, image_applied,
    tot_out, tot_in,
    dsem, in_sem, ga_s, ga_r, ob_s, ob_r, id_s, id_r, su_s, su_r,
    rs_s, rs_r, t1_s, t1_r,
):
    me, order = lax.axis_index("tm"), lax.axis_index("order")
    rhs, share = packed.shape
    n = ids_in.shape[1]
    blocks = precond.shape[0]
    wide = share // CHUNKS
    bits = T.bit_length() - 1

    levels = [(1 << b,) for b in reversed(range(2, bits))] + [(3, 2, 1)]

    def level(x):
        return max([i for i, offsets in enumerate(levels) if any(x & o for o in offsets)], default=-1)

    def into(x):
        return [o for offsets in levels[level(x) + 1 :] for o in offsets]

    def place(x):
        out = me
        for b in range(bits):
            if x >> b & 1:
                out = out + (1 << b) * (1 - 2 * lax.rem(lax.div(me, 1 << b), 2))
        return out

    places = [place(x) for x in range(T)]

    def across(x):
        return places[x]

    def cols(c):
        return slice(c * wide, (c + 1) * wide)

    mesh_ids = pl.DeviceIdType.MESH
    apart = pl.when(me >= 0)

    def to_tm(k):
        return {"tm": lax.rem(me + k, T)}

    def to_order(k):
        return {"order": lax.rem(order + k, O)}

    def to_all(k, i):
        return {"tm": lax.rem(me + k, T), "order": lax.rem(order + i, O)}

    def load(x):
        return pltpu.make_async_copy(
            design.at[:, pl.ds(pl.multiple_of(across(x) * share, 128), share)],
            dv.at[x],
            dsem.at[x],
        )

    def remote(src, dst, ssem, rsem, to):
        return pltpu.make_async_remote_copy(
            src_ref=src, dst_ref=dst, send_sem=ssem, recv_sem=rsem,
            device_id=to, device_id_type=mesh_ids,
        )

    get_direc = pltpu.make_async_copy(direc_in.at[:, 0, :], direc, in_sem.at[0])
    get_res = pltpu.make_async_copy(res_in.at[:, 0, :], res, in_sem.at[1])
    get_sol = pltpu.make_async_copy(sol_in.at[:, 0, :], sol, in_sem.at[3])
    get_precond = pltpu.make_async_copy(precond_in, precond, in_sem.at[2])
    get_direc.start()
    get_small = [
        pltpu.make_async_copy(src, dst, in_sem.at[4 + k])
        for k, (src, dst) in enumerate((
            (ids_hbm, ids_in), (ar_hbm, ar_ref), (ma_hbm, ma_ref), (aro_hbm, aro_ref),
            (mao_hbm, mao_ref), (gaps_hbm, gaps_in), (kaula_hbm, kaula),
        ))
    ]
    barrier = pltpu.get_barrier_semaphore()
    for x in into(0):
        pl.semaphore_signal(
            barrier, inc=1, device_id={"tm": across(x)}, device_id_type=mesh_ids
        )
    for k in range(1, O):
        pl.semaphore_signal(barrier, inc=1, device_id=to_order(k), device_id_type=mesh_ids)
    plan = sorted(range(1, T), key=lambda x: (level(x), x))
    for copy in get_small:
        copy.start()
    for x in range(T):
        load(x).start()
    get_precond.start()
    get_res.start()
    get_sol.start()
    get_direc.wait()
    packed[...] = direc[...].astype(jnp.bfloat16)
    get_small[0].wait()
    pl.semaphore_wait(barrier, len(into(0)) + O - 1)

    id_copies, ga_copies = {}, {}

    def pass_on(x, c, offsets):
        for o in offsets:
            to = x | o
            if c == 0:
                id_copies[to] = remote(
                    ids_all.at[x - 1] if x else ids_in, ids_all.at[to - 1],
                    id_s, id_r.at[to - 1], {"tm": across(o)},
                )
                id_copies[to].start()
            ga_copies[to, c] = remote(
                (got.at[x - 1] if x else packed).at[:, cols(c)], got.at[to - 1, :, cols(c)],
                ga_s, ga_r.at[to - 1, c], {"tm": across(o)},
            )
            ga_copies[to, c].start()

    def arrive(x, c):
        if c == 0:
            id_copies[x].wait_recv()
        ga_copies[x, c].wait_recv()
        pass_on(x, c, into(x))

    for o in into(0):
        for c in range(CHUNKS):
            pass_on(0, c, [o])

    for copy in get_small[1:5]:
        copy.wait()
    ids = ids_in[0:1, :].astype(jnp.float32)
    building = filters(ar_ref, ma_ref, aro_ref, mao_ref, ids, pt)
    next(building)

    def preconditioned(v, at):
        out = []
        for m in range(at.start // 128, at.stop // 128):
            x = v[:, m * 128 - at.start : (m + 1) * 128 - at.start]
            top, rest = halves(x)
            both = dot(jnp.concatenate([top, rest], axis=0), split[m], NT)
            out.append(both[:rhs, :128] + both[rhs:, :128] + both[:rhs, 128:])
        return jnp.concatenate(out, axis=1)

    def observe(x, c, at):
        if c == 0:
            load(x).wait()

        @apart
        def _():
            for k in range(0, 3 * n, n):
                obs_out[:, k : k + n] += dot(got[x - 1, :, at], dv[x, k : k + n, at], NT)

    next(building)
    ca, ab, fwd, bwd = next(building)
    first, last = ids[:, 0:1], ids[:, n - 1 : n]
    head_map = spread(ca, jnp.where(ids == first, 1.0, 0.0))
    tail_map = spread(ab, jnp.where(ids == last, 1.0, 0.0))
    head_map = jnp.concatenate(
        [dot(head_map[:, c * n : (c + 1) * n], pt[c], NT, HI) for c in range(3)], axis=1
    )
    both_maps = jnp.concatenate([tail_map, head_map], axis=0)
    top, rest = halves(jnp.concatenate([both_maps] * 4, axis=0))
    map_high[...] = top
    map_low[...] = rest
    for c in range(3):
        top, rest = halves(dot(pt[c], pt[c], NT, HI))
        back_high[c] = top
        back_low[c] = rest
    load(0).wait()
    obs_out[...] = dot(packed[...], dv[0], NT)
    far = [x for x in plan if level(x) < len(levels) - 1]
    near = [x for x in plan if level(x) == len(levels) - 1]
    for x in far:
        for c in range(CHUNKS):
            arrive(x, c)
    for x in near[:3] + far + near[3:]:
        for c in range(CHUNKS):
            if x in near:
                arrive(x, c)
            if x == T - 1:
                observe(x, c, cols(c))
        if x < T - 1:
            observe(x, 0, slice(0, share))
    quarter = rhs // 4
    for copy in get_small[5:]:
        copy.wait()
    gaps3 = jnp.concatenate([gaps_in[0:1, :].astype(jnp.float32)] * 3, axis=1)
    obs = obs_out[...]
    summary = dot3(obs * gaps3, map_high[...], map_low[...], NT)
    row = lax.broadcasted_iota(jnp.int32, summary.shape, 0)
    lane = lax.broadcasted_iota(jnp.int32, summary.shape, 1)
    turn = lax.rem(me, 4)
    summary = jnp.where(lane // 32 == (row // quarter + turn) % 4, summary, 0.0)
    summary = summary[: 2 * quarter] + summary[2 * quarter :]
    summary = summary[:quarter] + summary[quarter:]
    summ_out[...] = summary
    summ_in[order * T + me] = summary
    su_copies = []
    for k in list(range(1, T)) + [0]:
        for i in range(O):
            if i or k:
                su_copies.append(
                    remote(summ_out, summ_in.at[order * T + me], su_s, su_r, to_all(k, i))
                )
    ob_copies = [
        remote(obs_out, obs_in.at[k - 1], ob_s, ob_r, to_order(k))
        for k in range(1, O)
    ]
    for copy in su_copies + ob_copies:
        copy.start()

    direct = T <= 8

    def ranges():
        ids_e = []
        for e in range(T):
            v = ids
            for x in range(1, T):
                v = jnp.where(across(x) == e, ids_all[x - 1].astype(jnp.float32), v)
            ids_e.append(v)
        firsts = [v[:, 0:1] for v in ids_e]
        lasts = [v[:, n - 1 : n] for v in ids_e]
        runs = jnp.concatenate(
            [ca * jnp.where(v == f, 1.0, 0.0) for v, f in zip(ids_e, firsts)], axis=0
        )
        energy = dot(runs, tall(ca, n), NT, HI)
        energies = [bands(energy[16 * e : 16 * e + 16]) for e in range(T)]
        links = [None] + [
            jnp.where(lasts[e - 1] == firsts[e], 1.0, 0.0) for e in range(1, T)
        ]
        throughs = [jnp.where(firsts[e] == lasts[e], 1.0, 0.0) for e in range(T)]
        return links, throughs, energies

    if direct:
        @apart
        def _():
            links, throughs, energies = ranges()
            weights = state_weights(T, me, (16, n), links, throughs, fwd, bwd, energies)
            top, rest = halves(dot(weights, tall(both_maps, n), NN, HI))
            cross_high[...] = top
            cross_low[...] = rest
    else:
        links, throughs, energies = ranges()
    ob_all = remote(obs_in, obs_in, ob_s, ob_r, to_tm(1))
    ob_all.wait_recv()
    for k in range(1, O):
        obs = obs + obs_in[k - 1]
    masked = obs * gaps3
    for c in range(3):
        at = slice(c * n, (c + 1) * n)
        local_back[:, at] = dot3(masked[:, at], back_high[c], back_low[c], NN)
    others = summ_in.at[pl.ds(1, T * O - 1)]
    su_all = remote(others, others, su_s, su_r, to_tm(1))
    su_all.wait_recv()
    slot = lax.broadcasted_iota(jnp.int32, (quarter, n), 1) // 32
    sums = [sum([summ_in[i * T + e] for i in range(1, O)], summ_in[e]) for e in range(T)]
    groups = []
    for e in range(0, T, 4):
        rows = []
        for q in range(4):
            picked = sums[e + (3 - q) % 4]
            for at in range(3):
                picked = jnp.where(slot == at, sums[e + (at - q) % 4], picked)
            rows.append(pltpu.roll(picked, (n - 32 * q) % n, 1) if q else picked)
        groups.append(jnp.concatenate(rows, axis=0))
    if direct:
        adjoint = local_back[...] + dot3(
            jnp.concatenate(groups, axis=1), cross_high[...], cross_low[...], NN
        )
    else:
        lane = lax.broadcasted_iota(jnp.int32, (rhs, n), 1)
        tails = [
            jnp.where(lane < 16, pltpu.roll(groups[e // 4], (n - 32 * (e % 4)) % n, 1), 0.0)
            for e in range(T)
        ]
        heads = [
            jnp.where(lane < 16, pltpu.roll(groups[e // 4], (n - 32 * (e % 4) - 16) % n, 1), 0.0)
            for e in range(T)
        ]
        state = jnp.zeros((rhs, n), jnp.float32)
        mine_in, mine_back, back, ins = state, state, state, []
        for e in range(T):
            entering = state if e == 0 else state * links[e]
            ins.append(entering)
            mine_in = jnp.where(me == e, entering, mine_in)
            state = tails[e] + throughs[e] * banded(entering, fwd)
        for e in range(T - 1, 0, -1):
            back = heads[e] + banded(ins[e], energies[e]) + throughs[e] * banded(back, bwd)
            back = back * links[e]
            mine_back = jnp.where(me == e - 1, back, mine_back)
        states = mine_back + pltpu.roll(mine_in, 16, 1)
        adjoint = local_back[...] + dot(states, tall(both_maps, n), NN, HI)
    weighted = (adjoint * gaps3).astype(jnp.bfloat16)

    rs_copies = {}

    def part(x):
        return dot(weighted, dv[x], NN)

    def sum_of(x, c):
        total = parts[([0] + far).index(x), :, cols(c)]
        for o in into(x):
            rs_copies[x | o, c].wait_recv()
            total = total + rs_in[(x | o) - 1, :, cols(c)].astype(jnp.float32)
        return total

    def narrow(v):
        return sum([v[:, k : k + 128] for k in range(128, v.shape[1], 128)], v[:, :128])

    def give_precond():
        get_precond.wait()
        for m in range(blocks):
            top, rest = halves(precond[m])
            split[m, :128] = top
            split[m, 128:] = rest
        get_res.wait()
        known = preconditioned(res[...], slice(0, share))
        applied[...] = known
        first_sum[...] = narrow(res[...] * known)

    def last_offset(x):
        return x & max(levels[level(x)])

    def send(x, c):
        rs_copies[x, c] = remote(
            rs_out.at[x - 1, :, cols(c)], rs_in.at[x - 1, :, cols(c)],
            rs_s, rs_r.at[x - 1, c], {"tm": across(last_offset(x))},
        )
        rs_copies[x, c].start()

    leaves = [x for x in reversed(plan) if level(x) == len(levels) - 1]
    for x in [x for x in leaves if x > 3]:
        @apart
        def _(x=x):
            rs_out[x - 1] = part(x).astype(LINK)
        for c in range(CHUNKS):
            send(x, c)
    @apart
    def _():
        for x in far:
            parts[1 + far.index(x)] = part(x)
        parts[0] = part(0) + kaula[...] * direc[...]
    give_precond()
    for x in (3, 2, 1):
        @apart
        def _(x=x):
            rs_out[x - 1] = part(x).astype(LINK)
        for c in range(CHUNKS):
            send(x, c)
    for x in reversed(far):
        for c in range(CHUNKS):
            rs_out[x - 1, :, cols(c)] = sum_of(x, c).astype(LINK)
            send(x, c)
    inner_sums = [first_sum[...]] + [jnp.zeros((rhs, 128), jnp.float32)] * 3
    get_sol.wait()
    for c in range(CHUNKS):
        piece = sum_of(0, c)
        image_out[:, cols(c)] = piece
        moved = preconditioned(piece, cols(c))
        image_applied[:, cols(c)] = moved
        known = applied[:, cols(c)]
        for q, product in enumerate((direc[:, cols(c)] * piece, piece * known, piece * moved)):
            inner_sums[q + 1] += narrow(product)
    lane = lax.broadcasted_iota(jnp.int32, (rhs, 128), 1)
    row = lax.broadcasted_iota(jnp.int32, (rhs, 128), 0)
    total = jnp.zeros((rhs, 128), jnp.float32)
    for q, product in enumerate(inner_sums):
        total = jnp.where(lane == q * rhs + row, jnp.sum(product, axis=1, keepdims=True), total)
    total = jnp.sum(total, axis=0, keepdims=True)
    tot_out[...] = total
    tot_copies = []
    for i in range(O):
        for k in range(T):
            if i or k:
                at = i * T + k - 1
                tot_copies.append(remote(tot_out, tot_in.at[at], t1_s, t1_r, to_all(k, i)))
    for copy in tot_copies:
        copy.start()
    tot_all = remote(tot_in, tot_in, t1_s, t1_r, to_tm(1))
    tot_all.wait_recv()
    total = total + jnp.sum(tot_in[...], axis=0)
    wide = jnp.broadcast_to(total[0:1, :], (rhs, 128))
    old_rz, curvature, cross, quad = [
        jnp.sum(jnp.where(lane == q * rhs + row, wide, 0.0), axis=1, keepdims=True)
        for q in range(4)
    ]
    step = old_rz / curvature
    new_rz = old_rz - 2.0 * step * cross + step * step * quad
    app, imapp, image = applied[...], image_applied[...], image_out[...]
    d, r = direc[...], res[...]
    new_sol[...] = sol[...] + step * d
    new_res[...] = r - step * image
    new_dir[...] = app - step * imapp + (new_rz / old_rz) * d
    sent = [(ids_all, id_s, id_r.at[0]), (got, ga_s, ga_r.at[0, 0]), (rs_out, rs_s, rs_r.at[0, 0])]
    for ref, out, back in sent:
        remote(ref, ref, out, back, to_tm(1)).wait_send()
    for copy in (su_all, ob_all, tot_all):
        copy.wait_send()


def finish(new_sol, new_res, new_dir, sol_out, res_out, dir_out, sem):
    copies = [
        pltpu.make_async_copy(src, dst.at[:, 0, :], sem.at[k])
        for k, (src, dst) in enumerate(
            ((new_sol, sol_out), (new_res, res_out), (new_dir, dir_out))
        )
    ]
    for copy in copies:
        copy.start()
    for copy in copies:
        copy.wait()


def on_device(
    T, O, design, gap_flags, segment_ids, ar_order, ma_order, ar_roots, ma_roots,
    kaula, precond, solution, residual, direction,
):
    n = segment_ids.shape[0]
    columns = design.shape[2]
    share = direction.shape[2]
    rhs = direction.shape[0]
    blocks = precond.shape[1]
    f32, bf16 = jnp.float32, jnp.bfloat16
    vmem = pl.BlockSpec(memory_space=pltpu.VMEM)
    hbm = pl.BlockSpec(memory_space=pl.ANY)
    V, S, D = pltpu.VMEM, pltpu.SMEM, lambda *k: pltpu.SemaphoreType.DMA(k) if k else pltpu.SemaphoreType.DMA
    vec = pltpu.VMEM((rhs, share), f32)
    results = pl.pallas_call(
        functools.partial(kernel, T, O),
        out_shape=[vec] * 3,
        in_specs=[hbm] * 12,
        out_specs=[vmem] * 3,
        scratch_shapes=[
            V((1, n), jnp.int32), V((1, n), jnp.int32), S((3, 4), f32), S((3, 4), f32),
            S((3,), jnp.int32), S((3,), jnp.int32), V((1, share), f32),
            V((T, 3 * n, share), bf16), V((blocks, 128, 128), f32), V((rhs, share), f32),
            V((rhs, share), f32), V((rhs, share), f32), V((rhs, share), bf16), V((blocks, 256, 128), bf16),
            V((rhs, share), f32), V((T - 1, rhs, share), bf16),
            V((rhs, 3 * n), f32), V((O - 1, rhs, 3 * n), f32), V((T - 1, 1, n), jnp.int32),
            V((rhs // 4, n), f32), V((T * O, rhs // 4, n), f32), V((3, n, n), f32), V((3, n, n), bf16), V((3, n, n), bf16),
            V((rhs, 3 * n), f32),
            V((n, 3 * n), bf16), V((n, 3 * n), bf16), V((32 * T, 3 * n), bf16), V((32 * T, 3 * n), bf16),
            V((T - 1, rhs, share), LINK), V((T - 1, rhs, share), LINK),
            V((max(T // 4, 1), rhs, share), f32), V((rhs, 128), f32),
            V((rhs, share), f32), V((rhs, share), f32),
            V((1, 128), f32), V((T * O - 1, 1, 128), f32),
            D(T), D(11), D(), D(T - 1, CHUNKS), D(), D(), D(), D(T - 1), D(), D(),
            D(), D(T - 1, CHUNKS), D(), D(),
        ],
        compiler_params=pltpu.CompilerParams(
            collective_id=0, has_side_effects=True, vmem_limit_bytes=28 * 1024 * 1024
        ),
    )(*[
        pltpu.with_memory_space_constraint(v, pltpu.HBM)
        for v in (
            design.reshape(3 * n, columns), segment_ids.reshape(1, n), gap_flags.reshape(1, n),
            ar_roots, ma_roots, ar_order, ma_order, kaula, precond[0], solution, residual,
            direction,
        )
    ])
    full = jax.ShapeDtypeStruct(direction.shape, f32)
    return tuple(
        pl.pallas_call(
            finish,
            out_shape=[full] * 3,
            in_specs=[vmem] * 3,
            out_specs=[hbm] * 3,
            scratch_shapes=[D(3)],
            compiler_params=pltpu.CompilerParams(vmem_limit_bytes=1024 * 1024),
        )(*[pltpu.with_memory_space_constraint(v, pltpu.VMEM) for v in results])
    )


def solution(mesh):
    vec = P(None, "order", "tm")
    in_specs = (
        P(None, "tm", "order"), P("tm"), P("tm"), P(), P(), P(), P(), P("order", "tm"),
        P("order", "tm", None, None), vec, vec, vec,
    )
    body = functools.partial(on_device, mesh.shape["tm"], mesh.shape["order"])
    return jax.shard_map(
        body, mesh=mesh, in_specs=in_specs, out_specs=(vec, vec, vec), check_vma=False
    )
```

```python
import functools

import jax
import jax.numpy as jnp
from jax import lax
from jax.experimental import pallas as pl
from jax.experimental.pallas import tpu as pltpu
from jax.sharding import PartitionSpec as P

LINK = jnp.bfloat16
LAGS = 4
CHUNKS = 2
HI = lax.Precision.HIGHEST
NN = (((1,), (0,)), ((), ()))
NT = (((1,), (1,)), ((), ()))


def dot(a, b, dims, precision=None):
    return lax.dot_general(a, b, dims, precision=precision, preferred_element_type=jnp.float32)


def tall(block, rows):
    return jnp.concatenate(
        [block, jnp.zeros((rows - block.shape[0], block.shape[1]), jnp.float32)], axis=0
    )


def halves(x):
    top = x.astype(jnp.bfloat16)
    return top, (x - top.astype(jnp.float32)).astype(jnp.bfloat16)


def dot3(x, high, low, dims):
    rows = x.shape[0]
    top, rest = halves(x)
    both = dot(jnp.concatenate([top, rest], axis=0), high, dims)
    return both[:rows] + both[rows:] + dot(top, low, dims)


def bands(matrix):
    row = lax.broadcasted_iota(jnp.int32, matrix.shape, 0)
    col = lax.broadcasted_iota(jnp.int32, matrix.shape, 1)
    return [
        jnp.sum(jnp.where(row == col - 4 * shift, matrix, 0.0), axis=0, keepdims=True)
        for shift in range(1 - LAGS, LAGS)
    ]


def banded(vector, coeffs):
    width = vector.shape[1]
    total = None
    for shift, coeff in zip(range(1 - LAGS, LAGS), coeffs):
        moved = vector if shift == 0 else pltpu.roll(vector, 4 * shift % width, 1)
        total = moved * coeff if total is None else total + moved * coeff
    return total


def columns(ref, order_ref, comp):
    out = []
    for k in range(LAGS):
        column = jnp.zeros(comp.shape, jnp.float32)
        for c in range(3):
            value = jnp.where(k < order_ref[c], ref[c, k], 0.0)
            column = jnp.where(comp == c, value, column)
        out.append(column)
    return out


def stack(pieces):
    row = lax.broadcasted_iota(jnp.int32, pieces[0].shape, 0)
    real = row % 4 < 3
    both = [jnp.where(row < 4, pieces[i], pieces[i + 1]) for i in range(0, LAGS, 2)]
    return jnp.concatenate([jnp.where(real, block, 0.0) for block in both], axis=0)


def filters(ar_ref, ma_ref, aro_ref, mao_ref, ids, pt_ref):
    n = ids.shape[1]
    lane = lax.broadcasted_iota(jnp.int32, (8, n), 1)
    comp = lax.broadcasted_iota(jnp.int32, (8, n), 0) % 4

    def lagged(v, k):
        return v if k == 0 else jnp.where(lane >= k, pltpu.roll(v, k, 1), 0.0)

    def at(k):
        return jnp.where(lane == k, 1.0, 0.0)

    ar, ma = columns(ar_ref, aro_ref, comp), columns(ma_ref, mao_ref, comp)
    a, b = [1.0] + [0.0] * LAGS, [1.0] + [0.0] * LAGS
    for k in range(LAGS):
        a = [a[0]] + [a[j] - ar[k] * a[j - 1] for j in range(1, LAGS + 1)]
        b = [b[0]] + [b[j] - ma[k] * b[j - 1] for j in range(1, LAGS + 1)]
    h, power, m = at(0), ar, 1
    while m < n:
        s0, q0 = power[0] + power[1], power[0] * power[1]
        s1, q1 = power[2] + power[3], power[2] * power[3]
        e = [s0 + s1, q0 + q1 + s0 * s1, q0 * s1 + s0 * q1, q0 * q1]
        terms = [e[j] * lagged(h, (j + 1) * m) for j in range(LAGS) if (j + 1) * m < n]
        while len(terms) > 1:
            terms = [sum(terms[i + 1 : i + 2], terms[i]) for i in range(0, len(terms), 2)]
        h = h + terms[0]
        power, m = [p * p for p in power], 2 * m
    hs = [lagged(h, k) for k in range(LAGS + 1)]
    g = hs[0] + ((b[1] * hs[1] + b[2] * hs[2]) + (b[3] * hs[3] + b[4] * hs[4]))
    gs = [lagged(g, k) for k in range(LAGS)]
    ins, ends = [], []
    for i in range(1, LAGS + 1):
        acc, end = jnp.zeros_like(g), jnp.zeros_like(g)
        for k in range(LAGS + 1 - i):
            acc = acc + b[i + k] * at(k) - a[i + k] * gs[k]
            end = end - a[i + k] * at(n - 1 - k)
        ins.append(acc)
        ends.append(end)
    yield None
    row = lax.broadcasted_iota(jnp.int32, (n, n), 0)
    col = lax.broadcasted_iota(jnp.int32, (n, n), 1)
    grid = jnp.broadcast_to(ids, (n, n))
    joined = (grid == grid.T) & (col >= row)
    for c in range(3):
        t = pltpu.roll(jnp.broadcast_to(g[c : c + 1], (n, n)), 0, 1, stride=1, stride_axis=0)
        pt_ref[c] = jnp.where(joined, t, 0.0)
    yield None
    ca, ends = stack(hs[:LAGS]), stack(ends)
    flip = jnp.where(row + col == n - 1, 1.0, 0.0).astype(jnp.float32)
    ab = dot(stack(ins), flip, NN, HI)
    fwd = bands(dot(ca, tall(ends, n), NT, HI))
    bwd = bands(dot(ends, tall(ca, n), NT, HI))
    yield ca, ab, fwd, bwd


def spread(block, mask):
    row = lax.broadcasted_iota(jnp.int32, block.shape, 0)
    return jnp.concatenate(
        [jnp.where(row % 4 == c, block * mask, 0.0) for c in range(3)], axis=1
    )


def state_weights(T, me, shape, links, throughs, fwd, bwd, energies):
    row = lax.broadcasted_iota(jnp.int32, shape, 0)
    lane = lax.broadcasted_iota(jnp.int32, shape, 1)
    eye = jnp.where(row == lane, 1.0, 0.0)
    zero = jnp.zeros(shape, jnp.float32)
    state, ins, mine = {}, [], {}

    def keep(blocks, e, into):
        for key, v in blocks.items():
            mine[into, key] = jnp.where(me == e, v, mine.get((into, key), zero))

    for e in range(T):
        entering = {q: v * links[e] for q, v in state.items()}
        ins.append(entering)
        keep(entering, e, "in")
        state = {q: throughs[e] * banded(v, fwd) for q, v in entering.items()}
        state[e] = eye
    back = {}
    for e in range(T - 1, 0, -1):
        new = {key: throughs[e] * banded(v, bwd) for key, v in back.items()}
        for q, v in ins[e].items():
            moved = banded(v, energies[e])
            new["tail", q] = new["tail", q] + moved if ("tail", q) in new else moved
        new["head", e] = eye
        back = {key: v * links[e] for key, v in new.items()}
        keep(back, e - 1, "back")
    out = []
    for e in range(T):
        entering = pltpu.roll(mine["in", e], 16, 1) if ("in", e) in mine else zero
        out.append(mine.get(("back", ("tail", e)), zero) + entering)
        out.append(mine.get(("back", ("head", e)), zero))
    return jnp.concatenate(out, axis=0)


def kernel(
    T, O,
    design, ids_hbm, gaps_hbm, ar_hbm, ma_hbm, aro_hbm, mao_hbm, kaula_hbm, precond_in,
    sol_in, res_in, direc_in,
    new_sol, new_res, new_dir,
    ids_in, gaps_in, ar_ref, ma_ref, aro_ref, mao_ref, kaula, dv, precond, sol, res, direc, packed, split,
    image_out, got, obs_out, obs_in, ids_all, summ_out, summ_in, pt, back_high, back_low, local_back,
    map_high, map_low, cross_high, cross_low, rs_out, rs_in, parts, first_sum, applied, image_applied,
    tot_out, tot_in,
    dsem, in_sem, ga_s, ga_r, ob_s, ob_r, id_s, id_r, su_s, su_r,
    rs_s, rs_r, t1_s, t1_r,
):
    me, order = lax.axis_index("tm"), lax.axis_index("order")
    rhs, share = packed.shape
    n = ids_in.shape[1]
    blocks = precond.shape[0]
    wide = share // CHUNKS
    bits = T.bit_length() - 1

    levels = [(1 << b,) for b in reversed(range(2, bits))] + [(3, 2, 1)]

    def level(x):
        return max([i for i, offsets in enumerate(levels) if any(x & o for o in offsets)], default=-1)

    def into(x):
        return [o for offsets in levels[level(x) + 1 :] for o in offsets]

    def place(x):
        out = me
        for b in range(bits):
            if x >> b & 1:
                out = out + (1 << b) * (1 - 2 * lax.rem(lax.div(me, 1 << b), 2))
        return out

    places = [place(x) for x in range(T)]

    def across(x):
        return places[x]

    def cols(c):
        return slice(c * wide, (c + 1) * wide)

    mesh_ids = pl.DeviceIdType.MESH
    apart = pl.when(me >= 0)

    def to_tm(k):
        return {"tm": lax.rem(me + k, T)}

    def to_order(k):
        return {"order": lax.rem(order + k, O)}

    def to_all(k, i):
        return {"tm": lax.rem(me + k, T), "order": lax.rem(order + i, O)}

    def load(x):
        return pltpu.make_async_copy(
            design.at[:, pl.ds(pl.multiple_of(across(x) * share, 128), share)],
            dv.at[x],
            dsem.at[x],
        )

    def remote(src, dst, ssem, rsem, to):
        return pltpu.make_async_remote_copy(
            src_ref=src, dst_ref=dst, send_sem=ssem, recv_sem=rsem,
            device_id=to, device_id_type=mesh_ids,
        )

    get_direc = pltpu.make_async_copy(direc_in.at[:, 0, :], direc, in_sem.at[0])
    get_res = pltpu.make_async_copy(res_in.at[:, 0, :], res, in_sem.at[1])
    get_sol = pltpu.make_async_copy(sol_in.at[:, 0, :], sol, in_sem.at[3])
    get_precond = pltpu.make_async_copy(precond_in, precond, in_sem.at[2])
    get_direc.start()
    get_small = [
        pltpu.make_async_copy(src, dst, in_sem.at[4 + k])
        for k, (src, dst) in enumerate((
            (ids_hbm, ids_in), (ar_hbm, ar_ref), (ma_hbm, ma_ref), (aro_hbm, aro_ref),
            (mao_hbm, mao_ref), (gaps_hbm, gaps_in), (kaula_hbm, kaula),
        ))
    ]
    barrier = pltpu.get_barrier_semaphore()
    for x in into(0):
        pl.semaphore_signal(
            barrier, inc=1, device_id={"tm": across(x)}, device_id_type=mesh_ids
        )
    for k in range(1, O):
        pl.semaphore_signal(barrier, inc=1, device_id=to_order(k), device_id_type=mesh_ids)
    plan = sorted(range(1, T), key=lambda x: (level(x), x))
    for copy in get_small:
        copy.start()
    for x in range(T):
        load(x).start()
    get_precond.start()
    get_res.start()
    get_sol.start()
    get_direc.wait()
    packed[...] = direc[...].astype(jnp.bfloat16)
    get_small[0].wait()
    pl.semaphore_wait(barrier, len(into(0)) + O - 1)

    id_copies, ga_copies = {}, {}

    def pass_on(x, c, offsets):
        for o in offsets:
            to = x | o
            if c == 0:
                id_copies[to] = remote(
                    ids_all.at[x - 1] if x else ids_in, ids_all.at[to - 1],
                    id_s, id_r.at[to - 1], {"tm": across(o)},
                )
                id_copies[to].start()
            ga_copies[to, c] = remote(
                (got.at[x - 1] if x else packed).at[:, cols(c)], got.at[to - 1, :, cols(c)],
                ga_s, ga_r.at[to - 1, c], {"tm": across(o)},
            )
            ga_copies[to, c].start()

    def arrive(x, c):
        if c == 0:
            id_copies[x].wait_recv()
        ga_copies[x, c].wait_recv()
        pass_on(x, c, into(x))

    for o in into(0):
        for c in range(CHUNKS):
            pass_on(0, c, [o])

    for copy in get_small[1:5]:
        copy.wait()
    ids = ids_in[0:1, :].astype(jnp.float32)
    building = filters(ar_ref, ma_ref, aro_ref, mao_ref, ids, pt)
    next(building)

    def preconditioned(v, at):
        out = []
        for m in range(at.start // 128, at.stop // 128):
            x = v[:, m * 128 - at.start : (m + 1) * 128 - at.start]
            top, rest = halves(x)
            both = dot(jnp.concatenate([top, rest], axis=0), split[m], NT)
            out.append(both[:rhs, :128] + both[rhs:, :128] + both[:rhs, 128:])
        return jnp.concatenate(out, axis=1)

    def observe(x, c, at):
        if c == 0:
            load(x).wait()

        @apart
        def _():
            for k in range(0, 3 * n, n):
                obs_out[:, k : k + n] += dot(got[x - 1, :, at], dv[x, k : k + n, at], NT)

    next(building)
    ca, ab, fwd, bwd = next(building)
    first, last = ids[:, 0:1], ids[:, n - 1 : n]
    head_map = spread(ca, jnp.where(ids == first, 1.0, 0.0))
    tail_map = spread(ab, jnp.where(ids == last, 1.0, 0.0))
    head_map = jnp.concatenate(
        [dot(head_map[:, c * n : (c + 1) * n], pt[c], NT, HI) for c in range(3)], axis=1
    )
    both_maps = jnp.concatenate([tail_map, head_map], axis=0)
    top, rest = halves(jnp.concatenate([both_maps] * 4, axis=0))
    map_high[...] = top
    map_low[...] = rest
    for c in range(3):
        top, rest = halves(dot(pt[c], pt[c], NT, HI))
        back_high[c] = top
        back_low[c] = rest
    load(0).wait()
    obs_out[...] = dot(packed[...], dv[0], NT)
    far = [x for x in plan if level(x) < len(levels) - 1]
    near = [x for x in plan if level(x) == len(levels) - 1]
    for x in far:
        for c in range(CHUNKS):
            arrive(x, c)
    for x in near[:3] + far + near[3:]:
        for c in range(CHUNKS):
            if x in near:
                arrive(x, c)
            if x == T - 1:
                observe(x, c, cols(c))
        if x < T - 1:
            observe(x, 0, slice(0, share))
    quarter = rhs // 4
    for copy in get_small[5:]:
        copy.wait()
    gaps3 = jnp.concatenate([gaps_in[0:1, :].astype(jnp.float32)] * 3, axis=1)
    obs = obs_out[...]
    summary = dot3(obs * gaps3, map_high[...], map_low[...], NT)
    row = lax.broadcasted_iota(jnp.int32, summary.shape, 0)
    lane = lax.broadcasted_iota(jnp.int32, summary.shape, 1)
    turn = lax.rem(me, 4)
    summary = jnp.where(lane // 32 == (row // quarter + turn) % 4, summary, 0.0)
    summary = summary[: 2 * quarter] + summary[2 * quarter :]
    summary = summary[:quarter] + summary[quarter:]
    summ_out[...] = summary
    summ_in[order * T + me] = summary
    su_copies = []
    for k in list(range(1, T)) + [0]:
        for i in range(O):
            if i or k:
                su_copies.append(
                    remote(summ_out, summ_in.at[order * T + me], su_s, su_r, to_all(k, i))
                )
    ob_copies = [
        remote(obs_out, obs_in.at[k - 1], ob_s, ob_r, to_order(k))
        for k in range(1, O)
    ]
    for copy in su_copies + ob_copies:
        copy.start()

    direct = T <= 8

    def ranges():
        ids_e = []
        for e in range(T):
            v = ids
            for x in range(1, T):
                v = jnp.where(across(x) == e, ids_all[x - 1].astype(jnp.float32), v)
            ids_e.append(v)
        firsts = [v[:, 0:1] for v in ids_e]
        lasts = [v[:, n - 1 : n] for v in ids_e]
        runs = jnp.concatenate(
            [ca * jnp.where(v == f, 1.0, 0.0) for v, f in zip(ids_e, firsts)], axis=0
        )
        energy = dot(runs, tall(ca, n), NT, HI)
        energies = [bands(energy[16 * e : 16 * e + 16]) for e in range(T)]
        links = [None] + [
            jnp.where(lasts[e - 1] == firsts[e], 1.0, 0.0) for e in range(1, T)
        ]
        throughs = [jnp.where(firsts[e] == lasts[e], 1.0, 0.0) for e in range(T)]
        return links, throughs, energies

    if direct:
        @apart
        def _():
            links, throughs, energies = ranges()
            weights = state_weights(T, me, (16, n), links, throughs, fwd, bwd, energies)
            top, rest = halves(dot(weights, tall(both_maps, n), NN, HI))
            cross_high[...] = top
            cross_low[...] = rest
    else:
        links, throughs, energies = ranges()
    ob_all = remote(obs_in, obs_in, ob_s, ob_r, to_tm(1))
    ob_all.wait_recv()
    for k in range(1, O):
        obs = obs + obs_in[k - 1]
    masked = obs * gaps3
    for c in range(3):
        at = slice(c * n, (c + 1) * n)
        local_back[:, at] = dot3(masked[:, at], back_high[c], back_low[c], NN)
    others = summ_in.at[pl.ds(1, T * O - 1)]
    su_all = remote(others, others, su_s, su_r, to_tm(1))
    su_all.wait_recv()
    slot = lax.broadcasted_iota(jnp.int32, (quarter, n), 1) // 32
    sums = [sum([summ_in[i * T + e] for i in range(1, O)], summ_in[e]) for e in range(T)]
    groups = []
    for e in range(0, T, 4):
        rows = []
        for q in range(4):
            picked = sums[e + (3 - q) % 4]
            for at in range(3):
                picked = jnp.where(slot == at, sums[e + (at - q) % 4], picked)
            rows.append(pltpu.roll(picked, (n - 32 * q) % n, 1) if q else picked)
        groups.append(jnp.concatenate(rows, axis=0))
    if direct:
        adjoint = local_back[...] + dot3(
            jnp.concatenate(groups, axis=1), cross_high[...], cross_low[...], NN
        )
    else:
        lane = lax.broadcasted_iota(jnp.int32, (rhs, n), 1)
        tails = [
            jnp.where(lane < 16, pltpu.roll(groups[e // 4], (n - 32 * (e % 4)) % n, 1), 0.0)
            for e in range(T)
        ]
        heads = [
            jnp.where(lane < 16, pltpu.roll(groups[e // 4], (n - 32 * (e % 4) - 16) % n, 1), 0.0)
            for e in range(T)
        ]
        state = jnp.zeros((rhs, n), jnp.float32)
        mine_in, mine_back, back, ins = state, state, state, []
        for e in range(T):
            entering = state if e == 0 else state * links[e]
            ins.append(entering)
            mine_in = jnp.where(me == e, entering, mine_in)
            state = tails[e] + throughs[e] * banded(entering, fwd)
        for e in range(T - 1, 0, -1):
            back = heads[e] + banded(ins[e], energies[e]) + throughs[e] * banded(back, bwd)
            back = back * links[e]
            mine_back = jnp.where(me == e - 1, back, mine_back)
        states = mine_back + pltpu.roll(mine_in, 16, 1)
        adjoint = local_back[...] + dot(states, tall(both_maps, n), NN, HI)
    weighted = (adjoint * gaps3).astype(jnp.bfloat16)

    rs_copies = {}

    def part(x):
        return dot(weighted, dv[x], NN)

    def sum_of(x, c):
        total = parts[([0] + far).index(x), :, cols(c)]
        for y in reversed(range(1, T)):
            if y ^ back_over(y) == x:
                rs_copies[y, c].wait_recv()
                total = total + rs_in[y - 1, :, cols(c)].astype(jnp.float32)
        return total

    def narrow(v):
        return sum([v[:, k : k + 128] for k in range(128, v.shape[1], 128)], v[:, :128])

    def give_precond():
        get_precond.wait()
        for m in range(blocks):
            top, rest = halves(precond[m])
            split[m, :128] = top
            split[m, 128:] = rest
        get_res.wait()
        known = preconditioned(res[...], slice(0, share))
        applied[...] = known
        first_sum[...] = narrow(res[...] * known)

    def back_over(x):
        return x if x & 3 == 3 else x & max(levels[level(x)])

    def send(x, c):
        rs_copies[x, c] = remote(
            rs_out.at[x - 1, :, cols(c)], rs_in.at[x - 1, :, cols(c)],
            rs_s, rs_r.at[x - 1, c], {"tm": across(back_over(x))},
        )
        rs_copies[x, c].start()

    leaves = [x for x in reversed(plan) if level(x) == len(levels) - 1]
    for x in [x for x in leaves if x > 3 and x & 3 < 3]:
        @apart
        def _(x=x):
            rs_out[x - 1] = part(x).astype(LINK)
        for c in range(CHUNKS):
            send(x, c)
    @apart
    def _():
        for x in far:
            parts[1 + far.index(x)] = part(x)
        parts[0] = part(0) + kaula[...] * direc[...]
    give_precond()
    for x in [x for x in leaves if x & 3 == 3] + [2, 1]:
        @apart
        def _(x=x):
            rs_out[x - 1] = part(x).astype(LINK)
        for c in range(CHUNKS):
            send(x, c)
    for x in reversed(far):
        for c in range(CHUNKS):
            rs_out[x - 1, :, cols(c)] = sum_of(x, c).astype(LINK)
            send(x, c)
    inner_sums = [first_sum[...]] + [jnp.zeros((rhs, 128), jnp.float32)] * 3
    get_sol.wait()
    for c in range(CHUNKS):
        piece = sum_of(0, c)
        image_out[:, cols(c)] = piece
        moved = preconditioned(piece, cols(c))
        image_applied[:, cols(c)] = moved
        known = applied[:, cols(c)]
        for q, product in enumerate((direc[:, cols(c)] * piece, piece * known, piece * moved)):
            inner_sums[q + 1] += narrow(product)
    lane = lax.broadcasted_iota(jnp.int32, (rhs, 128), 1)
    row = lax.broadcasted_iota(jnp.int32, (rhs, 128), 0)
    total = jnp.zeros((rhs, 128), jnp.float32)
    for q, product in enumerate(inner_sums):
        total = jnp.where(lane == q * rhs + row, jnp.sum(product, axis=1, keepdims=True), total)
    total = jnp.sum(total, axis=0, keepdims=True)
    tot_out[...] = total
    tot_copies = []
    for i in range(O):
        for k in range(T):
            if i or k:
                at = i * T + k - 1
                tot_copies.append(remote(tot_out, tot_in.at[at], t1_s, t1_r, to_all(k, i)))
    for copy in tot_copies:
        copy.start()
    tot_all = remote(tot_in, tot_in, t1_s, t1_r, to_tm(1))
    tot_all.wait_recv()
    total = total + jnp.sum(tot_in[...], axis=0)
    wide = jnp.broadcast_to(total[0:1, :], (rhs, 128))
    old_rz, curvature, cross, quad = [
        jnp.sum(jnp.where(lane == q * rhs + row, wide, 0.0), axis=1, keepdims=True)
        for q in range(4)
    ]
    step = old_rz / curvature
    new_rz = old_rz - 2.0 * step * cross + step * step * quad
    app, imapp, image = applied[...], image_applied[...], image_out[...]
    d, r = direc[...], res[...]
    new_sol[...] = sol[...] + step * d
    new_res[...] = r - step * image
    new_dir[...] = app - step * imapp + (new_rz / old_rz) * d
    sent = [(ids_all, id_s, id_r.at[0]), (got, ga_s, ga_r.at[0, 0]), (rs_out, rs_s, rs_r.at[0, 0])]
    for ref, out, back in sent:
        remote(ref, ref, out, back, to_tm(1)).wait_send()
    for copy in (su_all, ob_all, tot_all):
        copy.wait_send()


def finish(new_sol, new_res, new_dir, sol_out, res_out, dir_out, sem):
    copies = [
        pltpu.make_async_copy(src, dst.at[:, 0, :], sem.at[k])
        for k, (src, dst) in enumerate(
            ((new_sol, sol_out), (new_res, res_out), (new_dir, dir_out))
        )
    ]
    for copy in copies:
        copy.start()
    for copy in copies:
        copy.wait()


def on_device(
    T, O, design, gap_flags, segment_ids, ar_order, ma_order, ar_roots, ma_roots,
    kaula, precond, solution, residual, direction,
):
    n = segment_ids.shape[0]
    columns = design.shape[2]
    share = direction.shape[2]
    rhs = direction.shape[0]
    blocks = precond.shape[1]
    f32, bf16 = jnp.float32, jnp.bfloat16
    vmem = pl.BlockSpec(memory_space=pltpu.VMEM)
    hbm = pl.BlockSpec(memory_space=pl.ANY)
    V, S, D = pltpu.VMEM, pltpu.SMEM, lambda *k: pltpu.SemaphoreType.DMA(k) if k else pltpu.SemaphoreType.DMA
    vec = pltpu.VMEM((rhs, share), f32)
    results = pl.pallas_call(
        functools.partial(kernel, T, O),
        out_shape=[vec] * 3,
        in_specs=[hbm] * 12,
        out_specs=[vmem] * 3,
        scratch_shapes=[
            V((1, n), jnp.int32), V((1, n), jnp.int32), S((3, 4), f32), S((3, 4), f32),
            S((3,), jnp.int32), S((3,), jnp.int32), V((1, share), f32),
            V((T, 3 * n, share), bf16), V((blocks, 128, 128), f32), V((rhs, share), f32),
            V((rhs, share), f32), V((rhs, share), f32), V((rhs, share), bf16), V((blocks, 256, 128), bf16),
            V((rhs, share), f32), V((T - 1, rhs, share), bf16),
            V((rhs, 3 * n), f32), V((O - 1, rhs, 3 * n), f32), V((T - 1, 1, n), jnp.int32),
            V((rhs // 4, n), f32), V((T * O, rhs // 4, n), f32), V((3, n, n), f32), V((3, n, n), bf16), V((3, n, n), bf16),
            V((rhs, 3 * n), f32),
            V((n, 3 * n), bf16), V((n, 3 * n), bf16), V((32 * T, 3 * n), bf16), V((32 * T, 3 * n), bf16),
            V((T - 1, rhs, share), LINK), V((T - 1, rhs, share), LINK),
            V((max(T // 4, 1), rhs, share), f32), V((rhs, 128), f32),
            V((rhs, share), f32), V((rhs, share), f32),
            V((1, 128), f32), V((T * O - 1, 1, 128), f32),
            D(T), D(11), D(), D(T - 1, CHUNKS), D(), D(), D(), D(T - 1), D(), D(),
            D(), D(T - 1, CHUNKS), D(), D(),
        ],
        compiler_params=pltpu.CompilerParams(
            collective_id=0, has_side_effects=True, vmem_limit_bytes=28 * 1024 * 1024
        ),
    )(*[
        pltpu.with_memory_space_constraint(v, pltpu.HBM)
        for v in (
            design.reshape(3 * n, columns), segment_ids.reshape(1, n), gap_flags.reshape(1, n),
            ar_roots, ma_roots, ar_order, ma_order, kaula, precond[0], solution, residual,
            direction,
        )
    ])
    full = jax.ShapeDtypeStruct(direction.shape, f32)
    return tuple(
        pl.pallas_call(
            finish,
            out_shape=[full] * 3,
            in_specs=[vmem] * 3,
            out_specs=[hbm] * 3,
            scratch_shapes=[D(3)],
            compiler_params=pltpu.CompilerParams(vmem_limit_bytes=1024 * 1024),
        )(*[pltpu.with_memory_space_constraint(v, pltpu.VMEM) for v in results])
    )


def solution(mesh):
    vec = P(None, "order", "tm")
    in_specs = (
        P(None, "tm", "order"), P("tm"), P("tm"), P(), P(), P(), P(), P("order", "tm"),
        P("order", "tm", None, None), vec, vec, vec,
    )
    body = functools.partial(on_device, mesh.shape["tm"], mesh.shape["order"])
    return jax.shard_map(
        body, mesh=mesh, in_specs=in_specs, out_specs=(vec, vec, vec), check_vma=False
    )
```

```python
import functools

import jax
import jax.numpy as jnp
from jax import lax
from jax.experimental import pallas as pl
from jax.experimental.pallas import tpu as pltpu
from jax.sharding import PartitionSpec as P

LINK = jnp.bfloat16
LAGS = 4
CHUNKS = 2
HI = lax.Precision.HIGHEST
NN = (((1,), (0,)), ((), ()))
NT = (((1,), (1,)), ((), ()))


def dot(a, b, dims, precision=None):
    return lax.dot_general(a, b, dims, precision=precision, preferred_element_type=jnp.float32)


def tall(block, rows):
    return jnp.concatenate(
        [block, jnp.zeros((rows - block.shape[0], block.shape[1]), jnp.float32)], axis=0
    )


def halves(x):
    top = x.astype(jnp.bfloat16)
    return top, (x - top.astype(jnp.float32)).astype(jnp.bfloat16)


def dot3(x, high, low, dims):
    rows = x.shape[0]
    top, rest = halves(x)
    both = dot(jnp.concatenate([top, rest], axis=0), high, dims)
    return both[:rows] + both[rows:] + dot(top, low, dims)


def bands(matrix):
    row = lax.broadcasted_iota(jnp.int32, matrix.shape, 0)
    col = lax.broadcasted_iota(jnp.int32, matrix.shape, 1)
    return [
        jnp.sum(jnp.where(row == col - 4 * shift, matrix, 0.0), axis=0, keepdims=True)
        for shift in range(1 - LAGS, LAGS)
    ]


def banded(vector, coeffs):
    width = vector.shape[1]
    total = None
    for shift, coeff in zip(range(1 - LAGS, LAGS), coeffs):
        moved = vector if shift == 0 else pltpu.roll(vector, 4 * shift % width, 1)
        total = moved * coeff if total is None else total + moved * coeff
    return total


def columns(ref, order_ref, comp):
    out = []
    for k in range(LAGS):
        column = jnp.zeros(comp.shape, jnp.float32)
        for c in range(3):
            value = jnp.where(k < order_ref[c], ref[c, k], 0.0)
            column = jnp.where(comp == c, value, column)
        out.append(column)
    return out


def stack(pieces):
    row = lax.broadcasted_iota(jnp.int32, pieces[0].shape, 0)
    real = row % 4 < 3
    both = [jnp.where(row < 4, pieces[i], pieces[i + 1]) for i in range(0, LAGS, 2)]
    return jnp.concatenate([jnp.where(real, block, 0.0) for block in both], axis=0)


def filters(ar_ref, ma_ref, aro_ref, mao_ref, ids, pt_ref):
    n = ids.shape[1]
    lane = lax.broadcasted_iota(jnp.int32, (8, n), 1)
    comp = lax.broadcasted_iota(jnp.int32, (8, n), 0) % 4

    def lagged(v, k):
        return v if k == 0 else jnp.where(lane >= k, pltpu.roll(v, k, 1), 0.0)

    def at(k):
        return jnp.where(lane == k, 1.0, 0.0)

    ar, ma = columns(ar_ref, aro_ref, comp), columns(ma_ref, mao_ref, comp)
    a, b = [1.0] + [0.0] * LAGS, [1.0] + [0.0] * LAGS
    for k in range(LAGS):
        a = [a[0]] + [a[j] - ar[k] * a[j - 1] for j in range(1, LAGS + 1)]
        b = [b[0]] + [b[j] - ma[k] * b[j - 1] for j in range(1, LAGS + 1)]
    h, power, m = at(0), ar, 1
    while m < n:
        s0, q0 = power[0] + power[1], power[0] * power[1]
        s1, q1 = power[2] + power[3], power[2] * power[3]
        e = [s0 + s1, q0 + q1 + s0 * s1, q0 * s1 + s0 * q1, q0 * q1]
        terms = [e[j] * lagged(h, (j + 1) * m) for j in range(LAGS) if (j + 1) * m < n]
        while len(terms) > 1:
            terms = [sum(terms[i + 1 : i + 2], terms[i]) for i in range(0, len(terms), 2)]
        h = h + terms[0]
        power, m = [p * p for p in power], 2 * m
    hs = [lagged(h, k) for k in range(LAGS + 1)]
    g = hs[0] + ((b[1] * hs[1] + b[2] * hs[2]) + (b[3] * hs[3] + b[4] * hs[4]))
    gs = [lagged(g, k) for k in range(LAGS)]
    ins, ends = [], []
    for i in range(1, LAGS + 1):
        acc, end = jnp.zeros_like(g), jnp.zeros_like(g)
        for k in range(LAGS + 1 - i):
            acc = acc + b[i + k] * at(k) - a[i + k] * gs[k]
            end = end - a[i + k] * at(n - 1 - k)
        ins.append(acc)
        ends.append(end)
    yield None
    row = lax.broadcasted_iota(jnp.int32, (n, n), 0)
    col = lax.broadcasted_iota(jnp.int32, (n, n), 1)
    grid = jnp.broadcast_to(ids, (n, n))
    joined = (grid == grid.T) & (col >= row)
    for c in range(3):
        t = pltpu.roll(jnp.broadcast_to(g[c : c + 1], (n, n)), 0, 1, stride=1, stride_axis=0)
        pt_ref[c] = jnp.where(joined, t, 0.0)
    yield None
    ca, ends = stack(hs[:LAGS]), stack(ends)
    flip = jnp.where(row + col == n - 1, 1.0, 0.0).astype(jnp.float32)
    ab = dot(stack(ins), flip, NN, HI)
    fwd = bands(dot(ca, tall(ends, n), NT, HI))
    bwd = bands(dot(ends, tall(ca, n), NT, HI))
    yield ca, ab, fwd, bwd


def spread(block, mask):
    row = lax.broadcasted_iota(jnp.int32, block.shape, 0)
    return jnp.concatenate(
        [jnp.where(row % 4 == c, block * mask, 0.0) for c in range(3)], axis=1
    )


def state_weights(T, me, shape, links, throughs, fwd, bwd, energies):
    row = lax.broadcasted_iota(jnp.int32, shape, 0)
    lane = lax.broadcasted_iota(jnp.int32, shape, 1)
    eye = jnp.where(row == lane, 1.0, 0.0)
    zero = jnp.zeros(shape, jnp.float32)
    state, ins, mine = {}, [], {}

    def keep(blocks, e, into):
        for key, v in blocks.items():
            mine[into, key] = jnp.where(me == e, v, mine.get((into, key), zero))

    for e in range(T):
        entering = {q: v * links[e] for q, v in state.items()}
        ins.append(entering)
        keep(entering, e, "in")
        state = {q: throughs[e] * banded(v, fwd) for q, v in entering.items()}
        state[e] = eye
    back = {}
    for e in range(T - 1, 0, -1):
        new = {key: throughs[e] * banded(v, bwd) for key, v in back.items()}
        for q, v in ins[e].items():
            moved = banded(v, energies[e])
            new["tail", q] = new["tail", q] + moved if ("tail", q) in new else moved
        new["head", e] = eye
        back = {key: v * links[e] for key, v in new.items()}
        keep(back, e - 1, "back")
    out = []
    for e in range(T):
        entering = pltpu.roll(mine["in", e], 16, 1) if ("in", e) in mine else zero
        out.append(mine.get(("back", ("tail", e)), zero) + entering)
        out.append(mine.get(("back", ("head", e)), zero))
    return jnp.concatenate(out, axis=0)


def kernel(
    T, O,
    design, ids_hbm, gaps_hbm, ar_hbm, ma_hbm, aro_hbm, mao_hbm, kaula_hbm, precond_in,
    sol_in, res_in, direc_in,
    new_sol, new_res, new_dir,
    ids_in, gaps_in, ar_ref, ma_ref, aro_ref, mao_ref, kaula, dv, precond, sol, res, direc, packed, split,
    image_out, got, obs_out, obs_in, ids_all, summ_out, summ_in, pt, back_high, back_low, local_back,
    map_high, map_low, cross_high, cross_low, rs_out, rs_in, parts, first_sum, applied, image_applied,
    tot_out, tot_in,
    dsem, in_sem, ga_s, ga_r, ob_s, ob_r, id_s, id_r, su_s, su_r,
    rs_s, rs_r, t1_s, t1_r,
):
    me, order = lax.axis_index("tm"), lax.axis_index("order")
    rhs, share = packed.shape
    n = ids_in.shape[1]
    blocks = precond.shape[0]
    bounds = [0, max(128, share * 10 // 16 // 128 * 128), share]
    bits = T.bit_length() - 1

    levels = [(1 << b,) for b in reversed(range(2, bits))] + [(3, 2, 1)]

    def level(x):
        return max([i for i, offsets in enumerate(levels) if any(x & o for o in offsets)], default=-1)

    def into(x):
        return [o for offsets in levels[level(x) + 1 :] for o in offsets]

    def place(x):
        out = me
        for b in range(bits):
            if x >> b & 1:
                out = out + (1 << b) * (1 - 2 * lax.rem(lax.div(me, 1 << b), 2))
        return out

    places = [place(x) for x in range(T)]

    def across(x):
        return places[x]

    def cols(c):
        return slice(bounds[c], bounds[c + 1])

    mesh_ids = pl.DeviceIdType.MESH
    apart = pl.when(me >= 0)

    def to_tm(k):
        return {"tm": lax.rem(me + k, T)}

    def to_order(k):
        return {"order": lax.rem(order + k, O)}

    def to_all(k, i):
        return {"tm": lax.rem(me + k, T), "order": lax.rem(order + i, O)}

    def load(x):
        return pltpu.make_async_copy(
            design.at[:, pl.ds(pl.multiple_of(across(x) * share, 128), share)],
            dv.at[x],
            dsem.at[x],
        )

    def remote(src, dst, ssem, rsem, to):
        return pltpu.make_async_remote_copy(
            src_ref=src, dst_ref=dst, send_sem=ssem, recv_sem=rsem,
            device_id=to, device_id_type=mesh_ids,
        )

    get_direc = pltpu.make_async_copy(direc_in.at[:, 0, :], direc, in_sem.at[0])
    get_res = pltpu.make_async_copy(res_in.at[:, 0, :], res, in_sem.at[1])
    get_sol = pltpu.make_async_copy(sol_in.at[:, 0, :], sol, in_sem.at[3])
    get_precond = pltpu.make_async_copy(precond_in, precond, in_sem.at[2])
    get_direc.start()
    get_small = [
        pltpu.make_async_copy(src, dst, in_sem.at[4 + k])
        for k, (src, dst) in enumerate((
            (ids_hbm, ids_in), (ar_hbm, ar_ref), (ma_hbm, ma_ref), (aro_hbm, aro_ref),
            (mao_hbm, mao_ref), (gaps_hbm, gaps_in), (kaula_hbm, kaula),
        ))
    ]
    barrier = pltpu.get_barrier_semaphore()
    for x in into(0):
        pl.semaphore_signal(
            barrier, inc=1, device_id={"tm": across(x)}, device_id_type=mesh_ids
        )
    for k in range(1, O):
        pl.semaphore_signal(barrier, inc=1, device_id=to_order(k), device_id_type=mesh_ids)
    plan = sorted(range(1, T), key=lambda x: (level(x), x))
    for copy in get_small:
        copy.start()
    for x in range(T):
        load(x).start()
    get_precond.start()
    get_res.start()
    get_sol.start()
    get_direc.wait()
    packed[...] = direc[...].astype(jnp.bfloat16)
    get_small[0].wait()
    pl.semaphore_wait(barrier, len(into(0)) + O - 1)

    id_copies, ga_copies = {}, {}

    def pass_on(x, c, offsets):
        for o in offsets:
            to = x | o
            if c == 0:
                id_copies[to] = remote(
                    ids_all.at[x - 1] if x else ids_in, ids_all.at[to - 1],
                    id_s, id_r.at[to - 1], {"tm": across(o)},
                )
                id_copies[to].start()
            ga_copies[to, c] = remote(
                (got.at[x - 1] if x else packed).at[:, cols(c)], got.at[to - 1, :, cols(c)],
                ga_s, ga_r.at[to - 1, c], {"tm": across(o)},
            )
            ga_copies[to, c].start()

    def arrive(x, c):
        if c == 0:
            id_copies[x].wait_recv()
        ga_copies[x, c].wait_recv()
        pass_on(x, c, into(x))

    for o in into(0):
        for c in range(CHUNKS):
            pass_on(0, c, [o])

    for copy in get_small[1:5]:
        copy.wait()
    ids = ids_in[0:1, :].astype(jnp.float32)
    building = filters(ar_ref, ma_ref, aro_ref, mao_ref, ids, pt)
    next(building)

    def preconditioned(v, at):
        out = []
        for m in range(at.start // 128, at.stop // 128):
            x = v[:, m * 128 - at.start : (m + 1) * 128 - at.start]
            top, rest = halves(x)
            both = dot(jnp.concatenate([top, rest], axis=0), split[m], NT)
            out.append(both[:rhs, :128] + both[rhs:, :128] + both[:rhs, 128:])
        return jnp.concatenate(out, axis=1)

    def observe(x, c, at):
        if c == 0:
            load(x).wait()

        @apart
        def _():
            for k in range(0, 3 * n, n):
                obs_out[:, k : k + n] += dot(got[x - 1, :, at], dv[x, k : k + n, at], NT)

    next(building)
    ca, ab, fwd, bwd = next(building)
    first, last = ids[:, 0:1], ids[:, n - 1 : n]
    head_map = spread(ca, jnp.where(ids == first, 1.0, 0.0))
    tail_map = spread(ab, jnp.where(ids == last, 1.0, 0.0))
    head_map = jnp.concatenate(
        [dot(head_map[:, c * n : (c + 1) * n], pt[c], NT, HI) for c in range(3)], axis=1
    )
    both_maps = jnp.concatenate([tail_map, head_map], axis=0)
    top, rest = halves(jnp.concatenate([both_maps] * 4, axis=0))
    map_high[...] = top
    map_low[...] = rest
    for c in range(3):
        top, rest = halves(dot(pt[c], pt[c], NT, HI))
        back_high[c] = top
        back_low[c] = rest
    load(0).wait()
    obs_out[...] = dot(packed[...], dv[0], NT)
    far = [x for x in plan if level(x) < len(levels) - 1]
    near = [x for x in plan if level(x) == len(levels) - 1]
    for x in far:
        for c in range(CHUNKS):
            arrive(x, c)
    for x in near[:3] + far + near[3:]:
        for c in range(CHUNKS):
            if x in near:
                arrive(x, c)
            if x == T - 1:
                observe(x, c, cols(c))
        if x < T - 1:
            observe(x, 0, slice(0, share))
    quarter = rhs // 4
    for copy in get_small[5:]:
        copy.wait()
    gaps3 = jnp.concatenate([gaps_in[0:1, :].astype(jnp.float32)] * 3, axis=1)
    obs = obs_out[...]
    summary = dot3(obs * gaps3, map_high[...], map_low[...], NT)
    row = lax.broadcasted_iota(jnp.int32, summary.shape, 0)
    lane = lax.broadcasted_iota(jnp.int32, summary.shape, 1)
    turn = lax.rem(me, 4)
    summary = jnp.where(lane // 32 == (row // quarter + turn) % 4, summary, 0.0)
    summary = summary[: 2 * quarter] + summary[2 * quarter :]
    summary = summary[:quarter] + summary[quarter:]
    summ_out[...] = summary
    summ_in[order * T + me] = summary
    su_copies = []
    for k in list(range(1, T)) + [0]:
        for i in range(O):
            if i or k:
                su_copies.append(
                    remote(summ_out, summ_in.at[order * T + me], su_s, su_r, to_all(k, i))
                )
    ob_copies = [
        remote(obs_out, obs_in.at[k - 1], ob_s, ob_r, to_order(k))
        for k in range(1, O)
    ]
    for copy in su_copies + ob_copies:
        copy.start()

    direct = T <= 8

    def ranges():
        ids_e = []
        for e in range(T):
            v = ids
            for x in range(1, T):
                v = jnp.where(across(x) == e, ids_all[x - 1].astype(jnp.float32), v)
            ids_e.append(v)
        firsts = [v[:, 0:1] for v in ids_e]
        lasts = [v[:, n - 1 : n] for v in ids_e]
        runs = jnp.concatenate(
            [ca * jnp.where(v == f, 1.0, 0.0) for v, f in zip(ids_e, firsts)], axis=0
        )
        energy = dot(runs, tall(ca, n), NT, HI)
        energies = [bands(energy[16 * e : 16 * e + 16]) for e in range(T)]
        links = [None] + [
            jnp.where(lasts[e - 1] == firsts[e], 1.0, 0.0) for e in range(1, T)
        ]
        throughs = [jnp.where(firsts[e] == lasts[e], 1.0, 0.0) for e in range(T)]
        return links, throughs, energies

    if direct:
        @apart
        def _():
            links, throughs, energies = ranges()
            weights = state_weights(T, me, (16, n), links, throughs, fwd, bwd, energies)
            top, rest = halves(dot(weights, tall(both_maps, n), NN, HI))
            cross_high[...] = top
            cross_low[...] = rest
    else:
        links, throughs, energies = ranges()
    ob_all = remote(obs_in, obs_in, ob_s, ob_r, to_tm(1))
    ob_all.wait_recv()
    for k in range(1, O):
        obs = obs + obs_in[k - 1]
    masked = obs * gaps3
    for c in range(3):
        at = slice(c * n, (c + 1) * n)
        local_back[:, at] = dot3(masked[:, at], back_high[c], back_low[c], NN)
    others = summ_in.at[pl.ds(1, T * O - 1)]
    su_all = remote(others, others, su_s, su_r, to_tm(1))
    su_all.wait_recv()
    slot = lax.broadcasted_iota(jnp.int32, (quarter, n), 1) // 32
    sums = [sum([summ_in[i * T + e] for i in range(1, O)], summ_in[e]) for e in range(T)]
    groups = []
    for e in range(0, T, 4):
        rows = []
        for q in range(4):
            picked = sums[e + (3 - q) % 4]
            for at in range(3):
                picked = jnp.where(slot == at, sums[e + (at - q) % 4], picked)
            rows.append(pltpu.roll(picked, (n - 32 * q) % n, 1) if q else picked)
        groups.append(jnp.concatenate(rows, axis=0))
    if direct:
        adjoint = local_back[...] + dot3(
            jnp.concatenate(groups, axis=1), cross_high[...], cross_low[...], NN
        )
    else:
        lane = lax.broadcasted_iota(jnp.int32, (rhs, n), 1)
        tails = [
            jnp.where(lane < 16, pltpu.roll(groups[e // 4], (n - 32 * (e % 4)) % n, 1), 0.0)
            for e in range(T)
        ]
        heads = [
            jnp.where(lane < 16, pltpu.roll(groups[e // 4], (n - 32 * (e % 4) - 16) % n, 1), 0.0)
            for e in range(T)
        ]
        state = jnp.zeros((rhs, n), jnp.float32)
        mine_in, mine_back, back, ins = state, state, state, []
        for e in range(T):
            entering = state if e == 0 else state * links[e]
            ins.append(entering)
            mine_in = jnp.where(me == e, entering, mine_in)
            state = tails[e] + throughs[e] * banded(entering, fwd)
        for e in range(T - 1, 0, -1):
            back = heads[e] + banded(ins[e], energies[e]) + throughs[e] * banded(back, bwd)
            back = back * links[e]
            mine_back = jnp.where(me == e - 1, back, mine_back)
        states = mine_back + pltpu.roll(mine_in, 16, 1)
        adjoint = local_back[...] + dot(states, tall(both_maps, n), NN, HI)
    weighted = (adjoint * gaps3).astype(jnp.bfloat16)

    rs_copies = {}

    def part(x):
        return dot(weighted, dv[x], NN)

    def sum_of(x, c):
        total = parts[([0] + far).index(x), :, cols(c)]
        for y in reversed(range(1, T)):
            if y ^ back_over(y) == x:
                rs_copies[y, c].wait_recv()
                total = total + rs_in[y - 1, :, cols(c)].astype(jnp.float32)
        return total

    def narrow(v):
        return sum([v[:, k : k + 128] for k in range(128, v.shape[1], 128)], v[:, :128])

    def give_precond():
        get_precond.wait()
        for m in range(blocks):
            top, rest = halves(precond[m])
            split[m, :128] = top
            split[m, 128:] = rest
        get_res.wait()
        known = preconditioned(res[...], slice(0, share))
        applied[...] = known
        first_sum[...] = narrow(res[...] * known)

    def back_over(x):
        return x if x & 3 == 3 else x & max(levels[level(x)])

    def send(x, c):
        rs_copies[x, c] = remote(
            rs_out.at[x - 1, :, cols(c)], rs_in.at[x - 1, :, cols(c)],
            rs_s, rs_r.at[x - 1, c], {"tm": across(back_over(x))},
        )
        rs_copies[x, c].start()

    leaves = [x for x in reversed(plan) if level(x) == len(levels) - 1]
    for x in [x for x in leaves if x > 3 and x & 3 < 3]:
        @apart
        def _(x=x):
            rs_out[x - 1] = part(x).astype(LINK)
        for c in range(CHUNKS):
            send(x, c)
    @apart
    def _():
        for x in far:
            parts[1 + far.index(x)] = part(x)
        parts[0] = part(0) + kaula[...] * direc[...]
    for x in [x for x in leaves if x & 3 == 3] + [2, 1]:
        @apart
        def _(x=x):
            rs_out[x - 1] = part(x).astype(LINK)
        for c in range(CHUNKS):
            send(x, c)
    for x in reversed(far):
        for c in range(CHUNKS):
            rs_out[x - 1, :, cols(c)] = sum_of(x, c).astype(LINK)
            send(x, c)
    give_precond()
    inner_sums = [first_sum[...]] + [jnp.zeros((rhs, 128), jnp.float32)] * 3
    get_sol.wait()
    for c in range(CHUNKS):
        piece = sum_of(0, c)
        image_out[:, cols(c)] = piece
        moved = preconditioned(piece, cols(c))
        image_applied[:, cols(c)] = moved
        known = applied[:, cols(c)]
        for q, product in enumerate((direc[:, cols(c)] * piece, piece * known, piece * moved)):
            inner_sums[q + 1] += narrow(product)
    lane = lax.broadcasted_iota(jnp.int32, (rhs, 128), 1)
    row = lax.broadcasted_iota(jnp.int32, (rhs, 128), 0)
    total = jnp.zeros((rhs, 128), jnp.float32)
    for q, product in enumerate(inner_sums):
        total = jnp.where(lane == q * rhs + row, jnp.sum(product, axis=1, keepdims=True), total)
    total = jnp.sum(total, axis=0, keepdims=True)
    tot_out[...] = total
    tot_copies = []
    for i in range(O):
        for k in range(T):
            if i or k:
                at = i * T + k - 1
                tot_copies.append(remote(tot_out, tot_in.at[at], t1_s, t1_r, to_all(k, i)))
    for copy in tot_copies:
        copy.start()
    tot_all = remote(tot_in, tot_in, t1_s, t1_r, to_tm(1))
    tot_all.wait_recv()
    total = total + jnp.sum(tot_in[...], axis=0)
    wide = jnp.broadcast_to(total[0:1, :], (rhs, 128))
    old_rz, curvature, cross, quad = [
        jnp.sum(jnp.where(lane == q * rhs + row, wide, 0.0), axis=1, keepdims=True)
        for q in range(4)
    ]
    step = old_rz / curvature
    new_rz = old_rz - 2.0 * step * cross + step * step * quad
    app, imapp, image = applied[...], image_applied[...], image_out[...]
    d, r = direc[...], res[...]
    new_sol[...] = sol[...] + step * d
    new_res[...] = r - step * image
    new_dir[...] = app - step * imapp + (new_rz / old_rz) * d
    sent = [(ids_all, id_s, id_r.at[0]), (got, ga_s, ga_r.at[0, 0]), (rs_out, rs_s, rs_r.at[0, 0])]
    for ref, out, back in sent:
        remote(ref, ref, out, back, to_tm(1)).wait_send()
    for copy in (su_all, ob_all, tot_all):
        copy.wait_send()


def finish(new_sol, new_res, new_dir, sol_out, res_out, dir_out, sem):
    copies = [
        pltpu.make_async_copy(src, dst.at[:, 0, :], sem.at[k])
        for k, (src, dst) in enumerate(
            ((new_sol, sol_out), (new_res, res_out), (new_dir, dir_out))
        )
    ]
    for copy in copies:
        copy.start()
    for copy in copies:
        copy.wait()


def on_device(
    T, O, design, gap_flags, segment_ids, ar_order, ma_order, ar_roots, ma_roots,
    kaula, precond, solution, residual, direction,
):
    n = segment_ids.shape[0]
    columns = design.shape[2]
    share = direction.shape[2]
    rhs = direction.shape[0]
    blocks = precond.shape[1]
    f32, bf16 = jnp.float32, jnp.bfloat16
    vmem = pl.BlockSpec(memory_space=pltpu.VMEM)
    hbm = pl.BlockSpec(memory_space=pl.ANY)
    V, S, D = pltpu.VMEM, pltpu.SMEM, lambda *k: pltpu.SemaphoreType.DMA(k) if k else pltpu.SemaphoreType.DMA
    vec = pltpu.VMEM((rhs, share), f32)
    results = pl.pallas_call(
        functools.partial(kernel, T, O),
        out_shape=[vec] * 3,
        in_specs=[hbm] * 12,
        out_specs=[vmem] * 3,
        scratch_shapes=[
            V((1, n), jnp.int32), V((1, n), jnp.int32), S((3, 4), f32), S((3, 4), f32),
            S((3,), jnp.int32), S((3,), jnp.int32), V((1, share), f32),
            V((T, 3 * n, share), bf16), V((blocks, 128, 128), f32), V((rhs, share), f32),
            V((rhs, share), f32), V((rhs, share), f32), V((rhs, share), bf16), V((blocks, 256, 128), bf16),
            V((rhs, share), f32), V((T - 1, rhs, share), bf16),
            V((rhs, 3 * n), f32), V((O - 1, rhs, 3 * n), f32), V((T - 1, 1, n), jnp.int32),
            V((rhs // 4, n), f32), V((T * O, rhs // 4, n), f32), V((3, n, n), f32), V((3, n, n), bf16), V((3, n, n), bf16),
            V((rhs, 3 * n), f32),
            V((n, 3 * n), bf16), V((n, 3 * n), bf16), V((32 * T, 3 * n), bf16), V((32 * T, 3 * n), bf16),
            V((T - 1, rhs, share), LINK), V((T - 1, rhs, share), LINK),
            V((max(T // 4, 1), rhs, share), f32), V((rhs, 128), f32),
            V((rhs, share), f32), V((rhs, share), f32),
            V((1, 128), f32), V((T * O - 1, 1, 128), f32),
            D(T), D(11), D(), D(T - 1, CHUNKS), D(), D(), D(), D(T - 1), D(), D(),
            D(), D(T - 1, CHUNKS), D(), D(),
        ],
        compiler_params=pltpu.CompilerParams(
            collective_id=0, has_side_effects=True, vmem_limit_bytes=28 * 1024 * 1024
        ),
    )(*[
        pltpu.with_memory_space_constraint(v, pltpu.HBM)
        for v in (
            design.reshape(3 * n, columns), segment_ids.reshape(1, n), gap_flags.reshape(1, n),
            ar_roots, ma_roots, ar_order, ma_order, kaula, precond[0], solution, residual,
            direction,
        )
    ])
    full = jax.ShapeDtypeStruct(direction.shape, f32)
    return tuple(
        pl.pallas_call(
            finish,
            out_shape=[full] * 3,
            in_specs=[vmem] * 3,
            out_specs=[hbm] * 3,
            scratch_shapes=[D(3)],
            compiler_params=pltpu.CompilerParams(vmem_limit_bytes=1024 * 1024),
        )(*[pltpu.with_memory_space_constraint(v, pltpu.VMEM) for v in results])
    )


def solution(mesh):
    vec = P(None, "order", "tm")
    in_specs = (
        P(None, "tm", "order"), P("tm"), P("tm"), P(), P(), P(), P(), P("order", "tm"),
        P("order", "tm", None, None), vec, vec, vec,
    )
    body = functools.partial(on_device, mesh.shape["tm"], mesh.shape["order"])
    return jax.shard_map(
        body, mesh=mesh, in_specs=in_specs, out_specs=(vec, vec, vec), check_vma=False
    )
```
